32 devices in a mesh: groups: 2 (over y), tx: 16 (over z, x, core).
Axes of the slice: x: 2, y: 2, z: 4, core: 2. Of those that a mesh axis runs over, the one named last changes fastest.
Arguments:
- mask: bfloat16 [8192, 1024], P(('groups', 'tx')), parts along dimension 0, may hold values from -1 to 1
- kernel_spectra: float32 [2, 96, 12, 128], replicated, may hold values from -3 to 3
- kernel_weights: float32 [12], replicated, may hold values from 0.1 to 1
- threshold: float32 [1], replicated, may hold values from 0.4 to 1.2
- eval_tile: int32 [16384], P(('groups', 'tx')), parts along dimension 0, may hold values from 0 to 15, as said below
- site_coords: float32 [2, 16, 16384], P(None, None, ('groups', 'tx')), parts along dimension 2, may hold values from 0 to 1
- bias_steps: int32 [16384], P(('groups', 'tx')), parts along dimension 0, may hold values from -4 to 4
Outputs:
- resist: float32 [8192, 1024], P(('groups', 'tx')), parts along dimension 0
- new_bias: float32 [16384], P(('groups', 'tx')), parts along dimension 0
The draws below stay inside these ranges and needn't reach their ends.
There are 2 independent parts, one for each index of `groups`. The reference program is written for one: setup_inputs(seed, part) draws one part's arguments, and reference() takes and returns one part's arrays. A program takes and returns all parts, laid end to end along the dimension named above; an argument that names none is the same for every part. Nothing has to cross between parts.
Inputs may be any that keep to these rules, and one draw needn't show every extreme that they name: `eval_tile`: the evaluating tile of a fragment owned by tile t is t - 1, t or t + 1. One owning tile sends at most 256 fragments to each evaluating tile and exactly 256 to at least one of them; in every draw some tile receives exactly 256 fragments from each of the three owners beside it or itself.
All inputs are finite; a program needn't handle non-finite values.
Results may differ from the reference program's by a relative error of at most 0.0019.
Values may be sent and summed in bfloat16 or wider, within the bound.
A program may use at most 64 MiB of HBM per device.

```python
import math
import jax
import jax.numpy as jnp
from jax import lax

ROWS_DEV = 256
COLS = 1024
HALO = 256
BLUR_REACH = 8
KERNELS = 12
SITES = 16
FRAG_DEV = 512
WINDOW = 768
ROW_FREQS = 96
COL_FREQS = 128
REGION_ROWS = 4096
FRAGS = 8192
N_TX = 16


def permuted_order(order_key):
    return jax.random.permutation(order_key, FRAG_DEV)


def draw_eval_tile(key, part):
    tile_total = FRAGS // FRAG_DEV
    capacity = FRAG_DEV // 2
    key_full, key_split, key_dense, key_order = jax.random.split(key, 4)
    owners = jnp.arange(tile_total, dtype=jnp.int32)
    full_side = jax.random.randint(key_full, (tile_total,), 0, 3)
    dense_tile = jax.random.randint(key_dense, (), 1, tile_total - 1)
    full_side = jnp.where(owners == dense_tile - 1, 2, full_side)
    full_side = jnp.where(owners == dense_tile, 1, full_side)
    full_side = jnp.where(owners == dense_tile + 1, 0, full_side)
    split_count = jax.random.randint(key_split, (tile_total,), 0, capacity + 1)
    sides = jnp.arange(3, dtype=jnp.int32)
    is_full = sides[None, :] == full_side[:, None]
    other_rank = jnp.cumsum(1 - is_full.astype(jnp.int32), axis=1) - 1
    counts = jnp.where(is_full, capacity, jnp.where(other_rank == 0, split_count[:, None], capacity - split_count[:, None]))
    first_row = jnp.where(sides == 0, 0, capacity)
    last_row = jnp.where(sides == 2, 0, capacity)
    counts = jnp.where((owners == 0)[:, None], first_row[None, :], counts)
    counts = jnp.where((owners == tile_total - 1)[:, None], last_row[None, :], counts)
    position = jnp.arange(FRAG_DEV, dtype=jnp.int32)
    side_of = (position[None, :] >= counts[:, 0:1]).astype(jnp.int32) + (position[None, :] >= counts[:, 0:1] + counts[:, 1:2]).astype(jnp.int32)
    order_keys = jax.random.split(key_order, tile_total)
    orders = jax.vmap(permuted_order)(order_keys)
    shuffled = jnp.take_along_axis(side_of, orders, axis=1)
    return (owners[:, None] + shuffled - 1).reshape(-1).astype(jnp.int32)


def with_ends(array, stream_key, low, largest):
    index_at = [jax.random.randint(jax.random.fold_in(stream_key, axis), (), 0, length) for axis, length in enumerate(array.shape)]
    widest = array.shape.index(max(array.shape))
    neighbour = index_at[:widest] + [(index_at[widest] + 1) % array.shape[widest]] + index_at[widest + 1:]
    return array.at[tuple(index_at)].set(low).at[tuple(neighbour)].set(largest)


def block_levels(own_key, dims, cuts, smallest, largest):
    def one(dim, parts):
        steps = jax.random.uniform(jax.random.fold_in(jax.random.fold_in(own_key, 6), dim), (parts,), jnp.float32, smallest / len(cuts), largest / len(cuts))
        return jnp.repeat(jnp.exp(steps), dims[dim] // parts).reshape((-1,) + (1,) * (len(dims) - dim - 1))

    factor_of = one(*cuts[0])
    for cut in cuts[1:]:
        factor_of = factor_of * one(*cut)
    return factor_of


def noise(rng, dims, spread, most, held_as=jnp.bfloat16):
    result = jax.random.normal(rng, dims, jnp.float32) * spread
    return jnp.minimum(jnp.maximum(result, -most), most).astype(held_as)


def setup_inputs(seed: int = 0, part: int = 0) -> dict:
    seeds = jax.random.split(jax.random.key(seed), 8)
    own_keys = jax.random.split(jax.random.fold_in(seeds[7], part), 8)
    mask = jnp.clip(jax.random.uniform(own_keys[0], (REGION_ROWS, COLS), jnp.float32, -1.0, 1.0) * block_levels(own_keys[0], (REGION_ROWS, COLS), ((0, 16),), -0.4, 0.0), -1.0, 1.0).astype(jnp.bfloat16)
    kernel_spectra = noise(seeds[1], (2, ROW_FREQS, KERNELS, COL_FREQS), 0.5, 3.0, jnp.float32)
    kernel_weights = jnp.clip(jnp.exp(jax.random.uniform(seeds[2], (KERNELS,), jnp.float32, math.log(0.1), math.log(1.0))), 0.1, 1.0)
    threshold = jnp.clip(jax.random.uniform(seeds[3], (1,), jnp.float32, 0.4, 1.2), 0.4, 1.2)
    eval_tile = draw_eval_tile(jax.random.fold_in(jax.random.fold_in(seeds[7], part), 71), part)
    site_coords = jnp.clip(1.0 * jax.random.uniform(own_keys[5], (2, SITES, FRAGS), jnp.float32) ** block_levels(own_keys[5], (2, SITES, FRAGS), ((2, 16),), -0.2, 0.2), 0.0, 1.0)
    bias_steps = with_ends(jax.random.randint(own_keys[6], (FRAGS,), -4, 5), jax.random.fold_in(own_keys[6], 1), -4, 4).astype(jnp.int32)
    return {"mask": mask, "kernel_spectra": kernel_spectra, "kernel_weights": kernel_weights, "threshold": threshold, "eval_tile": eval_tile, "site_coords": site_coords, "bias_steps": bias_steps}


blur_sigma = 3.0
bias_step = 0.5
bias_gain = 2.0

def twiddle(position, frequency, period, amplitude):
    phase_index = position[:, None] * frequency[None, :] % period
    phase_angle = phase_index.astype(jnp.float32) * (2.0 * math.pi / period)
    return (jnp.cos(phase_angle) * amplitude, jnp.sin(phase_angle) * amplitude)

def centered(count):
    return jnp.arange(count, dtype=jnp.int32) - count // 2

def imaging_tables(tile_rows, tile_cols, window_rows, row_freqs, col_freqs, halo_rows):
    col_cos, col_sin = twiddle(jnp.arange(tile_cols, dtype=jnp.int32), centered(col_freqs), tile_cols, 1.0 / math.sqrt(tile_cols))
    col_forward = jnp.concatenate([col_cos, -col_sin], axis=1).astype(jnp.bfloat16)
    row_cos, row_sin = twiddle(centered(row_freqs), jnp.arange(window_rows, dtype=jnp.int32), window_rows, 1.0 / math.sqrt(window_rows))
    row_forward = jnp.concatenate([row_cos, -row_sin], axis=0).astype(jnp.bfloat16)
    back_cos, back_sin = twiddle(jnp.arange(tile_rows, dtype=jnp.int32) + halo_rows, centered(row_freqs), window_rows, 1.0 / math.sqrt(row_freqs))
    row_inverse = jnp.concatenate([back_cos, back_sin], axis=0).astype(jnp.bfloat16)
    out_cos, out_sin = twiddle(centered(col_freqs), jnp.arange(tile_cols, dtype=jnp.int32), tile_cols, 1.0 / math.sqrt(col_freqs))
    upper_half = jnp.concatenate([out_cos, out_sin], axis=1)
    lower_half = jnp.concatenate([-out_sin, out_cos], axis=1)
    col_inverse = jnp.concatenate([upper_half, lower_half], axis=0).astype(jnp.bfloat16)
    return (col_forward, row_forward, row_inverse, col_inverse)

def tile_intensity(col_spectra, tables, kernel_spectra, kernel_weights):
    row_forward = tables[1]
    row_inverse = tables[2]
    col_inverse = tables[3]
    row_freqs = kernel_spectra.shape[1]
    kernel_count = kernel_spectra.shape[2]
    col_freqs = kernel_spectra.shape[3]
    tile_rows = row_inverse.shape[0] // 2
    tile_cols = col_inverse.shape[1] // 2
    row_product = jnp.dot(row_forward, col_spectra, preferred_element_type=jnp.float32)
    spec_real = row_product[:row_freqs, :col_freqs] - row_product[row_freqs:, col_freqs:]
    spec_imag = row_product[:row_freqs, col_freqs:] + row_product[row_freqs:, :col_freqs]
    kern_real = kernel_spectra[0]
    kern_imag = kernel_spectra[1]
    prod_real = (kern_real * spec_real[:, None, :] - kern_imag * spec_imag[:, None, :]).astype(jnp.bfloat16)
    prod_imag = (kern_real * spec_imag[:, None, :] + kern_imag * spec_real[:, None, :]).astype(jnp.bfloat16)
    flat_width = kernel_count * col_freqs
    joined = jnp.concatenate([prod_real.reshape(row_freqs, flat_width), prod_imag.reshape(row_freqs, flat_width)], axis=1)
    back_product = jnp.dot(row_inverse, joined, preferred_element_type=jnp.float32)
    half_real = (back_product[:tile_rows, :flat_width] - back_product[tile_rows:, flat_width:]).astype(jnp.bfloat16)
    half_imag = (back_product[:tile_rows, flat_width:] + back_product[tile_rows:, :flat_width]).astype(jnp.bfloat16)
    stacked = jnp.concatenate([half_real.reshape(tile_rows, kernel_count, col_freqs), half_imag.reshape(tile_rows, kernel_count, col_freqs)], axis=2)
    stacked = jnp.transpose(stacked, (1, 0, 2))

    def add_kernel(intensity_sum, inputs):
        kernel_block, kernel_weight = inputs
        field_pair = jnp.dot(kernel_block, col_inverse, preferred_element_type=jnp.float32)
        field_real = field_pair[:, :tile_cols]
        field_imag = field_pair[:, tile_cols:]
        return (intensity_sum + kernel_weight * (field_real * field_real + field_imag * field_imag), None)
    start_sum = jnp.zeros((tile_rows, tile_cols), jnp.float32)
    intensity_sum, unused_out = lax.scan(add_kernel, start_sum, (stacked, kernel_weights))
    return intensity_sum.astype(jnp.bfloat16)

def blur_weight(offset, reach):
    offset_value = offset.astype(jnp.float32)
    all_offsets = jnp.arange(-reach, reach + 1, dtype=jnp.int32).astype(jnp.float32)
    norm_sum = jnp.sum(jnp.exp(-all_offsets * all_offsets / (2.0 * blur_sigma * blur_sigma)))
    inside = jnp.abs(offset) <= reach
    return jnp.where(inside, jnp.exp(-offset_value * offset_value / (2.0 * blur_sigma * blur_sigma)) / norm_sum, jnp.float32(0.0))

def blur_tables(tile_rows, tile_cols, reach):
    col_diff = jnp.arange(tile_cols, dtype=jnp.int32)[None, :] - jnp.arange(tile_cols, dtype=jnp.int32)[:, None]
    col_blur = blur_weight(col_diff, reach).astype(jnp.bfloat16)
    row_diff = jnp.arange(tile_rows + 2 * reach, dtype=jnp.int32)[None, :] - reach - jnp.arange(tile_rows, dtype=jnp.int32)[:, None]
    row_blur = blur_weight(row_diff, reach).astype(jnp.bfloat16)
    return (col_blur, row_blur)

def sample_resist(resist, row_frac, col_frac, row_base, tile_rows):
    tile_cols = resist.shape[1]
    row_pos = row_frac * (tile_rows - 1)
    col_pos = col_frac * (tile_cols - 1)
    row_low = jnp.minimum(jnp.floor(row_pos), tile_rows - 2)
    col_low = jnp.minimum(jnp.floor(col_pos), tile_cols - 2)
    row_part = row_pos - row_low
    col_part = col_pos - col_low
    first_index = (row_low.astype(jnp.int32) + row_base) * tile_cols + col_low.astype(jnp.int32)
    flat_resist = resist.reshape(-1)
    upper_left = flat_resist[first_index]
    upper_right = flat_resist[first_index + 1]
    lower_left = flat_resist[first_index + tile_cols]
    lower_right = flat_resist[first_index + tile_cols + 1]
    top_line = (1.0 - col_part) * upper_left + col_part * upper_right
    bottom_line = (1.0 - col_part) * lower_left + col_part * lower_right
    return (1.0 - row_part) * top_line + row_part * bottom_line

def reference(mask, kernel_spectra, kernel_weights, threshold, eval_tile, site_coords, bias_steps):
    tables = imaging_tables(ROWS_DEV, COLS, WINDOW, ROW_FREQS, COL_FREQS, HALO)
    padded_mask = jnp.pad(mask, ((HALO, HALO), (0, 0)))

    def one_tile(tile_index):
        window = lax.dynamic_slice_in_dim(padded_mask, (tile_index * ROWS_DEV).astype(jnp.int32), WINDOW, 0)
        col_spectra = jnp.dot(window, tables[0], preferred_element_type=jnp.float32).astype(jnp.bfloat16)
        return tile_intensity(col_spectra, tables, kernel_spectra, kernel_weights)
    tile_numbers = jnp.arange(N_TX, dtype=jnp.int32)
    intensity = lax.map(one_tile, tile_numbers).reshape(REGION_ROWS, COLS)
    col_blur, row_blur = blur_tables(ROWS_DEV, COLS, BLUR_REACH)
    padded_intensity = jnp.pad(intensity, ((BLUR_REACH, BLUR_REACH), (0, 0)))
    col_blurred = jnp.dot(padded_intensity, col_blur, preferred_element_type=jnp.float32).astype(jnp.bfloat16)

    def blur_tile(tile_index):
        row_block = lax.dynamic_slice_in_dim(col_blurred, (tile_index * ROWS_DEV).astype(jnp.int32), ROWS_DEV + 2 * BLUR_REACH, 0)
        return jnp.dot(row_blur, row_block, preferred_element_type=jnp.float32)
    resist = lax.map(blur_tile, tile_numbers).reshape(REGION_ROWS, COLS)
    site_values = sample_resist(resist, site_coords[0], site_coords[1], eval_tile[None, :] * ROWS_DEV, ROWS_DEV)
    site_mean = lax.optimization_barrier(jnp.mean(site_values, axis=0))
    new_bias = bias_step * bias_steps.astype(jnp.float32) - bias_gain * (site_mean - threshold[0])
    return (resist, new_bias)
```

```python
import math

import jax
import jax.numpy as jnp
import ml_dtypes
import numpy as np
from jax import lax
from jax.experimental import pallas as pl
from jax.experimental.pallas import tpu as pltpu
from jax.sharding import PartitionSpec as P

HALO = 256
REACH = 8
SITES = 16
GRID_STEP = 4
BLOCK = 64
SIGMA = 3.0
CHUNKS = 4
BF = jnp.bfloat16
F32 = jnp.float32
MESH = pl.DeviceIdType.MESH
LOADED = ("mask", "colf", "rowf", "ev", "sc", "ks", "redges", "rinv", "cinv", "rmid", "redge", "wide_t", "bias")


def host_bf16(x):
    return np.asarray(x, np.float32).astype(ml_dtypes.bfloat16)


def twiddle(position, frequency, period, amplitude):
    index = (position[:, None] * frequency[None, :]) % period
    angle = index.astype(np.float64) * (2.0 * math.pi / period)
    return np.cos(angle) * amplitude, np.sin(angle) * amplitude


def gauss(offset):
    every = np.arange(-REACH, REACH + 1)
    norm = np.sum(np.exp(-every * every / (2.0 * SIGMA * SIGMA)))
    value = np.exp(-offset * offset / (2.0 * SIGMA * SIGMA)) / norm
    return np.where(np.abs(offset) <= REACH, value, 0.0)


def tables(rows, cols, row_freqs, col_freqs):
    window = rows + 2 * HALO
    f = np.arange(col_freqs) - col_freqs // 2
    g = np.arange(row_freqs) - row_freqs // 2
    c, s = twiddle(np.arange(cols), f, cols, 1.0 / math.sqrt(cols))
    col_forward = host_bf16(np.concatenate([c, -s], 1))
    c, s = twiddle(g, np.arange(window), window, 1.0 / math.sqrt(window))
    row_forward = host_bf16(np.concatenate([c, -s], 0))
    c, s = twiddle(np.arange(rows) + HALO, g, window, 1.0 / math.sqrt(row_freqs))
    row_inverse = host_bf16(np.block([[c, -s], [s, c]]))
    ends = np.r_[0:REACH, rows - REACH:rows]
    inverse_ends = np.ascontiguousarray(row_inverse[np.concatenate([ends, rows + ends])])
    row_forward = np.concatenate([
        row_forward[:, HALO:HALO + rows], row_forward[:, HALO + rows:], row_forward[:, :HALO]], 0)
    picked = np.arange(0, cols, GRID_STEP)
    c, s = twiddle(f, picked, cols, 1.0 / math.sqrt(col_freqs))
    col_inverse = host_bf16(np.block([[c, s], [-s, c]]))
    diff = np.arange(cols)[None, :] - picked[:, None]
    order = np.arange(1, col_freqs)
    base = np.arange(cols)
    kernel = 1.0 + 2.0 * np.cos(2 * math.pi * ((base[:, None] * order[None, :]) % cols) / cols).sum(1)
    kernel = (kernel + np.cos(2 * math.pi * ((base * col_freqs) % cols) / cols)) / picked.size
    interp = kernel[diff % cols]
    lines = np.arange(cols)
    col_blur = host_bf16(gauss((lines[None, :] - lines[:, None]).astype(np.float64)))
    spread = interp @ col_blur.astype(np.float64)
    high = host_bf16(spread)
    wide = np.ascontiguousarray(high.reshape(picked.size, CHUNKS, cols // CHUNKS).transpose(1, 0, 2))
    sums = spread.sum(0).astype(np.float32)[None]
    row_diff = np.arange(rows + 2 * REACH)[None, :] - REACH - np.arange(rows)[:, None]
    row_blur = host_bf16(gauss(row_diff.astype(np.float64)))
    row_mid = np.ascontiguousarray(row_blur[:, REACH:REACH + rows])
    row_edge = np.concatenate([row_blur[:, :REACH], row_blur[:, REACH + rows:]], 1)
    return (col_forward, row_forward, row_inverse, inverse_ends, col_inverse, row_mid, row_edge, wide,
            np.ascontiguousarray(high.T), sums)


def dot(a, b):
    return jnp.dot(a, b, preferred_element_type=F32)


def dot_nt(a, b):
    return lax.dot_general(a, b, (((1,), (1,)), ((), ())), preferred_element_type=F32)


def split3(x):
    high = x.astype(BF)
    rest = x - high.astype(F32)
    mid = rest.astype(BF)
    low = (rest - mid.astype(F32)).astype(BF)
    return jnp.concatenate([high, mid, low], axis=0)


def hat(distance):
    return jnp.maximum(1.0 - jnp.abs(distance), 0.0)


def kernel(weights_h, thresh_h, *refs):
    n = len(LOADED)
    sources = dict(zip(LOADED, refs[:n]))
    tile_h, bias_out, center_out = refs[n:n + 3]
    held = dict(zip(LOADED, refs[n + 3:2 * n + 3]))
    (weights, thresh, psnd, prec, prod, snd, recs, inten, hsnd, halo, rsnd, ret, sel, tile, rt,
     local_sem, send_sem, recv_sem) = refs[2 * n + 3:]
    mask, colf, rowf, ev, sc, ksv, rends, rinv, cinv, rmid, redge, wide_t, bias = (held[k] for k in LOADED)
    t = lax.axis_index("tx")
    count = lax.axis_size("tx")
    has_left = t > 0
    has_right = t < count - 1
    rows, cols = mask.shape
    coarse = cols // GRID_STEP
    kernels, row_freqs, col_freqs = ksv.shape[1:]
    frags = ev.shape[1]
    cap = frags // 2

    barrier = pltpu.get_barrier_semaphore()

    @pl.when(has_left)
    def _():
        pl.semaphore_signal(barrier, inc=1, device_id={"tx": t - 1}, device_id_type=MESH)

    @pl.when(has_right)
    def _():
        pl.semaphore_signal(barrier, inc=1, device_id={"tx": t + 1}, device_id_type=MESH)

    loads = {k: pltpu.make_async_copy(sources[k], held[k], local_sem.at[i])
             for i, k in enumerate(LOADED)}
    for k in LOADED:
        loads[k].start()
    load_weights = pltpu.make_async_copy(weights_h, weights, local_sem.at[n])
    load_weights.start()
    load_thresh = pltpu.make_async_copy(thresh_h, thresh, local_sem.at[n + 1])
    load_thresh.start()

    def to_left(kind, src, dst):
        return pltpu.make_async_remote_copy(
            src_ref=src, dst_ref=dst, send_sem=send_sem.at[kind, 0], recv_sem=recv_sem.at[kind, 0],
            device_id={"tx": t - 1}, device_id_type=MESH)

    def to_right(kind, src, dst):
        return pltpu.make_async_remote_copy(
            src_ref=src, dst_ref=dst, send_sem=send_sem.at[kind, 1], recv_sem=recv_sem.at[kind, 1],
            device_id={"tx": t + 1}, device_id_type=MESH)

    pairs = (
        (to_left(0, psnd.at[0], prec.at[1]), to_right(0, psnd.at[1], prec.at[0])),
        (to_left(1, snd.at[0], recs.at[2]), to_right(1, snd.at[2], recs.at[0])),
        (to_left(2, hsnd.at[0], halo.at[1]), to_right(2, hsnd.at[1], halo.at[0])),
        (to_left(3, rsnd.at[0], ret.at[2]), to_right(3, rsnd.at[2], ret.at[0])),
    )

    def start(kind):
        @pl.when(has_left)
        def _():
            pairs[kind][0].start()

        @pl.when(has_right)
        def _():
            pairs[kind][1].start()

    def arrive(kind):
        @pl.when(has_right)
        def _():
            pairs[kind][0].wait_recv()

        @pl.when(has_left)
        def _():
            pairs[kind][1].wait_recv()

    @pl.when(jnp.logical_not(has_left))
    def _():
        prec[0] = jnp.zeros(prec.shape[1:], BF)
        recs[0] = jnp.zeros(recs.shape[1:], F32)
        halo[0] = jnp.zeros(halo.shape[1:], F32)
        ret[0] = jnp.zeros(ret.shape[1:], F32)

    @pl.when(jnp.logical_not(has_right))
    def _():
        prec[1] = jnp.zeros(prec.shape[1:], BF)
        recs[2] = jnp.zeros(recs.shape[1:], F32)
        halo[1] = jnp.zeros(halo.shape[1:], F32)
        ret[2] = jnp.zeros(ret.shape[1:], F32)

    loads["mask"].wait()
    loads["colf"].wait()
    win = dot(mask[...], colf[...]).astype(BF)
    loads["rowf"].wait()
    product = dot(rowf[...], win)

    def spectrum(i):
        base = 2 * row_freqs * i
        upper = product[base:base + row_freqs]
        lower = product[base + row_freqs:base + 2 * row_freqs]
        return (upper[:, :col_freqs] - lower[:, col_freqs:], upper[:, col_freqs:] + lower[:, :col_freqs])

    own_real, own_imag = spectrum(0)
    for i in range(2):
        psnd[i] = jnp.concatenate(spectrum(i + 1), axis=1).astype(BF)

    between = jnp.logical_and(has_left, has_right)

    @pl.when(between)
    def _():
        pl.semaphore_wait(barrier, 2)

    @pl.when(jnp.logical_not(between))
    def _():
        pl.semaphore_wait(barrier, 1)

    start(0)

    loads["ev"].wait()
    loads["sc"].wait()
    offset = ev[...] - t + 1
    member = jnp.where(lax.broadcasted_iota(jnp.int32, (8, frags), 0) == offset, 1.0, 0.0)
    upper = jnp.where(
        lax.broadcasted_iota(jnp.int32, (frags, frags), 0)
        <= lax.broadcasted_iota(jnp.int32, (frags, frags), 1), 1.0, 0.0).astype(BF)
    inclusive = dot(member.astype(BF), upper)
    rank = jnp.sum(member * (inclusive - 1.0), axis=0, keepdims=True)
    slot = offset.astype(F32) * float(cap) + rank
    slot_line = lax.broadcasted_iota(jnp.int32, (3 * cap, frags), 0).astype(F32)
    sel[...] = jnp.where(slot_line == slot, 1.0, 0.0).astype(BF)
    records = jnp.concatenate([sc[0], sc[1]], axis=0)
    packed = dot_nt(split3(records), sel[...])
    n_rec = 2 * SITES
    packed = packed[:n_rec] + packed[n_rec:2 * n_rec] + packed[2 * n_rec:]
    snd[0] = packed[:, :cap]
    recs[1] = packed[:, cap:2 * cap]
    snd[2] = packed[:, 2 * cap:]
    start(1)

    for k in ("ks", "redges", "rinv", "cinv", "rmid", "redge"):
        loads[k].wait()
    load_weights.wait()
    arrive(0)
    near = prec[0].astype(F32) + prec[1].astype(F32)
    real = own_real + near[:, :col_freqs]
    imag = own_imag + near[:, col_freqs:]

    half = cinv.shape[1] // 2
    pairs_n = kernels // 2
    ends = []
    for pair in range(pairs_n):
        blocks = []
        for k in (2 * pair, 2 * pair + 1):
            kr = ksv[0, k]
            ki = ksv[1, k]
            blocks.append(jnp.concatenate(
                [(kr * real - ki * imag).astype(BF), (kr * imag + ki * real).astype(BF)], axis=0))
        block = jnp.concatenate(blocks, axis=1)
        prod[pair] = block
        field = dot(rends[...], block).astype(BF)
        for i in range(2):
            part = field[:, i * col_freqs:(i + 1) * col_freqs]
            ends.append(jnp.concatenate([part[:2 * REACH], part[2 * REACH:]], axis=1))
    e = dot(jnp.concatenate(ends, axis=0), cinv[...])
    total = jnp.zeros((2 * REACH, half), F32)
    for k in range(kernels):
        er = e[2 * REACH * k:2 * REACH * (k + 1), :half]
        ei = e[2 * REACH * k:2 * REACH * (k + 1), half:]
        total = total + weights[k] * (er * er + ei * ei)
    rounded = total.astype(BF).astype(F32)
    hsnd[0] = rounded[:REACH]
    hsnd[1] = rounded[REACH:]
    start(2)

    total = jnp.zeros((rows, half), F32)
    for pair in range(pairs_n):
        field = dot(rinv[...], prod[pair]).astype(BF)
        for i in range(2):
            part = field[:, i * col_freqs:(i + 1) * col_freqs]
            e = dot(jnp.concatenate([part[:rows], part[rows:]], axis=1), cinv[...])
            er = e[:, :half]
            ei = e[:, half:]
            total = total + weights[2 * pair + i] * (er * er + ei * ei)

    rounded = total.astype(BF)
    inten[...] = rounded
    center = jnp.sum(total) * (1.0 / (rows * half))
    blurred = dot(rmid[...], inten[...])
    arrive(2)
    edge = jnp.concatenate([halo[0], halo[1]], axis=0).astype(BF)
    blurred = blurred + dot(redge[...], edge)
    high = blurred.astype(BF)
    low = (blurred - high.astype(F32)).astype(BF)
    loads["wide_t"].wait()
    rt[...] = (dot_nt(wide_t[...], high) + dot_nt(wide_t[...], low) - center).astype(BF)
    tile[...] = (blurred - center).astype(BF)
    center_out[...] = jnp.zeros(center_out.shape, F32) + center
    store = pltpu.make_async_copy(tile, tile_h, local_sem.at[n + 2])
    store.start()
    arrive(1)

    blocks_n = cols // BLOCK
    row_line = lax.broadcasted_iota(jnp.int32, (rows, cap), 0).astype(F32)
    col_line = lax.broadcasted_iota(jnp.int32, (BLOCK, cap), 0).astype(F32)
    end_line = lax.broadcasted_iota(jnp.int32, (8, cap), 0).astype(F32) + float(BLOCK)

    def evaluate(block):
        def one(s, acc):
            p = recs[block, pl.ds(s, 1), :] * float(rows - 1)
            q = recs[block, pl.ds(SITES + s, 1), :] * float(cols - 1)
            wr = hat(row_line - p).astype(BF)
            lines = dot(rt[...], wr)
            h = jnp.floor(q * (1.0 / BLOCK))
            local = q - h * float(BLOCK)
            chosen = lines[:BLOCK]
            after = jnp.zeros((8, cap), F32)
            for k in range(1, blocks_n):
                here = lines[k * BLOCK:(k + 1) * BLOCK]
                chosen = jnp.where(h == float(k), here, chosen)
                after = jnp.where(h == float(k - 1), here[:8], after)
            weighted = chosen * hat(col_line - local)
            for g in range(BLOCK // 8):
                acc = acc + weighted[g * 8:(g + 1) * 8]
            return acc + after * hat(end_line - local)

        def step(i, acc):
            for j in range(8):
                acc = one(8 * i + j, acc)
            return acc

        acc = lax.fori_loop(0, SITES // 8, step, jnp.zeros((8, cap), F32))
        mean = jnp.sum(acc, axis=0, keepdims=True) * (1.0 / SITES) + center
        return jnp.broadcast_to(mean, (8, cap))

    rsnd[0] = evaluate(0)
    rsnd[2] = evaluate(2)
    start(3)
    ret[1] = evaluate(1)
    arrive(3)
    back = jnp.concatenate([ret[0], ret[1], ret[2]], axis=1)
    found = dot(split3(back), sel[...])
    mean = found[0:1] + found[8:9] + found[16:17]
    load_thresh.wait()
    loads["bias"].wait()
    bias_out[...] = 0.5 * bias[...].astype(F32) - 2.0 * (mean - thresh[0, 0]).reshape(frags)

    for kind in range(4):
        @pl.when(has_left)
        def _():
            pairs[kind][0].wait_send()

        @pl.when(has_right)
        def _():
            pairs[kind][1].wait_send()
    store.wait()


def finish(tile_h, wide_h, sums_h, center_h, bias_h, resist_h, nb_h, tile, wide, sums, center, out, sem):
    chunks = wide.shape[0]
    width = wide.shape[2]
    first = pltpu.make_async_copy(tile_h, tile, sem.at[0])
    second = pltpu.make_async_copy(center_h, center, sem.at[1])
    third = pltpu.make_async_copy(sums_h, sums, sem.at[2])
    through = pltpu.make_async_copy(bias_h, nb_h, sem.at[3])
    loads = [pltpu.make_async_copy(wide_h.at[i], wide.at[i], sem.at[4 + i]) for i in range(chunks)]
    stores = [pltpu.make_async_copy(out.at[i], resist_h.at[:, pl.ds(i * width, width)], sem.at[4 + chunks + i])
              for i in range(chunks)]
    first.start()
    loads[0].start()
    second.start()
    third.start()
    for load in loads[1:]:
        load.start()
    through.start()
    first.wait()
    second.wait()
    third.wait()
    for i in range(chunks):
        loads[i].wait()
        out[i] = dot(tile[...], wide[i]) + center[0:1, 0:1] * sums[0:1, i * width:(i + 1) * width]
        stores[i].start()
    for store in stores:
        store.wait()
    through.wait()


def shards(mask, kernel_spectra, kernel_weights, threshold, eval_tile, site_coords, bias_steps):
    rows, cols = mask.shape
    row_freqs, kernels, col_freqs = kernel_spectra.shape[1:]
    frags = eval_tile.shape[0]
    cap = frags // 2
    names = ("colf", "rowf", "rinv", "redges", "cinv", "rmid", "redge", "wide", "wide_t", "sums")
    values = dict(zip(names, (jnp.asarray(x) for x in tables(rows, cols, row_freqs, col_freqs))))
    values["mask"] = mask
    values["ks"] = jnp.transpose(kernel_spectra, (0, 2, 1, 3))
    values["ev"] = eval_tile.reshape(1, frags)
    values["sc"] = site_coords
    values["bias"] = bias_steps
    ordered = [values[k] for k in LOADED]
    vmem = pl.BlockSpec(memory_space=pltpu.VMEM)
    hbm = pl.BlockSpec(memory_space=pltpu.HBM)
    anyw = pl.BlockSpec(memory_space=pl.ANY)
    coarse = cols // GRID_STEP
    tile, new_bias, center = pl.pallas_call(
        kernel,
        out_shape=(jax.ShapeDtypeStruct((rows, coarse), BF), jax.ShapeDtypeStruct((frags,), F32),
                   jax.ShapeDtypeStruct((8, 128), F32)),
        in_specs=[hbm] * (2 + len(ordered)),
        out_specs=(anyw, vmem, vmem),
        scratch_shapes=[pltpu.VMEM(x.shape, x.dtype) for x in ordered] + [
            pltpu.SMEM((kernels,), F32),
            pltpu.SMEM((1, 1), F32),
            pltpu.VMEM((2, row_freqs, 2 * col_freqs), BF),
            pltpu.VMEM((2, row_freqs, 2 * col_freqs), BF),
            pltpu.VMEM((kernels // 2, 2 * row_freqs, 2 * col_freqs), BF),
            pltpu.VMEM((3, 2 * SITES, cap), F32),
            pltpu.VMEM((3, 2 * SITES, cap), F32),
            pltpu.VMEM((rows, coarse), BF),
            pltpu.VMEM((2, REACH, coarse), F32),
            pltpu.VMEM((2, REACH, coarse), F32),
            pltpu.VMEM((3, 8, cap), F32),
            pltpu.VMEM((3, 8, cap), F32),
            pltpu.VMEM((3 * cap, frags), BF),
            pltpu.VMEM((rows, coarse), BF),
            pltpu.VMEM((cols, rows), BF),
            pltpu.SemaphoreType.DMA((len(ordered) + 3,)),
            pltpu.SemaphoreType.DMA((4, 2)),
            pltpu.SemaphoreType.DMA((4, 2)),
        ],
        compiler_params=pltpu.CompilerParams(
            collective_id=0, has_side_effects=True, vmem_limit_bytes=63 << 20),
    )(kernel_weights, threshold.reshape(1, 1), *ordered)
    width = cols // CHUNKS
    return pl.pallas_call(
        finish,
        out_shape=(jax.ShapeDtypeStruct((rows, cols), F32), jax.ShapeDtypeStruct((frags,), F32)),
        in_specs=[anyw] * 5,
        out_specs=(anyw, anyw),
        scratch_shapes=[
            pltpu.VMEM((rows, coarse), BF),
            pltpu.VMEM((CHUNKS, coarse, width), BF),
            pltpu.VMEM((1, cols), F32),
            pltpu.VMEM((8, 128), F32),
            pltpu.VMEM((CHUNKS, rows, width), F32),
            pltpu.SemaphoreType.DMA((4 + 2 * CHUNKS,)),
        ],
    )(tile, values["wide"], values["sums"], center, new_bias)


def solution(mesh):
    placed = (
        P(("groups", "tx"), None),
        P(),
        P(),
        P(),
        P(("groups", "tx")),
        P(None, None, ("groups", "tx")),
        P(("groups", "tx")),
    )
    return jax.shard_map(
        shards,
        mesh=mesh,
        in_specs=placed,
        out_specs=(P(("groups", "tx"), None), P(("groups", "tx"))),
        check_vma=False,
    )
```

```python
import math

import jax
import jax.numpy as jnp
import ml_dtypes
import numpy as np
from jax import lax
from jax.experimental import pallas as pl
from jax.experimental.pallas import tpu as pltpu
from jax.sharding import PartitionSpec as P

HALO = 256
REACH = 8
SITES = 16
GRID_STEP = 4
BLOCK = 64
SIGMA = 3.0
CHUNKS = 4
BF = jnp.bfloat16
F32 = jnp.float32
MESH = pl.DeviceIdType.MESH
LOADED = ("mask", "colf", "rowf", "ev", "sc", "ks", "redges", "rinv", "cinv", "rmid", "redge", "wide_t", "bias")


def host_bf16(x):
    return np.asarray(x, np.float32).astype(ml_dtypes.bfloat16)


def twiddle(position, frequency, period, amplitude):
    index = (position[:, None] * frequency[None, :]) % period
    angle = index.astype(np.float64) * (2.0 * math.pi / period)
    return np.cos(angle) * amplitude, np.sin(angle) * amplitude


def gauss(offset):
    every = np.arange(-REACH, REACH + 1)
    norm = np.sum(np.exp(-every * every / (2.0 * SIGMA * SIGMA)))
    value = np.exp(-offset * offset / (2.0 * SIGMA * SIGMA)) / norm
    return np.where(np.abs(offset) <= REACH, value, 0.0)


def tables(rows, cols, row_freqs, col_freqs):
    window = rows + 2 * HALO
    f = np.arange(col_freqs) - col_freqs // 2
    g = np.arange(row_freqs) - row_freqs // 2
    c, s = twiddle(np.arange(cols), f, cols, 1.0 / math.sqrt(cols))
    col_forward = host_bf16(np.concatenate([c, -s], 1))
    c, s = twiddle(g, np.arange(window), window, 1.0 / math.sqrt(window))
    row_forward = host_bf16(np.concatenate([c, -s], 0))
    c, s = twiddle(np.arange(rows) + HALO, g, window, 1.0 / math.sqrt(row_freqs))
    row_inverse = host_bf16(np.block([[c, -s], [s, c]]))
    ends = np.r_[0:REACH, rows - REACH:rows]
    inverse_ends = np.ascontiguousarray(row_inverse[np.concatenate([ends, rows + ends])])
    row_forward = np.concatenate([
        row_forward[:, HALO:HALO + rows], row_forward[:, HALO + rows:], row_forward[:, :HALO]], 0)
    picked = np.arange(0, cols, GRID_STEP)
    c, s = twiddle(f, picked, cols, 1.0 / math.sqrt(col_freqs))
    col_inverse = host_bf16(np.block([[c, s], [-s, c]]))
    diff = np.arange(cols)[None, :] - picked[:, None]
    order = np.arange(1, col_freqs)
    base = np.arange(cols)
    kernel = 1.0 + 2.0 * np.cos(2 * math.pi * ((base[:, None] * order[None, :]) % cols) / cols).sum(1)
    kernel = (kernel + np.cos(2 * math.pi * ((base * col_freqs) % cols) / cols)) / picked.size
    interp = kernel[diff % cols]
    lines = np.arange(cols)
    col_blur = host_bf16(gauss((lines[None, :] - lines[:, None]).astype(np.float64)))
    spread = interp @ col_blur.astype(np.float64)
    high = host_bf16(spread)
    wide = np.ascontiguousarray(high.reshape(picked.size, CHUNKS, cols // CHUNKS).transpose(1, 0, 2))
    sums = spread.sum(0).astype(np.float32)[None]
    row_diff = np.arange(rows + 2 * REACH)[None, :] - REACH - np.arange(rows)[:, None]
    row_blur = host_bf16(gauss(row_diff.astype(np.float64)))
    row_mid = np.ascontiguousarray(row_blur[:, REACH:REACH + rows])
    row_edge = np.concatenate([row_blur[:, :REACH], row_blur[:, REACH + rows:]], 1)
    return (col_forward, row_forward, row_inverse, inverse_ends, col_inverse, row_mid, row_edge, wide,
            np.ascontiguousarray(high.T), sums)


def dot(a, b):
    return jnp.dot(a, b, preferred_element_type=F32)


def dot_nt(a, b):
    return lax.dot_general(a, b, (((1,), (1,)), ((), ())), preferred_element_type=F32)


def split3(x):
    high = x.astype(BF)
    rest = x - high.astype(F32)
    mid = rest.astype(BF)
    low = (rest - mid.astype(F32)).astype(BF)
    return jnp.concatenate([high, mid, low], axis=0)


def hat(distance):
    return jnp.maximum(1.0 - jnp.abs(distance), 0.0)


def kernel(weights_h, thresh_h, *refs):
    n = len(LOADED)
    sources = dict(zip(LOADED, refs[:n]))
    tile_h, bias_out, center_out = refs[n:n + 3]
    held = dict(zip(LOADED, refs[n + 3:2 * n + 3]))
    (weights, thresh, psnd, prec, prod, snd, recs, inten, hsnd, halo, rsnd, ret, sel, tile, rt,
     local_sem, send_sem, recv_sem) = refs[2 * n + 3:]
    mask, colf, rowf, ev, sc, ksv, rends, rinv, cinv, rmid, redge, wide_t, bias = (held[k] for k in LOADED)
    t = lax.axis_index("tx")
    count = lax.axis_size("tx")
    has_left = t > 0
    has_right = t < count - 1
    rows, cols = mask.shape
    coarse = cols // GRID_STEP
    kernels, row_freqs, col_freqs = ksv.shape[1:]
    frags = ev.shape[1]
    cap = frags // 2

    barrier = pltpu.get_barrier_semaphore()

    @pl.when(has_left)
    def _():
        pl.semaphore_signal(barrier, inc=1, device_id={"tx": t - 1}, device_id_type=MESH)

    @pl.when(has_right)
    def _():
        pl.semaphore_signal(barrier, inc=1, device_id={"tx": t + 1}, device_id_type=MESH)

    loads = {k: pltpu.make_async_copy(sources[k], held[k], local_sem.at[i])
             for i, k in enumerate(LOADED)}
    for k in LOADED:
        loads[k].start()
    load_weights = pltpu.make_async_copy(weights_h, weights, local_sem.at[n])
    load_weights.start()
    load_thresh = pltpu.make_async_copy(thresh_h, thresh, local_sem.at[n + 1])
    load_thresh.start()

    def to_left(kind, src, dst):
        return pltpu.make_async_remote_copy(
            src_ref=src, dst_ref=dst, send_sem=send_sem.at[kind, 0], recv_sem=recv_sem.at[kind, 0],
            device_id={"tx": t - 1}, device_id_type=MESH)

    def to_right(kind, src, dst):
        return pltpu.make_async_remote_copy(
            src_ref=src, dst_ref=dst, send_sem=send_sem.at[kind, 1], recv_sem=recv_sem.at[kind, 1],
            device_id={"tx": t + 1}, device_id_type=MESH)

    pairs = (
        (to_left(0, psnd.at[0], prec.at[1]), to_right(0, psnd.at[1], prec.at[0])),
        (to_left(1, snd.at[0], recs.at[2]), to_right(1, snd.at[2], recs.at[0])),
        (to_left(2, hsnd.at[0], halo.at[1]), to_right(2, hsnd.at[1], halo.at[0])),
        (to_left(3, rsnd.at[0], ret.at[2]), to_right(3, rsnd.at[2], ret.at[0])),
    )

    def start(kind):
        @pl.when(has_left)
        def _():
            pairs[kind][0].start()

        @pl.when(has_right)
        def _():
            pairs[kind][1].start()

    def arrive(kind):
        @pl.when(has_right)
        def _():
            pairs[kind][0].wait_recv()

        @pl.when(has_left)
        def _():
            pairs[kind][1].wait_recv()

    @pl.when(jnp.logical_not(has_left))
    def _():
        prec[0] = jnp.zeros(prec.shape[1:], BF)
        recs[0] = jnp.zeros(recs.shape[1:], F32)
        halo[0] = jnp.zeros(halo.shape[1:], F32)
        ret[0] = jnp.zeros(ret.shape[1:], F32)

    @pl.when(jnp.logical_not(has_right))
    def _():
        prec[1] = jnp.zeros(prec.shape[1:], BF)
        recs[2] = jnp.zeros(recs.shape[1:], F32)
        halo[1] = jnp.zeros(halo.shape[1:], F32)
        ret[2] = jnp.zeros(ret.shape[1:], F32)

    loads["mask"].wait()
    loads["colf"].wait()
    win = dot(mask[...], colf[...]).astype(BF)
    loads["rowf"].wait()
    product = dot(rowf[...], win)

    def spectrum(i):
        base = 2 * row_freqs * i
        upper = product[base:base + row_freqs]
        lower = product[base + row_freqs:base + 2 * row_freqs]
        return (upper[:, :col_freqs] - lower[:, col_freqs:], upper[:, col_freqs:] + lower[:, :col_freqs])

    own_real, own_imag = spectrum(0)
    for i in range(2):
        psnd[i] = jnp.concatenate(spectrum(i + 1), axis=1).astype(BF)

    between = jnp.logical_and(has_left, has_right)

    @pl.when(between)
    def _():
        pl.semaphore_wait(barrier, 2)

    @pl.when(jnp.logical_not(between))
    def _():
        pl.semaphore_wait(barrier, 1)

    start(0)

    loads["ev"].wait()
    loads["sc"].wait()
    offset = ev[...] - t + 1
    member = jnp.where(lax.broadcasted_iota(jnp.int32, (8, frags), 0) == offset, 1.0, 0.0)
    upper = jnp.where(
        lax.broadcasted_iota(jnp.int32, (frags, frags), 0)
        <= lax.broadcasted_iota(jnp.int32, (frags, frags), 1), 1.0, 0.0).astype(BF)
    inclusive = dot(member.astype(BF), upper)
    rank = jnp.sum(member * (inclusive - 1.0), axis=0, keepdims=True)
    slot = offset.astype(F32) * float(cap) + rank
    slot_line = lax.broadcasted_iota(jnp.int32, (3 * cap, frags), 0).astype(F32)
    sel[...] = jnp.where(slot_line == slot, 1.0, 0.0).astype(BF)
    records = jnp.concatenate([sc[0], sc[1]], axis=0)
    packed = dot_nt(split3(records), sel[...])
    n_rec = 2 * SITES
    packed = packed[:n_rec] + packed[n_rec:2 * n_rec] + packed[2 * n_rec:]
    snd[0] = packed[:, :cap]
    recs[1] = packed[:, cap:2 * cap]
    snd[2] = packed[:, 2 * cap:]
    start(1)

    for k in ("ks", "redges", "rinv", "cinv", "rmid", "redge"):
        loads[k].wait()
    load_weights.wait()
    arrive(0)
    near = prec[0].astype(F32) + prec[1].astype(F32)
    real = own_real + near[:, :col_freqs]
    imag = own_imag + near[:, col_freqs:]

    half = cinv.shape[1] // 2
    pairs_n = kernels // 2
    ends = []
    for pair in range(pairs_n):
        blocks = []
        for k in (2 * pair, 2 * pair + 1):
            kr = ksv[0, k]
            ki = ksv[1, k]
            blocks.append(jnp.concatenate(
                [(kr * real - ki * imag).astype(BF), (kr * imag + ki * real).astype(BF)], axis=0))
        block = jnp.concatenate(blocks, axis=1)
        prod[pair] = block
        field = dot(rends[...], block).astype(BF)
        for i in range(2):
            part = field[:, i * col_freqs:(i + 1) * col_freqs]
            ends.append(jnp.concatenate([part[:2 * REACH], part[2 * REACH:]], axis=1))
    e = dot(jnp.concatenate(ends, axis=0), cinv[...])
    total = jnp.zeros((2 * REACH, half), F32)
    for k in range(kernels):
        er = e[2 * REACH * k:2 * REACH * (k + 1), :half]
        ei = e[2 * REACH * k:2 * REACH * (k + 1), half:]
        total = total + weights[k] * (er * er + ei * ei)
    rounded = total.astype(BF).astype(F32)
    hsnd[0] = rounded[:REACH]
    hsnd[1] = rounded[REACH:]
    start(2)

    total = jnp.zeros((rows, half), F32)
    for pair in range(pairs_n):
        field = dot(rinv[...], prod[pair]).astype(BF)
        for i in range(2):
            part = field[:, i * col_freqs:(i + 1) * col_freqs]
            e = dot(jnp.concatenate([part[:rows], part[rows:]], axis=1), cinv[...])
            er = e[:, :half]
            ei = e[:, half:]
            total = total + weights[2 * pair + i] * (er * er + ei * ei)

    rounded = total.astype(BF)
    inten[...] = rounded
    center = jnp.sum(total) * (1.0 / (rows * half))
    blurred = dot(rmid[...], inten[...])
    arrive(2)
    edge = jnp.concatenate([halo[0], halo[1]], axis=0).astype(BF)
    blurred = blurred + dot(redge[...], edge)
    high = blurred.astype(BF)
    low = (blurred - high.astype(F32)).astype(BF)
    loads["wide_t"].wait()
    rt[...] = (dot_nt(wide_t[...], high) + dot_nt(wide_t[...], low) - center).astype(BF)
    tile[...] = (blurred - center).astype(BF)
    center_out[...] = jnp.zeros(center_out.shape, F32) + center
    store = pltpu.make_async_copy(tile, tile_h, local_sem.at[n + 2])
    store.start()
    arrive(1)

    blocks_n = cols // BLOCK
    row_line = lax.broadcasted_iota(jnp.int32, (rows, cap), 0).astype(F32)
    col_line = lax.broadcasted_iota(jnp.int32, (BLOCK, cap), 0).astype(F32)
    end_line = lax.broadcasted_iota(jnp.int32, (8, cap), 0).astype(F32) + float(BLOCK)

    def evaluate(block):
        def one(s, acc):
            p = recs[block, pl.ds(s, 1), :] * float(rows - 1)
            q = recs[block, pl.ds(SITES + s, 1), :] * float(cols - 1)
            wr = hat(row_line - p).astype(BF)
            lines = dot(rt[...], wr)
            h = jnp.floor(q * (1.0 / BLOCK))
            local = q - h * float(BLOCK)
            chosen = lines[:BLOCK]
            after = jnp.zeros((8, cap), F32)
            for k in range(1, blocks_n):
                here = lines[k * BLOCK:(k + 1) * BLOCK]
                chosen = jnp.where(h == float(k), here, chosen)
                after = jnp.where(h == float(k - 1), here[:8], after)
            weighted = chosen * hat(col_line - local)
            for g in range(BLOCK // 8):
                acc = acc + weighted[g * 8:(g + 1) * 8]
            return acc + after * hat(end_line - local)

        def step(i, acc):
            for j in range(8):
                acc = one(8 * i + j, acc)
            return acc

        acc = lax.fori_loop(0, SITES // 8, step, jnp.zeros((8, cap), F32))
        mean = jnp.sum(acc, axis=0, keepdims=True) * (1.0 / SITES) + center
        return jnp.broadcast_to(mean, (8, cap))

    rsnd[0] = evaluate(0)
    rsnd[2] = evaluate(2)
    start(3)
    ret[1] = evaluate(1)
    arrive(3)
    back = jnp.concatenate([ret[0], ret[1], ret[2]], axis=1)
    found = dot(split3(back), sel[...])
    mean = found[0:1] + found[8:9] + found[16:17]
    load_thresh.wait()
    loads["bias"].wait()
    bias_out[...] = 0.5 * bias[...].astype(F32) - 2.0 * (mean - thresh[0, 0]).reshape(frags)

    for kind in range(4):
        @pl.when(has_left)
        def _():
            pairs[kind][0].wait_send()

        @pl.when(has_right)
        def _():
            pairs[kind][1].wait_send()
    store.wait()


def finish(tile, wide, sums, center, bias_h, resist_h, nb_h, out, sem):
    chunks = wide.shape[0]
    width = wide.shape[2]
    through = pltpu.make_async_copy(bias_h, nb_h, sem.at[3])
    stores = [pltpu.make_async_copy(out.at[i], resist_h.at[:, pl.ds(i * width, width)], sem.at[4 + chunks + i])
              for i in range(chunks)]
    through.start()
    for i in range(chunks):
        out[i] = dot(tile[...], wide[i]) + center[0:1, 0:1] * sums[0:1, i * width:(i + 1) * width]
        stores[i].start()
    for store in stores:
        store.wait()
    through.wait()


def shards(mask, kernel_spectra, kernel_weights, threshold, eval_tile, site_coords, bias_steps):
    rows, cols = mask.shape
    row_freqs, kernels, col_freqs = kernel_spectra.shape[1:]
    frags = eval_tile.shape[0]
    cap = frags // 2
    names = ("colf", "rowf", "rinv", "redges", "cinv", "rmid", "redge", "wide", "wide_t", "sums")
    values = dict(zip(names, (jnp.asarray(x) for x in tables(rows, cols, row_freqs, col_freqs))))
    values["mask"] = mask
    values["ks"] = jnp.transpose(kernel_spectra, (0, 2, 1, 3))
    values["ev"] = eval_tile.reshape(1, frags)
    values["sc"] = site_coords
    values["bias"] = bias_steps
    ordered = [values[k] for k in LOADED]
    vmem = pl.BlockSpec(memory_space=pltpu.VMEM)
    hbm = pl.BlockSpec(memory_space=pltpu.HBM)
    anyw = pl.BlockSpec(memory_space=pl.ANY)
    coarse = cols // GRID_STEP
    tile, new_bias, center = pl.pallas_call(
        kernel,
        out_shape=(pltpu.VMEM((rows, coarse), BF), pltpu.VMEM((frags,), F32), pltpu.VMEM((8, 128), F32)),
        in_specs=[hbm] * (2 + len(ordered)),
        out_specs=(anyw, vmem, vmem),
        scratch_shapes=[pltpu.VMEM(x.shape, x.dtype) for x in ordered] + [
            pltpu.SMEM((kernels,), F32),
            pltpu.SMEM((1, 1), F32),
            pltpu.VMEM((2, row_freqs, 2 * col_freqs), BF),
            pltpu.VMEM((2, row_freqs, 2 * col_freqs), BF),
            pltpu.VMEM((kernels // 2, 2 * row_freqs, 2 * col_freqs), BF),
            pltpu.VMEM((3, 2 * SITES, cap), F32),
            pltpu.VMEM((3, 2 * SITES, cap), F32),
            pltpu.VMEM((rows, coarse), BF),
            pltpu.VMEM((2, REACH, coarse), F32),
            pltpu.VMEM((2, REACH, coarse), F32),
            pltpu.VMEM((3, 8, cap), F32),
            pltpu.VMEM((3, 8, cap), F32),
            pltpu.VMEM((3 * cap, frags), BF),
            pltpu.VMEM((rows, coarse), BF),
            pltpu.VMEM((cols, rows), BF),
            pltpu.SemaphoreType.DMA((len(ordered) + 3,)),
            pltpu.SemaphoreType.DMA((4, 2)),
            pltpu.SemaphoreType.DMA((4, 2)),
        ],
        compiler_params=pltpu.CompilerParams(
            collective_id=0, has_side_effects=True, vmem_limit_bytes=int(60 * 2 ** 20)),
    )(kernel_weights, threshold.reshape(1, 1), *ordered)
    width = cols // CHUNKS
    return pl.pallas_call(
        finish,
        out_shape=(jax.ShapeDtypeStruct((rows, cols), F32), jax.ShapeDtypeStruct((frags,), F32)),
        in_specs=[vmem] * 4 + [anyw],
        out_specs=(anyw, anyw),
        scratch_shapes=[
            pltpu.VMEM((CHUNKS, rows, width), F32),
            pltpu.SemaphoreType.DMA((4 + 2 * CHUNKS,)),
        ],
        compiler_params=pltpu.CompilerParams(vmem_limit_bytes=4 << 20),
    )(tile, values["wide"], values["sums"], center, new_bias)


def solution(mesh):
    placed = (
        P(("groups", "tx"), None),
        P(),
        P(),
        P(),
        P(("groups", "tx")),
        P(None, None, ("groups", "tx")),
        P(("groups", "tx")),
    )
    return jax.shard_map(
        shards,
        mesh=mesh,
        in_specs=placed,
        out_specs=(P(("groups", "tx"), None), P(("groups", "tx"))),
        check_vma=False,
    )
```

```python
import math

import jax
import jax.numpy as jnp
import ml_dtypes
import numpy as np
from jax import lax
from jax.experimental import pallas as pl
from jax.experimental.pallas import tpu as pltpu
from jax.sharding import PartitionSpec as P

HALO = 256
REACH = 8
SITES = 16
GRID_STEP = 4
STEPS = 8
SIGMA = 3.0
CHUNKS = 4
BF = jnp.bfloat16
F32 = jnp.float32
MESH = pl.DeviceIdType.MESH
LOADED = ("mask", "colf", "rowf", "ev", "sc", "ks", "redges", "rinv", "cinv", "rmid", "redge", "ftab", "btab", "bias")


def host_bf16(x):
    return np.asarray(x, np.float32).astype(ml_dtypes.bfloat16)


def twiddle(position, frequency, period, amplitude):
    index = (position[:, None] * frequency[None, :]) % period
    angle = index.astype(np.float64) * (2.0 * math.pi / period)
    return np.cos(angle) * amplitude, np.sin(angle) * amplitude


def gauss(offset):
    every = np.arange(-REACH, REACH + 1)
    norm = np.sum(np.exp(-every * every / (2.0 * SIGMA * SIGMA)))
    value = np.exp(-offset * offset / (2.0 * SIGMA * SIGMA)) / norm
    return np.where(np.abs(offset) <= REACH, value, 0.0)


def tables(rows, cols, row_freqs, col_freqs):
    window = rows + 2 * HALO
    f = np.arange(col_freqs) - col_freqs // 2
    g = np.arange(row_freqs) - row_freqs // 2
    c, s = twiddle(np.arange(cols), f, cols, 1.0 / math.sqrt(cols))
    col_forward = host_bf16(np.concatenate([c, -s], 1))
    c, s = twiddle(g, np.arange(window), window, 1.0 / math.sqrt(window))
    row_forward = host_bf16(np.concatenate([c, -s], 0))
    c, s = twiddle(np.arange(rows) + HALO, g, window, 1.0 / math.sqrt(row_freqs))
    row_inverse = host_bf16(np.block([[c, -s], [s, c]]))
    ends = np.r_[0:REACH, rows - REACH:rows]
    inverse_ends = np.ascontiguousarray(row_inverse[np.concatenate([ends, rows + ends])])
    row_forward = np.concatenate([
        row_forward[:, HALO:HALO + rows], row_forward[:, HALO + rows:], row_forward[:, :HALO]], 0)
    picked = np.arange(0, cols, GRID_STEP)
    c, s = twiddle(f, picked, cols, 1.0 / math.sqrt(col_freqs))
    col_inverse = host_bf16(np.block([[c, s], [-s, c]]))
    diff = np.arange(cols)[None, :] - picked[:, None]
    order = np.arange(1, col_freqs)
    base = np.arange(cols)
    kernel = 1.0 + 2.0 * np.cos(2 * math.pi * ((base[:, None] * order[None, :]) % cols) / cols).sum(1)
    kernel = (kernel + np.cos(2 * math.pi * ((base * col_freqs) % cols) / cols)) / picked.size
    interp = kernel[diff % cols]
    lines = np.arange(cols)
    col_blur = host_bf16(gauss((lines[None, :] - lines[:, None]).astype(np.float64)))
    spread = interp @ col_blur.astype(np.float64)
    high = host_bf16(spread)
    wide = np.ascontiguousarray(high.reshape(picked.size, CHUNKS, cols // CHUNKS).transpose(1, 0, 2))
    sums = spread.sum(0).astype(np.float32)[None]
    row_diff = np.arange(rows + 2 * REACH)[None, :] - REACH - np.arange(rows)[:, None]
    row_blur = host_bf16(gauss(row_diff.astype(np.float64)))
    row_mid = np.ascontiguousarray(row_blur[:, REACH:REACH + rows])
    row_edge = np.concatenate([row_blur[:, :REACH], row_blur[:, REACH + rows:]], 1)
    return (col_forward, row_forward, row_inverse, inverse_ends, col_inverse, row_mid, row_edge, wide,
            sums) + site_tables(cols, col_freqs, interp, spread)


def site_tables(cols, col_freqs, interp, spread):
    coarse = cols // GRID_STEP
    span = cols // STEPS
    line = np.arange(cols)
    reach = np.arange(-REACH, REACH + 1)
    weight = host_bf16(gauss(reach.astype(np.float64))).astype(np.float64)
    periodic = np.zeros((cols, cols))
    for d, w in zip(reach, weight):
        periodic[(line - d) % cols, line] += w
    order = np.concatenate([np.arange(j, col_freqs, STEPS) for j in range(STEPS)])
    angle = 2.0 * math.pi * ((np.arange(col_freqs + 1)[:, None] * reach[None, :]) % cols) / cols
    response = (weight[None, :] * np.cos(angle)).sum(1)
    scale = (np.where(order == 0, 1.0, 2.0) * response[order] / coarse)[:, None]
    angle = 2.0 * math.pi * ((order[:, None] * GRID_STEP * np.arange(coarse)[None, :]) % cols) / cols
    cosine, sine = scale * np.cos(angle), scale * np.sin(angle)
    sine[0] = response[col_freqs] / coarse * np.cos(math.pi * np.arange(coarse))
    ends = np.r_[0:REACH, cols - REACH:cols]
    lacking = (spread - interp @ periodic)[:, ends].T
    steps = np.arange(-(-(span + 1) // 16) * 16)
    angle = 2.0 * math.pi * ((order[:, None] * steps[None, :]) % cols) / cols
    base_cos, base_sin = np.cos(angle), np.sin(angle)
    base_sin[0] = np.cos(2.0 * math.pi * ((col_freqs * steps) % cols) / cols)
    return (host_bf16(np.concatenate([cosine, sine, lacking], 0)), host_bf16(np.concatenate([base_cos, base_sin], 0)))


BLUR_SUM = float(host_bf16(gauss(np.arange(-REACH, REACH + 1.0))).astype(np.float64).sum())


def dot(a, b):
    return jnp.dot(a, b, preferred_element_type=F32)


def dot_nt(a, b):
    return lax.dot_general(a, b, (((1,), (1,)), ((), ())), preferred_element_type=F32)


def split3(x):
    high = x.astype(BF)
    rest = x - high.astype(F32)
    mid = rest.astype(BF)
    low = (rest - mid.astype(F32)).astype(BF)
    return jnp.concatenate([high, mid, low], axis=0)


def hat(distance):
    return jnp.maximum(1.0 - jnp.abs(distance), 0.0)


def kernel(weights_h, thresh_h, *refs):
    n = len(LOADED)
    sources = dict(zip(LOADED, refs[:n]))
    tile_out, bias_out, center_out = refs[n:n + 3]
    held = dict(zip(LOADED, refs[n + 3:2 * n + 3]))
    (weights, thresh, psnd, prec, prod, snd, recs, inten, hsnd, halo, rsnd, ret, sel, that,
     local_sem, send_sem, recv_sem) = refs[2 * n + 3:]
    mask, colf, rowf, ev, sc, ksv, rends, rinv, cinv, rmid, redge, ftab, btab, bias = (held[k] for k in LOADED)
    t = lax.axis_index("tx")
    count = lax.axis_size("tx")
    has_left = t > 0
    has_right = t < count - 1
    rows, cols = mask.shape
    coarse = cols // GRID_STEP
    kernels, row_freqs, col_freqs = ksv.shape[1:]
    frags = ev.shape[1]
    cap = frags // 2

    barrier = pltpu.get_barrier_semaphore()

    @pl.when(has_left)
    def _():
        pl.semaphore_signal(barrier, inc=1, device_id={"tx": t - 1}, device_id_type=MESH)

    @pl.when(has_right)
    def _():
        pl.semaphore_signal(barrier, inc=1, device_id={"tx": t + 1}, device_id_type=MESH)

    loads = {k: pltpu.make_async_copy(sources[k], held[k], local_sem.at[i])
             for i, k in enumerate(LOADED)}
    for k in LOADED:
        loads[k].start()
    load_weights = pltpu.make_async_copy(weights_h, weights, local_sem.at[n])
    load_weights.start()
    load_thresh = pltpu.make_async_copy(thresh_h, thresh, local_sem.at[n + 1])
    load_thresh.start()

    def to_left(kind, src, dst):
        return pltpu.make_async_remote_copy(
            src_ref=src, dst_ref=dst, send_sem=send_sem.at[kind, 0], recv_sem=recv_sem.at[kind, 0],
            device_id={"tx": t - 1}, device_id_type=MESH)

    def to_right(kind, src, dst):
        return pltpu.make_async_remote_copy(
            src_ref=src, dst_ref=dst, send_sem=send_sem.at[kind, 1], recv_sem=recv_sem.at[kind, 1],
            device_id={"tx": t + 1}, device_id_type=MESH)

    pairs = (
        (to_left(0, psnd.at[0], prec.at[1]), to_right(0, psnd.at[1], prec.at[0])),
        (to_left(1, snd.at[0], recs.at[2]), to_right(1, snd.at[2], recs.at[0])),
        (to_left(2, hsnd.at[0], halo.at[1]), to_right(2, hsnd.at[1], halo.at[0])),
        (to_left(3, rsnd.at[0], ret.at[2]), to_right(3, rsnd.at[2], ret.at[0])),
    )

    def start(kind):
        @pl.when(has_left)
        def _():
            pairs[kind][0].start()

        @pl.when(has_right)
        def _():
            pairs[kind][1].start()

    def arrive(kind):
        @pl.when(has_right)
        def _():
            pairs[kind][0].wait_recv()

        @pl.when(has_left)
        def _():
            pairs[kind][1].wait_recv()

    @pl.when(jnp.logical_not(has_left))
    def _():
        prec[0] = jnp.zeros(prec.shape[1:], BF)
        recs[0] = jnp.zeros(recs.shape[1:], F32)
        halo[0] = jnp.zeros(halo.shape[1:], F32)
        ret[0] = jnp.zeros(ret.shape[1:], F32)

    @pl.when(jnp.logical_not(has_right))
    def _():
        prec[1] = jnp.zeros(prec.shape[1:], BF)
        recs[2] = jnp.zeros(recs.shape[1:], F32)
        halo[1] = jnp.zeros(halo.shape[1:], F32)
        ret[2] = jnp.zeros(ret.shape[1:], F32)

    loads["mask"].wait()
    loads["colf"].wait()
    win = dot(mask[...], colf[...]).astype(BF)
    loads["rowf"].wait()
    product = dot(rowf[...], win)

    def spectrum(i):
        base = 2 * row_freqs * i
        upper = product[base:base + row_freqs]
        lower = product[base + row_freqs:base + 2 * row_freqs]
        return (upper[:, :col_freqs] - lower[:, col_freqs:], upper[:, col_freqs:] + lower[:, :col_freqs])

    own_real, own_imag = spectrum(0)
    for i in range(2):
        psnd[i] = jnp.concatenate(spectrum(i + 1), axis=1).astype(BF)

    between = jnp.logical_and(has_left, has_right)

    @pl.when(between)
    def _():
        pl.semaphore_wait(barrier, 2)

    @pl.when(jnp.logical_not(between))
    def _():
        pl.semaphore_wait(barrier, 1)

    start(0)

    loads["ev"].wait()
    loads["sc"].wait()
    offset = ev[...] - t + 1
    member = jnp.where(lax.broadcasted_iota(jnp.int32, (8, frags), 0) == offset, 1.0, 0.0)
    upper = jnp.where(
        lax.broadcasted_iota(jnp.int32, (frags, frags), 0)
        <= lax.broadcasted_iota(jnp.int32, (frags, frags), 1), 1.0, 0.0).astype(BF)
    inclusive = dot(member.astype(BF), upper)
    rank = jnp.sum(member * (inclusive - 1.0), axis=0, keepdims=True)
    slot = offset.astype(F32) * float(cap) + rank
    slot_line = lax.broadcasted_iota(jnp.int32, (3 * cap, frags), 0).astype(F32)
    sel[...] = jnp.where(slot_line == slot, 1.0, 0.0).astype(BF)
    records = jnp.concatenate([sc[0], sc[1]], axis=0)
    packed = dot_nt(split3(records), sel[...])
    n_rec = 2 * SITES
    packed = packed[:n_rec] + packed[n_rec:2 * n_rec] + packed[2 * n_rec:]
    snd[0] = packed[:, :cap]
    recs[1] = packed[:, cap:2 * cap]
    snd[2] = packed[:, 2 * cap:]
    start(1)

    for k in ("ks", "redges", "rinv", "cinv", "rmid", "redge"):
        loads[k].wait()
    load_weights.wait()
    arrive(0)
    near = prec[0].astype(F32) + prec[1].astype(F32)
    real = own_real + near[:, :col_freqs]
    imag = own_imag + near[:, col_freqs:]

    half = cinv.shape[1] // 2
    pairs_n = kernels // 2
    ends = []
    for pair in range(pairs_n):
        blocks = []
        for k in (2 * pair, 2 * pair + 1):
            kr = ksv[0, k]
            ki = ksv[1, k]
            blocks.append(jnp.concatenate(
                [(kr * real - ki * imag).astype(BF), (kr * imag + ki * real).astype(BF)], axis=0))
        block = jnp.concatenate(blocks, axis=1)
        prod[pair] = block
        field = dot(rends[...], block).astype(BF)
        for i in range(2):
            part = field[:, i * col_freqs:(i + 1) * col_freqs]
            ends.append(jnp.concatenate([part[:2 * REACH], part[2 * REACH:]], axis=1))
    e = dot(jnp.concatenate(ends, axis=0), cinv[...])
    total = jnp.zeros((2 * REACH, half), F32)
    for k in range(kernels):
        er = e[2 * REACH * k:2 * REACH * (k + 1), :half]
        ei = e[2 * REACH * k:2 * REACH * (k + 1), half:]
        total = total + weights[k] * (er * er + ei * ei)
    rounded = total.astype(BF).astype(F32)
    hsnd[0] = rounded[:REACH]
    hsnd[1] = rounded[REACH:]
    start(2)

    total = jnp.zeros((rows, half), F32)
    for pair in range(pairs_n):
        field = dot(rinv[...], prod[pair]).astype(BF)
        for i in range(2):
            part = field[:, i * col_freqs:(i + 1) * col_freqs]
            e = dot(jnp.concatenate([part[:rows], part[rows:]], axis=1), cinv[...])
            er = e[:, :half]
            ei = e[:, half:]
            total = total + weights[2 * pair + i] * (er * er + ei * ei)

    rounded = total.astype(BF)
    inten[...] = rounded
    center = jnp.sum(total) * (1.0 / (rows * half))
    blurred = dot(rmid[...], inten[...])
    arrive(2)
    edge = jnp.concatenate([halo[0], halo[1]], axis=0).astype(BF)
    blurred = blurred + dot(redge[...], edge)
    dev = (blurred - center).astype(BF)
    tile_out[...] = dev
    center_out[...] = jnp.zeros(center_out.shape, F32) + center
    loads["ftab"].wait()
    loads["btab"].wait()
    freqs = 2 * col_freqs
    lacking = jnp.sum(ftab[freqs:].astype(F32), axis=1, keepdims=True) * center
    spectra = dot_nt(ftab[...], dev)
    that[:freqs] = spectra[:freqs].astype(BF)
    that[freqs:] = (spectra[freqs:] + lacking).astype(BF)
    arrive(1)

    span = cols // STEPS
    row_line = lax.broadcasted_iota(jnp.int32, (rows, cap), 0).astype(BF)
    step_line = lax.broadcasted_iota(jnp.int32, (btab.shape[1], cap), 0).astype(BF)
    end_line = lax.broadcasted_iota(jnp.int32, (2 * REACH, cap), 0).astype(F32)
    end_line = jnp.where(end_line < REACH, end_line, end_line + float(cols - 2 * REACH))

    def pick(index, period, function):
        found = jnp.full(index.shape, float(np.round(function(2.0 * math.pi * (STEPS - 1) * period / STEPS), 9)), F32)
        for i in range(STEPS - 1):
            found = jnp.where(index == i, float(np.round(function(2.0 * math.pi * i * period / STEPS), 9)), found)
        return found

    def ramp(line, low, part):
        zero = jnp.zeros((), BF)
        upper = jnp.where(line == (low + 1.0).astype(BF), part.astype(BF), zero)
        return jnp.where(line == low.astype(BF), (1.0 - part).astype(BF), upper)

    def evaluate(block):
        p = recs[block, :SITES, :] * float(rows - 1)
        q = recs[block, SITES:, :] * float(cols - 1)
        p0 = jnp.minimum(jnp.floor(p), float(rows - 2))
        q0 = jnp.minimum(jnp.floor(q), float(cols - 2))
        h = jnp.floor(q0 * (1.0 / span))
        low = q0 - h * float(span)
        turn = [(pick(h, j, math.cos), pick(h, j, math.sin)) for j in range(1, STEPS // 2)]
        sign = pick(h, STEPS // 2, math.cos)
        p1 = p - p0
        q1 = q - q0
        acc = jnp.zeros((8, cap), F32)
        for s in range(SITES):
            at = slice(s, s + 1)
            g = dot(that[...], ramp(row_line, p0[at], p1[at]))
            e = dot(btab[...], ramp(step_line, low[at], q1[at]))
            inner = [None] * (STEPS // 2 + 1)
            cross = [None] * (STEPS // 2 + 1)
            for i in range(col_freqs // 8):
                j = i * 8 * STEPS // col_freqs
                k = min(j, STEPS - j)
                gc, gs = g[8 * i:8 * i + 8], g[col_freqs + 8 * i:col_freqs + 8 * i + 8]
                ec, es = e[8 * i:8 * i + 8], e[col_freqs + 8 * i:col_freqs + 8 * i + 8]
                term = gc * ec + gs * es
                inner[k] = term if inner[k] is None else inner[k] + term
                if k in (0, STEPS // 2):
                    continue
                term = gs * ec - gc * es if j == k else gc * es - gs * ec
                cross[k] = term if cross[k] is None else cross[k] + term
            value = inner[0] + sign[at] * inner[STEPS // 2]
            for k in range(1, STEPS // 2):
                value = value + turn[k - 1][0][at] * inner[k] + turn[k - 1][1][at] * cross[k]
            ends = g[freqs:] * hat(end_line - q[at])
            acc = acc + (value + (ends[:REACH] + ends[REACH:]))
        mean = jnp.sum(acc, axis=0, keepdims=True) * (1.0 / SITES) + center * BLUR_SUM
        return jnp.broadcast_to(mean, (8, cap))

    rsnd[0] = evaluate(0)
    rsnd[2] = evaluate(2)
    start(3)
    ret[1] = evaluate(1)
    arrive(3)
    back = jnp.concatenate([ret[0], ret[1], ret[2]], axis=1)
    found = dot(split3(back), sel[...])
    mean = found[0:1] + found[8:9] + found[16:17]
    load_thresh.wait()
    loads["bias"].wait()
    bias_out[...] = 0.5 * bias[...].astype(F32) - 2.0 * (mean - thresh[0, 0]).reshape(frags)

    for kind in range(4):
        @pl.when(has_left)
        def _():
            pairs[kind][0].wait_send()

        @pl.when(has_right)
        def _():
            pairs[kind][1].wait_send()


def finish(tile, wide, sums, center, bias_h, resist_h, nb_h, out, sem):
    chunks = wide.shape[0]
    width = wide.shape[2]
    through = pltpu.make_async_copy(bias_h, nb_h, sem.at[3])
    stores = [pltpu.make_async_copy(out.at[i], resist_h.at[:, pl.ds(i * width, width)], sem.at[4 + chunks + i])
              for i in range(chunks)]
    through.start()
    for i in range(chunks):
        out[i] = dot(tile[...], wide[i]) + center[0:1, 0:1] * sums[0:1, i * width:(i + 1) * width]
        stores[i].start()
    for store in stores:
        store.wait()
    through.wait()


def shards(mask, kernel_spectra, kernel_weights, threshold, eval_tile, site_coords, bias_steps):
    rows, cols = mask.shape
    row_freqs, kernels, col_freqs = kernel_spectra.shape[1:]
    frags = eval_tile.shape[0]
    cap = frags // 2
    names = ("colf", "rowf", "rinv", "redges", "cinv", "rmid", "redge", "wide", "sums", "ftab", "btab")
    values = dict(zip(names, (jnp.asarray(x) for x in tables(rows, cols, row_freqs, col_freqs))))
    values["mask"] = mask
    values["ks"] = jnp.transpose(kernel_spectra, (0, 2, 1, 3))
    values["ev"] = eval_tile.reshape(1, frags)
    values["sc"] = site_coords
    values["bias"] = bias_steps
    ordered = [values[k] for k in LOADED]
    vmem = pl.BlockSpec(memory_space=pltpu.VMEM)
    hbm = pl.BlockSpec(memory_space=pltpu.HBM)
    anyw = pl.BlockSpec(memory_space=pl.ANY)
    coarse = cols // GRID_STEP
    tile, new_bias, center = pl.pallas_call(
        kernel,
        out_shape=(pltpu.VMEM((rows, coarse), BF), pltpu.VMEM((frags,), F32), pltpu.VMEM((8, 128), F32)),
        in_specs=[hbm] * (2 + len(ordered)),
        out_specs=(vmem, vmem, vmem),
        scratch_shapes=[pltpu.VMEM(x.shape, x.dtype) for x in ordered] + [
            pltpu.SMEM((kernels,), F32),
            pltpu.SMEM((1, 1), F32),
            pltpu.VMEM((2, row_freqs, 2 * col_freqs), BF),
            pltpu.VMEM((2, row_freqs, 2 * col_freqs), BF),
            pltpu.VMEM((kernels // 2, 2 * row_freqs, 2 * col_freqs), BF),
            pltpu.VMEM((3, 2 * SITES, cap), F32),
            pltpu.VMEM((3, 2 * SITES, cap), F32),
            pltpu.VMEM((rows, coarse), BF),
            pltpu.VMEM((2, REACH, coarse), F32),
            pltpu.VMEM((2, REACH, coarse), F32),
            pltpu.VMEM((3, 8, cap), F32),
            pltpu.VMEM((3, 8, cap), F32),
            pltpu.VMEM((3 * cap, frags), BF),
            pltpu.VMEM((2 * col_freqs + 2 * REACH, rows), BF),
            pltpu.SemaphoreType.DMA((len(ordered) + 2,)),
            pltpu.SemaphoreType.DMA((4, 2)),
            pltpu.SemaphoreType.DMA((4, 2)),
        ],
        compiler_params=pltpu.CompilerParams(
            collective_id=0, has_side_effects=True, vmem_limit_bytes=int(60 * 2 ** 20)),
    )(kernel_weights, threshold.reshape(1, 1), *ordered)
    width = cols // CHUNKS
    return pl.pallas_call(
        finish,
        out_shape=(jax.ShapeDtypeStruct((rows, cols), F32), jax.ShapeDtypeStruct((frags,), F32)),
        in_specs=[vmem] * 4 + [anyw],
        out_specs=(anyw, anyw),
        scratch_shapes=[
            pltpu.VMEM((CHUNKS, rows, width), F32),
            pltpu.SemaphoreType.DMA((4 + 2 * CHUNKS,)),
        ],
        compiler_params=pltpu.CompilerParams(vmem_limit_bytes=4 << 20),
    )(tile, values["wide"], values["sums"], center, new_bias)


def solution(mesh):
    placed = (
        P(("groups", "tx"), None),
        P(),
        P(),
        P(),
        P(("groups", "tx")),
        P(None, None, ("groups", "tx")),
        P(("groups", "tx")),
    )
    return jax.shard_map(
        shards,
        mesh=mesh,
        in_specs=placed,
        out_specs=(P(("groups", "tx"), None), P(("groups", "tx"))),
        check_vma=False,
    )
```

```python
import math

import jax
import jax.numpy as jnp
import ml_dtypes
import numpy as np
from jax import lax
from jax.experimental import pallas as pl
from jax.experimental.pallas import tpu as pltpu
from jax.sharding import PartitionSpec as P

HALO = 256
REACH = 8
SITES = 16
GRID_STEP = 4
STEPS = 8
SIGMA = 3.0
CHUNKS = 4
BF = jnp.bfloat16
F32 = jnp.float32
MESH = pl.DeviceIdType.MESH
LOADED = ("mask", "colf", "rowf", "ev", "sc", "ks", "redges", "rinv", "cinv", "rmid", "redge", "ftab", "btab", "bias")


def host_bf16(x):
    return np.asarray(x, np.float32).astype(ml_dtypes.bfloat16)


def twiddle(position, frequency, period, amplitude):
    index = (position[:, None] * frequency[None, :]) % period
    angle = index.astype(np.float64) * (2.0 * math.pi / period)
    return np.cos(angle) * amplitude, np.sin(angle) * amplitude


def gauss(offset):
    every = np.arange(-REACH, REACH + 1)
    norm = np.sum(np.exp(-every * every / (2.0 * SIGMA * SIGMA)))
    value = np.exp(-offset * offset / (2.0 * SIGMA * SIGMA)) / norm
    return np.where(np.abs(offset) <= REACH, value, 0.0)


def tables(rows, cols, row_freqs, col_freqs):
    window = rows + 2 * HALO
    f = np.arange(col_freqs) - col_freqs // 2
    g = np.arange(row_freqs) - row_freqs // 2
    c, s = twiddle(np.arange(cols), f, cols, 1.0 / math.sqrt(cols))
    col_forward = host_bf16(np.concatenate([c, -s], 1))
    c, s = twiddle(g, np.arange(window), window, 1.0 / math.sqrt(window))
    row_forward = host_bf16(np.concatenate([c, -s], 0))
    c, s = twiddle(np.arange(rows) + HALO, g, window, 1.0 / math.sqrt(row_freqs))
    row_inverse = host_bf16(np.block([[c, -s], [s, c]]))
    ends = np.r_[0:REACH, rows - REACH:rows]
    inverse_ends = np.ascontiguousarray(row_inverse[np.concatenate([ends, rows + ends])])
    row_forward = np.concatenate([
        row_forward[:, HALO:HALO + rows], row_forward[:, HALO + rows:], row_forward[:, :HALO]], 0)
    picked = np.arange(0, cols, GRID_STEP)
    c, s = twiddle(f, picked, cols, 1.0 / math.sqrt(col_freqs))
    col_inverse = host_bf16(np.block([[c, s], [-s, c]]))
    diff = np.arange(cols)[None, :] - picked[:, None]
    order = np.arange(1, col_freqs)
    base = np.arange(cols)
    kernel = 1.0 + 2.0 * np.cos(2 * math.pi * ((base[:, None] * order[None, :]) % cols) / cols).sum(1)
    kernel = (kernel + np.cos(2 * math.pi * ((base * col_freqs) % cols) / cols)) / picked.size
    interp = kernel[diff % cols]
    lines = np.arange(cols)
    col_blur = host_bf16(gauss((lines[None, :] - lines[:, None]).astype(np.float64)))
    spread = interp @ col_blur.astype(np.float64)
    high = host_bf16(spread)
    wide = np.ascontiguousarray(high.reshape(picked.size, CHUNKS, cols // CHUNKS).transpose(1, 0, 2))
    sums = spread.sum(0).astype(np.float32)[None]
    row_diff = np.arange(rows + 2 * REACH)[None, :] - REACH - np.arange(rows)[:, None]
    row_blur = host_bf16(gauss(row_diff.astype(np.float64)))
    row_mid = np.ascontiguousarray(row_blur[:, REACH:REACH + rows])
    row_edge = np.concatenate([row_blur[:, :REACH], row_blur[:, REACH + rows:]], 1)
    return (col_forward, row_forward, row_inverse, inverse_ends, col_inverse, row_mid, row_edge, wide,
            sums) + site_tables(cols, col_freqs, interp, spread)


def site_tables(cols, col_freqs, interp, spread):
    coarse = cols // GRID_STEP
    span = cols // STEPS
    line = np.arange(cols)
    reach = np.arange(-REACH, REACH + 1)
    weight = host_bf16(gauss(reach.astype(np.float64))).astype(np.float64)
    periodic = np.zeros((cols, cols))
    for d, w in zip(reach, weight):
        periodic[(line - d) % cols, line] += w
    order = np.concatenate([np.arange(j, col_freqs, STEPS) for j in range(STEPS)])
    angle = 2.0 * math.pi * ((np.arange(col_freqs + 1)[:, None] * reach[None, :]) % cols) / cols
    response = (weight[None, :] * np.cos(angle)).sum(1)
    scale = (np.where(order == 0, 1.0, 2.0) * response[order] / coarse)[:, None]
    angle = 2.0 * math.pi * ((order[:, None] * GRID_STEP * np.arange(coarse)[None, :]) % cols) / cols
    cosine, sine = scale * np.cos(angle), scale * np.sin(angle)
    sine[0] = response[col_freqs] / coarse * np.cos(math.pi * np.arange(coarse))
    ends = np.r_[0:REACH, cols - REACH:cols]
    lacking = (spread - interp @ periodic)[:, ends].T
    steps = np.arange(-(-(span + 1) // 16) * 16)
    angle = 2.0 * math.pi * ((order[:, None] * steps[None, :]) % cols) / cols
    base_cos, base_sin = np.cos(angle), np.sin(angle)
    base_sin[0] = np.cos(2.0 * math.pi * ((col_freqs * steps) % cols) / cols)
    return (host_bf16(np.concatenate([cosine, sine, lacking], 0)), host_bf16(np.concatenate([base_cos, base_sin], 0)))


BLUR_SUM = float(host_bf16(gauss(np.arange(-REACH, REACH + 1.0))).astype(np.float64).sum())


def dot(a, b):
    return jnp.dot(a, b, preferred_element_type=F32)


def dot_nt(a, b):
    return lax.dot_general(a, b, (((1,), (1,)), ((), ())), preferred_element_type=F32)


def split3(x):
    high = x.astype(BF)
    rest = x - high.astype(F32)
    mid = rest.astype(BF)
    low = (rest - mid.astype(F32)).astype(BF)
    return jnp.concatenate([high, mid, low], axis=0)


def hat(distance):
    return jnp.maximum(1.0 - jnp.abs(distance), 0.0)


def kernel(weights_h, thresh_h, *refs):
    n = len(LOADED)
    sources = dict(zip(LOADED, refs[:n]))
    tile_out, bias_out, center_out = refs[n:n + 3]
    held = dict(zip(LOADED, refs[n + 3:2 * n + 3]))
    (weights, thresh, psnd, prec, prod, snd, recs, inten, hsnd, halo, rsnd, ret, sel, that,
     local_sem, send_sem, recv_sem) = refs[2 * n + 3:]
    mask, colf, rowf, ev, sc, ksv, rends, rinv, cinv, rmid, redge, ftab, btab, bias = (held[k] for k in LOADED)
    t = lax.axis_index("tx")
    count = lax.axis_size("tx")
    has_left = t > 0
    has_right = t < count - 1
    rows, cols = mask.shape
    coarse = cols // GRID_STEP
    kernels, row_freqs, col_freqs = ksv.shape[1:]
    frags = ev.shape[1]
    cap = frags // 2

    barrier = pltpu.get_barrier_semaphore()

    @pl.when(has_left)
    def _():
        pl.semaphore_signal(barrier, inc=1, device_id={"tx": t - 1}, device_id_type=MESH)

    @pl.when(has_right)
    def _():
        pl.semaphore_signal(barrier, inc=1, device_id={"tx": t + 1}, device_id_type=MESH)

    loads = {k: pltpu.make_async_copy(sources[k], held[k], local_sem.at[i])
             for i, k in enumerate(LOADED)}
    for k in LOADED:
        loads[k].start()
    load_weights = pltpu.make_async_copy(weights_h, weights, local_sem.at[n])
    load_weights.start()
    load_thresh = pltpu.make_async_copy(thresh_h, thresh, local_sem.at[n + 1])
    load_thresh.start()

    def to_left(kind, src, dst):
        return pltpu.make_async_remote_copy(
            src_ref=src, dst_ref=dst, send_sem=send_sem.at[kind, 0], recv_sem=recv_sem.at[kind, 0],
            device_id={"tx": t - 1}, device_id_type=MESH)

    def to_right(kind, src, dst):
        return pltpu.make_async_remote_copy(
            src_ref=src, dst_ref=dst, send_sem=send_sem.at[kind, 1], recv_sem=recv_sem.at[kind, 1],
            device_id={"tx": t + 1}, device_id_type=MESH)

    pairs = (
        (to_left(0, psnd.at[0], prec.at[1]), to_right(0, psnd.at[1], prec.at[0])),
        (to_left(1, snd.at[0], recs.at[2]), to_right(1, snd.at[2], recs.at[0])),
        (to_left(2, hsnd.at[0], halo.at[1]), to_right(2, hsnd.at[1], halo.at[0])),
        (to_left(3, rsnd.at[0], ret.at[2]), to_right(3, rsnd.at[2], ret.at[0])),
    )

    def start(kind):
        @pl.when(has_left)
        def _():
            pairs[kind][0].start()

        @pl.when(has_right)
        def _():
            pairs[kind][1].start()

    def arrive(kind):
        @pl.when(has_right)
        def _():
            pairs[kind][0].wait_recv()

        @pl.when(has_left)
        def _():
            pairs[kind][1].wait_recv()

    @pl.when(jnp.logical_not(has_left))
    def _():
        prec[0] = jnp.zeros(prec.shape[1:], BF)
        recs[0] = jnp.zeros(recs.shape[1:], F32)
        halo[0] = jnp.zeros(halo.shape[1:], F32)
        ret[0] = jnp.zeros(ret.shape[1:], F32)

    @pl.when(jnp.logical_not(has_right))
    def _():
        prec[1] = jnp.zeros(prec.shape[1:], BF)
        recs[2] = jnp.zeros(recs.shape[1:], F32)
        halo[1] = jnp.zeros(halo.shape[1:], F32)
        ret[2] = jnp.zeros(ret.shape[1:], F32)

    loads["mask"].wait()
    loads["colf"].wait()
    win = dot(mask[...], colf[...]).astype(BF)
    loads["rowf"].wait()
    product = dot(rowf[...], win)

    def spectrum(i):
        base = 2 * row_freqs * i
        upper = product[base:base + row_freqs]
        lower = product[base + row_freqs:base + 2 * row_freqs]
        return (upper[:, :col_freqs] - lower[:, col_freqs:], upper[:, col_freqs:] + lower[:, :col_freqs])

    own_real, own_imag = spectrum(0)
    for i in range(2):
        psnd[i] = jnp.concatenate(spectrum(i + 1), axis=1).astype(BF)

    between = jnp.logical_and(has_left, has_right)

    @pl.when(between)
    def _():
        pl.semaphore_wait(barrier, 2)

    @pl.when(jnp.logical_not(between))
    def _():
        pl.semaphore_wait(barrier, 1)

    start(0)

    loads["ev"].wait()
    loads["sc"].wait()
    offset = ev[...] - t + 1
    member = jnp.where(lax.broadcasted_iota(jnp.int32, (8, frags), 0) == offset, 1.0, 0.0)
    upper = jnp.where(
        lax.broadcasted_iota(jnp.int32, (frags, frags), 0)
        <= lax.broadcasted_iota(jnp.int32, (frags, frags), 1), 1.0, 0.0).astype(BF)
    inclusive = dot(member.astype(BF), upper)
    rank = jnp.sum(member * (inclusive - 1.0), axis=0, keepdims=True)
    slot = offset.astype(F32) * float(cap) + rank
    slot_line = lax.broadcasted_iota(jnp.int32, (3 * cap, frags), 0).astype(F32)
    sel[...] = jnp.where(slot_line == slot, 1.0, 0.0).astype(BF)
    records = jnp.concatenate([sc[0], sc[1]], axis=0)
    packed = dot_nt(split3(records), sel[...])
    n_rec = 2 * SITES
    packed = packed[:n_rec] + packed[n_rec:2 * n_rec] + packed[2 * n_rec:]
    snd[0] = packed[:, :cap]
    recs[1] = packed[:, cap:2 * cap]
    snd[2] = packed[:, 2 * cap:]
    start(1)

    for k in ("ks", "redges", "rinv", "cinv", "rmid", "redge"):
        loads[k].wait()
    load_weights.wait()
    arrive(0)
    near = prec[0].astype(F32) + prec[1].astype(F32)
    real = own_real + near[:, :col_freqs]
    imag = own_imag + near[:, col_freqs:]

    half = cinv.shape[1] // 2
    pairs_n = kernels // 2
    ends = []
    for pair in range(pairs_n):
        blocks = []
        for k in (2 * pair, 2 * pair + 1):
            kr = ksv[0, k]
            ki = ksv[1, k]
            blocks.append(jnp.concatenate(
                [(kr * real - ki * imag).astype(BF), (kr * imag + ki * real).astype(BF)], axis=0))
        block = jnp.concatenate(blocks, axis=1)
        prod[pair] = block
        field = dot(rends[...], block).astype(BF)
        for i in range(2):
            part = field[:, i * col_freqs:(i + 1) * col_freqs]
            ends.append(jnp.concatenate([part[:2 * REACH], part[2 * REACH:]], axis=1))
    e = dot(jnp.concatenate(ends, axis=0), cinv[...])
    total = jnp.zeros((2 * REACH, half), F32)
    for k in range(kernels):
        er = e[2 * REACH * k:2 * REACH * (k + 1), :half]
        ei = e[2 * REACH * k:2 * REACH * (k + 1), half:]
        total = total + weights[k] * (er * er + ei * ei)
    rounded = total.astype(BF).astype(F32)
    hsnd[0] = rounded[:REACH]
    hsnd[1] = rounded[REACH:]
    start(2)

    total = jnp.zeros((rows, half), F32)
    for pair in range(pairs_n):
        field = dot(rinv[...], prod[pair]).astype(BF)
        for i in range(2):
            part = field[:, i * col_freqs:(i + 1) * col_freqs]
            e = dot(jnp.concatenate([part[:rows], part[rows:]], axis=1), cinv[...])
            er = e[:, :half]
            ei = e[:, half:]
            total = total + weights[2 * pair + i] * (er * er + ei * ei)

    rounded = total.astype(BF)
    inten[...] = rounded
    center = jnp.sum(total) * (1.0 / (rows * half))
    blurred = dot(rmid[...], inten[...])
    arrive(2)
    edge = jnp.concatenate([halo[0], halo[1]], axis=0).astype(BF)
    blurred = blurred + dot(redge[...], edge)
    dev = (blurred - center).astype(BF)
    tile_out[...] = dev
    center_out[...] = jnp.zeros(center_out.shape, F32) + center
    loads["ftab"].wait()
    loads["btab"].wait()
    freqs = 2 * col_freqs
    lacking = jnp.sum(ftab[freqs:].astype(F32), axis=1, keepdims=True) * center
    spectra = dot_nt(ftab[...], dev)
    that[:freqs] = spectra[:freqs].astype(BF)
    that[freqs:] = (spectra[freqs:] + lacking).astype(BF)
    arrive(1)

    span = cols // STEPS
    row_line = lax.broadcasted_iota(jnp.int32, (rows, cap), 0).astype(BF)
    step_line = lax.broadcasted_iota(jnp.int32, (btab.shape[1], cap), 0).astype(BF)
    end_line = lax.broadcasted_iota(jnp.int32, (2 * REACH, cap), 0).astype(F32)
    end_line = jnp.where(end_line < REACH, end_line, end_line + float(cols - 2 * REACH))

    def pick(index, period, function):
        found = jnp.full(index.shape, float(np.round(function(2.0 * math.pi * (STEPS - 1) * period / STEPS), 9)), F32)
        for i in range(STEPS - 1):
            found = jnp.where(index == i, float(np.round(function(2.0 * math.pi * i * period / STEPS), 9)), found)
        return found

    def ramp(line, low, part):
        zero = jnp.zeros((), BF)
        upper = jnp.where(line == (low + 1.0).astype(BF), part.astype(BF), zero)
        return jnp.where(line == low.astype(BF), (1.0 - part).astype(BF), upper)

    def evaluate(block):
        p = recs[block, :SITES, :] * float(rows - 1)
        q = recs[block, SITES:, :] * float(cols - 1)
        p0 = jnp.minimum(jnp.floor(p), float(rows - 2))
        q0 = jnp.minimum(jnp.floor(q), float(cols - 2))
        h = jnp.floor(q0 * (1.0 / span))
        low = q0 - h * float(span)
        turn = [(pick(h, j, math.cos), pick(h, j, math.sin)) for j in range(1, STEPS // 2)]
        sign = pick(h, STEPS // 2, math.cos)
        p1 = p - p0
        q1 = q - q0
        acc = jnp.zeros((8, cap), F32)
        for s in range(SITES):
            at = slice(s, s + 1)
            g = dot(that[...], ramp(row_line, p0[at], p1[at]))
            e = dot(btab[...], ramp(step_line, low[at], q1[at]))
            inner = [None] * (STEPS // 2 + 1)
            cross = [None] * (STEPS // 2 + 1)
            for i in range(col_freqs // 8):
                j = i * 8 * STEPS // col_freqs
                k = min(j, STEPS - j)
                gc, gs = g[8 * i:8 * i + 8], g[col_freqs + 8 * i:col_freqs + 8 * i + 8]
                ec, es = e[8 * i:8 * i + 8], e[col_freqs + 8 * i:col_freqs + 8 * i + 8]
                term = gc * ec + gs * es
                inner[k] = term if inner[k] is None else inner[k] + term
                if k in (0, STEPS // 2):
                    continue
                term = gs * ec - gc * es if j == k else gc * es - gs * ec
                cross[k] = term if cross[k] is None else cross[k] + term
            value = inner[0] + sign[at] * inner[STEPS // 2]
            for k in range(1, STEPS // 2):
                value = value + turn[k - 1][0][at] * inner[k] + turn[k - 1][1][at] * cross[k]
            ends = g[freqs:] * hat(end_line - q[at])
            acc = acc + (value + (ends[:REACH] + ends[REACH:]))
        mean = jnp.sum(acc, axis=0, keepdims=True) * (1.0 / SITES) + center * BLUR_SUM
        return jnp.broadcast_to(mean, (8, cap))

    even = t % 2 == 0
    first = jnp.where(even, 0, 2)
    rsnd[first] = evaluate(first)

    @pl.when(jnp.logical_and(even, has_left))
    def _():
        pairs[3][0].start()

    @pl.when(jnp.logical_and(jnp.logical_not(even), has_right))
    def _():
        pairs[3][1].start()

    second = 2 - first
    rsnd[second] = evaluate(second)

    @pl.when(jnp.logical_and(even, has_right))
    def _():
        pairs[3][1].start()

    @pl.when(jnp.logical_and(jnp.logical_not(even), has_left))
    def _():
        pairs[3][0].start()

    ret[1] = evaluate(1)
    arrive(3)
    back = jnp.concatenate([ret[0], ret[1], ret[2]], axis=1)
    found = dot(split3(back), sel[...])
    mean = found[0:1] + found[8:9] + found[16:17]
    load_thresh.wait()
    loads["bias"].wait()
    bias_out[...] = 0.5 * bias[...].astype(F32) - 2.0 * (mean - thresh[0, 0]).reshape(frags)

    for kind in range(4):
        @pl.when(has_left)
        def _():
            pairs[kind][0].wait_send()

        @pl.when(has_right)
        def _():
            pairs[kind][1].wait_send()


def finish(tile, wide, sums, center, bias_h, resist_h, nb_h, out, sem):
    chunks = wide.shape[0]
    width = wide.shape[2]
    through = pltpu.make_async_copy(bias_h, nb_h, sem.at[3])
    stores = [pltpu.make_async_copy(out.at[i], resist_h.at[:, pl.ds(i * width, width)], sem.at[4 + chunks + i])
              for i in range(chunks)]
    through.start()
    for i in range(chunks):
        out[i] = dot(tile[...], wide[i]) + center[0:1, 0:1] * sums[0:1, i * width:(i + 1) * width]
        stores[i].start()
    for store in stores:
        store.wait()
    through.wait()


def shards(mask, kernel_spectra, kernel_weights, threshold, eval_tile, site_coords, bias_steps):
    rows, cols = mask.shape
    row_freqs, kernels, col_freqs = kernel_spectra.shape[1:]
    frags = eval_tile.shape[0]
    cap = frags // 2
    names = ("colf", "rowf", "rinv", "redges", "cinv", "rmid", "redge", "wide", "sums", "ftab", "btab")
    values = dict(zip(names, (jnp.asarray(x) for x in tables(rows, cols, row_freqs, col_freqs))))
    values["mask"] = mask
    values["ks"] = jnp.transpose(kernel_spectra, (0, 2, 1, 3))
    values["ev"] = eval_tile.reshape(1, frags)
    values["sc"] = site_coords
    values["bias"] = bias_steps
    ordered = [values[k] for k in LOADED]
    vmem = pl.BlockSpec(memory_space=pltpu.VMEM)
    hbm = pl.BlockSpec(memory_space=pltpu.HBM)
    anyw = pl.BlockSpec(memory_space=pl.ANY)
    coarse = cols // GRID_STEP
    tile, new_bias, center = pl.pallas_call(
        kernel,
        out_shape=(pltpu.VMEM((rows, coarse), BF), pltpu.VMEM((frags,), F32), pltpu.VMEM((8, 128), F32)),
        in_specs=[hbm] * (2 + len(ordered)),
        out_specs=(vmem, vmem, vmem),
        scratch_shapes=[pltpu.VMEM(x.shape, x.dtype) for x in ordered] + [
            pltpu.SMEM((kernels,), F32),
            pltpu.SMEM((1, 1), F32),
            pltpu.VMEM((2, row_freqs, 2 * col_freqs), BF),
            pltpu.VMEM((2, row_freqs, 2 * col_freqs), BF),
            pltpu.VMEM((kernels // 2, 2 * row_freqs, 2 * col_freqs), BF),
            pltpu.VMEM((3, 2 * SITES, cap), F32),
            pltpu.VMEM((3, 2 * SITES, cap), F32),
            pltpu.VMEM((rows, coarse), BF),
            pltpu.VMEM((2, REACH, coarse), F32),
            pltpu.VMEM((2, REACH, coarse), F32),
            pltpu.VMEM((3, 8, cap), F32),
            pltpu.VMEM((3, 8, cap), F32),
            pltpu.VMEM((3 * cap, frags), BF),
            pltpu.VMEM((2 * col_freqs + 2 * REACH, rows), BF),
            pltpu.SemaphoreType.DMA((len(ordered) + 2,)),
            pltpu.SemaphoreType.DMA((4, 2)),
            pltpu.SemaphoreType.DMA((4, 2)),
        ],
        compiler_params=pltpu.CompilerParams(
            collective_id=0, has_side_effects=True, vmem_limit_bytes=int(60 * 2 ** 20)),
    )(kernel_weights, threshold.reshape(1, 1), *ordered)
    width = cols // CHUNKS
    return pl.pallas_call(
        finish,
        out_shape=(jax.ShapeDtypeStruct((rows, cols), F32), jax.ShapeDtypeStruct((frags,), F32)),
        in_specs=[vmem] * 4 + [anyw],
        out_specs=(anyw, anyw),
        scratch_shapes=[
            pltpu.VMEM((CHUNKS, rows, width), F32),
            pltpu.SemaphoreType.DMA((4 + 2 * CHUNKS,)),
        ],
        compiler_params=pltpu.CompilerParams(vmem_limit_bytes=4 << 20),
    )(tile, values["wide"], values["sums"], center, new_bias)


def solution(mesh):
    placed = (
        P(("groups", "tx"), None),
        P(),
        P(),
        P(),
        P(("groups", "tx")),
        P(None, None, ("groups", "tx")),
        P(("groups", "tx")),
    )
    return jax.shard_map(
        shards,
        mesh=mesh,
        in_specs=placed,
        out_specs=(P(("groups", "tx"), None), P(("groups", "tx"))),
        check_vma=False,
    )
```

```python
import math

import jax
import jax.numpy as jnp
import ml_dtypes
import numpy as np
from jax import lax
from jax.experimental import pallas as pl
from jax.experimental.pallas import tpu as pltpu
from jax.sharding import PartitionSpec as P

HALO = 256
REACH = 8
EARLY = 5
SITES = 16
GRID_STEP = 4
STEPS = 8
SIGMA = 3.0
CHUNKS = 4
STRIP = 32
PREPARED = 1
BF = jnp.bfloat16
F32 = jnp.float32
MESH = pl.DeviceIdType.MESH
LOADED = ("mask", "colf", "rowf", "ev", "sc", "ks", "redges", "rinv", "cinv", "rmid", "redge", "ftab", "btab", "bias")


def host_bf16(x):
    return np.asarray(x, np.float32).astype(ml_dtypes.bfloat16)


def twiddle(position, frequency, period, amplitude):
    index = (position[:, None] * frequency[None, :]) % period
    angle = index.astype(np.float64) * (2.0 * math.pi / period)
    return np.cos(angle) * amplitude, np.sin(angle) * amplitude


def gauss(offset):
    every = np.arange(-REACH, REACH + 1)
    norm = np.sum(np.exp(-every * every / (2.0 * SIGMA * SIGMA)))
    value = np.exp(-offset * offset / (2.0 * SIGMA * SIGMA)) / norm
    return np.where(np.abs(offset) <= REACH, value, 0.0)


def tables(rows, cols, row_freqs, col_freqs):
    window = rows + 2 * HALO
    f = np.arange(col_freqs) - col_freqs // 2
    g = np.arange(row_freqs) - row_freqs // 2
    c, s = twiddle(np.arange(cols), f, cols, 1.0 / math.sqrt(cols))
    col_forward = host_bf16(np.concatenate([c, -s], 1))
    c, s = twiddle(g, np.arange(window), window, 1.0 / math.sqrt(window))
    row_forward = host_bf16(np.concatenate([c, -s], 0))
    c, s = twiddle(np.arange(rows) + HALO, g, window, 1.0 / math.sqrt(row_freqs))
    row_inverse = host_bf16(np.block([[c, -s], [s, c]]))
    ends = np.r_[0:REACH, rows - REACH:rows]
    inverse_ends = np.ascontiguousarray(row_inverse[np.concatenate([ends, rows + ends])])
    row_forward = np.concatenate([
        row_forward[:, HALO + rows:], row_forward[:, :HALO], row_forward[:, HALO:HALO + rows]], 0)
    picked = np.arange(0, cols, GRID_STEP)
    c, s = twiddle(f, picked, cols, 1.0 / math.sqrt(col_freqs))
    col_inverse = host_bf16(np.block([[c, s], [-s, c]]))
    diff = np.arange(cols)[None, :] - picked[:, None]
    order = np.arange(1, col_freqs)
    base = np.arange(cols)
    kernel = 1.0 + 2.0 * np.cos(2 * math.pi * ((base[:, None] * order[None, :]) % cols) / cols).sum(1)
    kernel = (kernel + np.cos(2 * math.pi * ((base * col_freqs) % cols) / cols)) / picked.size
    interp = kernel[diff % cols]
    lines = np.arange(cols)
    col_blur = host_bf16(gauss((lines[None, :] - lines[:, None]).astype(np.float64)))
    spread = interp @ col_blur.astype(np.float64)
    high = host_bf16(spread)
    wide = np.ascontiguousarray(high.reshape(picked.size, CHUNKS, cols // CHUNKS).transpose(1, 0, 2))
    sums = spread.sum(0).astype(np.float32)[None]
    row_diff = np.arange(rows + 2 * REACH)[None, :] - REACH - np.arange(rows)[:, None]
    row_blur = host_bf16(gauss(row_diff.astype(np.float64)))
    row_mid = np.ascontiguousarray(row_blur[:, REACH:REACH + rows])
    row_edge = np.concatenate([row_blur[:, :REACH], row_blur[:, REACH + rows:]], 1)
    row_edge = np.concatenate([row_edge[:2 * REACH], row_edge[rows - 2 * REACH:]], 0)
    return (col_forward, row_forward, row_inverse, inverse_ends, col_inverse, row_mid, row_edge, wide,
            sums) + site_tables(cols, col_freqs, interp, spread)


def site_tables(cols, col_freqs, interp, spread):
    coarse = cols // GRID_STEP
    span = cols // STEPS
    line = np.arange(cols)
    reach = np.arange(-REACH, REACH + 1)
    weight = host_bf16(gauss(reach.astype(np.float64))).astype(np.float64)
    periodic = np.zeros((cols, cols))
    for d, w in zip(reach, weight):
        periodic[(line - d) % cols, line] += w
    order = np.concatenate([np.arange(j, col_freqs, STEPS) for j in range(STEPS)])
    angle = 2.0 * math.pi * ((np.arange(col_freqs + 1)[:, None] * reach[None, :]) % cols) / cols
    response = (weight[None, :] * np.cos(angle)).sum(1)
    scale = (np.where(order == 0, 1.0, 2.0) * response[order] / coarse)[:, None]
    angle = 2.0 * math.pi * ((order[:, None] * GRID_STEP * np.arange(coarse)[None, :]) % cols) / cols
    cosine, sine = scale * np.cos(angle), scale * np.sin(angle)
    sine[0] = response[col_freqs] / coarse * np.cos(math.pi * np.arange(coarse))
    ends = np.r_[0:REACH, cols - REACH:cols]
    lacking = (spread - interp @ periodic)[:, ends].T
    steps = np.arange(-(-(span + 1) // 16) * 16)
    angle = 2.0 * math.pi * ((order[:, None] * steps[None, :]) % cols) / cols
    base_cos, base_sin = np.cos(angle), np.sin(angle)
    base_sin[0] = np.cos(2.0 * math.pi * ((col_freqs * steps) % cols) / cols)
    return (host_bf16(np.concatenate([cosine, sine, lacking], 0)), host_bf16(np.concatenate([base_cos, base_sin], 0)))


BLUR_SUM = float(host_bf16(gauss(np.arange(-REACH, REACH + 1.0))).astype(np.float64).sum())


def dot(a, b):
    return jnp.dot(a, b, preferred_element_type=F32)


def dot_nt(a, b):
    return lax.dot_general(a, b, (((1,), (1,)), ((), ())), preferred_element_type=F32)


def split3(x):
    high = x.astype(BF)
    rest = x - high.astype(F32)
    mid = rest.astype(BF)
    low = (rest - mid.astype(F32)).astype(BF)
    return jnp.concatenate([high, mid, low], axis=0)


def hat(distance):
    return jnp.maximum(1.0 - jnp.abs(distance), 0.0)


def kernel(weights_h, thresh_h, *refs):
    n = len(LOADED)
    sources = dict(zip(LOADED, refs[:n]))
    tile_out, bias_out, center_out = refs[n:n + 3]
    held = dict(zip(LOADED, refs[n + 3:2 * n + 3]))
    (weights, thresh, psnd, prec, prod, fields, snd, recs, inten, hsnd, halo, rsnd, ret, sel, that, row_part, col_part,
     local_sem, send_sem, recv_sem) = refs[2 * n + 3:]
    mask, colf, rowf, ev, sc, ksv, rends, rinv, cinv, rmid, redge, ftab, btab, bias = (held[k] for k in LOADED)
    t = lax.axis_index("tx")
    count = lax.axis_size("tx")
    has_left = t > 0
    has_right = t < count - 1
    rows, cols = mask.shape
    coarse = cols // GRID_STEP
    kernels, row_freqs, col_freqs = ksv.shape[1:]
    frags = ev.shape[1]
    cap = frags // 2

    barrier = pltpu.get_barrier_semaphore()

    @pl.when(has_left)
    def _():
        pl.semaphore_signal(barrier, inc=1, device_id={"tx": t - 1}, device_id_type=MESH)

    @pl.when(has_right)
    def _():
        pl.semaphore_signal(barrier, inc=1, device_id={"tx": t + 1}, device_id_type=MESH)

    loads = {k: pltpu.make_async_copy(sources[k], held[k], local_sem.at[i])
             for i, k in enumerate(LOADED)}
    for k in LOADED[:EARLY]:
        loads[k].start()
    load_weights = pltpu.make_async_copy(weights_h, weights, local_sem.at[n])
    load_thresh = pltpu.make_async_copy(thresh_h, thresh, local_sem.at[n + 1])

    def to_left(kind, src, dst):
        return pltpu.make_async_remote_copy(
            src_ref=src, dst_ref=dst, send_sem=send_sem.at[kind, 0], recv_sem=recv_sem.at[kind, 0],
            device_id={"tx": t - 1}, device_id_type=MESH)

    def to_right(kind, src, dst):
        return pltpu.make_async_remote_copy(
            src_ref=src, dst_ref=dst, send_sem=send_sem.at[kind, 1], recv_sem=recv_sem.at[kind, 1],
            device_id={"tx": t + 1}, device_id_type=MESH)

    pairs = (
        (to_left(0, psnd.at[0], prec.at[1]), to_right(0, psnd.at[1], prec.at[0])),
        (to_left(1, snd.at[0], recs.at[2]), to_right(1, snd.at[2], recs.at[0])),
        (to_left(2, hsnd.at[0], halo.at[1]), to_right(2, hsnd.at[1], halo.at[0])),
        (to_left(3, rsnd.at[0], ret.at[2]), to_right(3, rsnd.at[2], ret.at[0])),
    )

    even = t % 2 == 0
    odd = jnp.logical_not(even)

    def start_far(kind):
        @pl.when(jnp.logical_and(even, has_left))
        def _():
            pairs[kind][0].start()

        @pl.when(jnp.logical_and(odd, has_right))
        def _():
            pairs[kind][1].start()

    def start_near(kind):
        @pl.when(jnp.logical_and(even, has_right))
        def _():
            pairs[kind][1].start()

        @pl.when(jnp.logical_and(odd, has_left))
        def _():
            pairs[kind][0].start()

    def start(kind):
        start_far(kind)
        start_near(kind)

    def arrive(kind):
        @pl.when(has_right)
        def _():
            pairs[kind][0].wait_recv()

        @pl.when(has_left)
        def _():
            pairs[kind][1].wait_recv()

    @pl.when(jnp.logical_not(has_left))
    def _():
        prec[0] = jnp.zeros(prec.shape[1:], BF)
        recs[0] = jnp.zeros(recs.shape[1:], F32)
        halo[0] = jnp.zeros(halo.shape[1:], F32)
        ret[0] = jnp.zeros(ret.shape[1:], F32)

    @pl.when(jnp.logical_not(has_right))
    def _():
        prec[1] = jnp.zeros(prec.shape[1:], BF)
        recs[2] = jnp.zeros(recs.shape[1:], F32)
        halo[1] = jnp.zeros(halo.shape[1:], F32)
        ret[2] = jnp.zeros(ret.shape[1:], F32)

    loads["mask"].wait()
    loads["colf"].wait()
    for k in LOADED[EARLY:]:
        loads[k].start()
    load_weights.start()
    load_thresh.start()
    win = dot(mask[...], colf[...]).astype(BF)
    loads["rowf"].wait()

    def spectrum(i):
        product = dot(rowf[2 * row_freqs * i:2 * row_freqs * (i + 1)], win)
        upper = product[:row_freqs]
        lower = product[row_freqs:]
        return (upper[:, :col_freqs] - lower[:, col_freqs:], upper[:, col_freqs:] + lower[:, :col_freqs])

    for i in range(2):
        psnd[i] = jnp.concatenate(spectrum(i), axis=1).astype(BF)

    between = jnp.logical_and(has_left, has_right)

    @pl.when(between)
    def _():
        pl.semaphore_wait(barrier, 2)

    @pl.when(jnp.logical_not(between))
    def _():
        pl.semaphore_wait(barrier, 1)

    start(0)
    own_real, own_imag = spectrum(2)

    loads["ev"].wait()
    loads["sc"].wait()
    offset = ev[...] - t + 1
    member = jnp.where(lax.broadcasted_iota(jnp.int32, (8, frags), 0) == offset, 1.0, 0.0)
    upper = jnp.where(
        lax.broadcasted_iota(jnp.int32, (frags, frags), 0)
        <= lax.broadcasted_iota(jnp.int32, (frags, frags), 1), 1.0, 0.0).astype(BF)
    inclusive = dot(member.astype(BF), upper)
    rank = jnp.sum(member * (inclusive - 1.0), axis=0, keepdims=True)
    slot = offset.astype(F32) * float(cap) + rank
    slot_line = lax.broadcasted_iota(jnp.int32, (3 * cap, frags), 0).astype(F32)
    sel[...] = jnp.where(slot_line == slot, 1.0, 0.0).astype(BF)
    records = jnp.concatenate([sc[0], sc[1]], axis=0)
    packed = dot_nt(split3(records), sel[...])
    n_rec = 2 * SITES
    packed = packed[:n_rec] + packed[n_rec:2 * n_rec] + packed[2 * n_rec:]
    snd[0] = packed[:, :cap]
    recs[1] = packed[:, cap:2 * cap]
    snd[2] = packed[:, 2 * cap:]
    start(1)

    for k in ("ks", "redges", "rinv", "cinv", "rmid", "redge"):
        loads[k].wait()
    load_weights.wait()
    arrive(0)
    near = prec[0].astype(F32) + prec[1].astype(F32)
    real = own_real + near[:, :col_freqs]
    imag = own_imag + near[:, col_freqs:]

    half = cinv.shape[1] // 2
    pairs_n = kernels // 2
    ends = []
    for pair in range(pairs_n):
        blocks = []
        for k in (2 * pair, 2 * pair + 1):
            kr = ksv[0, k]
            ki = ksv[1, k]
            blocks.append(jnp.concatenate(
                [(kr * real - ki * imag).astype(BF), (kr * imag + ki * real).astype(BF)], axis=0))
        block = jnp.concatenate(blocks, axis=1)
        prod[pair] = block
        field = dot(rends[...], block).astype(BF)
        for i in range(2):
            part = field[:, i * col_freqs:(i + 1) * col_freqs]
            ends.append(jnp.concatenate([part[:2 * REACH], part[2 * REACH:]], axis=1))
    e = dot(jnp.concatenate(ends, axis=0), cinv[...])
    total = jnp.zeros((2 * REACH, half), F32)
    for k in range(kernels):
        er = e[2 * REACH * k:2 * REACH * (k + 1), :half]
        ei = e[2 * REACH * k:2 * REACH * (k + 1), half:]
        total = total + weights[k] * (er * er + ei * ei)
    rounded = total.astype(BF).astype(F32)
    hsnd[0] = rounded[:REACH]
    hsnd[1] = rounded[REACH:]
    start(2)

    strips = rows // STRIP
    for pair in range(pairs_n):
        field = dot(rinv[...], prod[pair]).astype(BF)
        for i in range(2):
            part = field[:, i * col_freqs:(i + 1) * col_freqs]
            part = jnp.concatenate([part[:rows], part[rows:]], axis=1)
            at = (2 * pair + i) * STRIP
            for strip in range(strips):
                fields[strip, at:at + STRIP] = part[strip * STRIP:(strip + 1) * STRIP]
    sums = jnp.zeros((8, half), F32)
    for strip in range(strips):
        e = dot(fields[strip], cinv[...])
        total = jnp.zeros((STRIP, half), F32)
        for k in range(kernels):
            er = e[STRIP * k:STRIP * (k + 1), :half]
            ei = e[STRIP * k:STRIP * (k + 1), half:]
            total = total + weights[k] * (er * er + ei * ei)
        inten[strip * STRIP:(strip + 1) * STRIP] = total.astype(BF)
        for i in range(STRIP // 8):
            sums = sums + total[8 * i:8 * (i + 1)]
    center = jnp.sum(sums) * (1.0 / (rows * half))
    blurred = dot(rmid[...], inten[...]) - center
    dev = blurred.astype(BF)
    tile_out[...] = dev
    center_out[...] = jnp.zeros(center_out.shape, F32) + center
    loads["ftab"].wait()
    loads["btab"].wait()
    freqs = 2 * col_freqs
    lacking = jnp.sum(ftab[freqs:].astype(F32), axis=1, keepdims=True) * center
    lacking = jnp.concatenate([jnp.zeros((freqs, 1), F32), lacking], axis=0)
    that[...] = (dot_nt(ftab[...], dev) + lacking).astype(BF)
    arrive(1)

    span = cols // STEPS
    row_line = lax.broadcasted_iota(jnp.int32, (rows, cap), 0).astype(BF)
    step_line = lax.broadcasted_iota(jnp.int32, (btab.shape[1], cap), 0).astype(BF)
    end_line = lax.broadcasted_iota(jnp.int32, (2 * REACH, cap), 0).astype(F32)
    end_line = jnp.where(end_line < REACH, end_line, end_line + float(cols - 2 * REACH))

    def pick(index, period, function):
        found = jnp.full(index.shape, float(np.round(function(2.0 * math.pi * (STEPS - 1) * period / STEPS), 9)), F32)
        for i in range(STEPS - 1):
            found = jnp.where(index == i, float(np.round(function(2.0 * math.pi * i * period / STEPS), 9)), found)
        return found

    def ramp(line, low, part):
        zero = jnp.zeros((), BF)
        upper = jnp.where(line == (low + 1.0).astype(BF), part.astype(BF), zero)
        return jnp.where(line == low.astype(BF), (1.0 - part).astype(BF), upper)

    def coords(block):
        p = recs[block, :SITES, :] * float(rows - 1)
        q = recs[block, SITES:, :] * float(cols - 1)
        p0 = jnp.minimum(jnp.floor(p), float(rows - 2))
        q0 = jnp.minimum(jnp.floor(q), float(cols - 2))
        h = jnp.floor(q0 * (1.0 / span))
        return q, h, p0, p - p0, q0 - h * float(span), q - q0

    def prepare(block, slot):
        q, h, p0, p1, low, q1 = coords(block)
        for s in range(SITES):
            at = slice(s, s + 1)
            row_part[slot, s] = ramp(row_line, p0[at], p1[at])
            col_part[slot, s] = dot(btab[...], ramp(step_line, low[at], q1[at]))

    def evaluate(block, slot=None):
        q, h, p0, p1, low, q1 = coords(block)
        turn = [(pick(h, j, math.cos), pick(h, j, math.sin)) for j in range(1, STEPS // 2)]
        sign = pick(h, STEPS // 2, math.cos)
        acc = jnp.zeros((8, cap), F32)
        for s in range(SITES):
            at = slice(s, s + 1)
            if slot is None:
                g = dot(that[...], ramp(row_line, p0[at], p1[at]))
                e = dot(btab[...], ramp(step_line, low[at], q1[at]))
            else:
                g = dot(that[...], row_part[slot, s])
                e = col_part.at[slot, s]
            inner = [None] * (STEPS // 2 + 1)
            cross = [None] * (STEPS // 2 + 1)
            for i in range(col_freqs // 8):
                j = i * 8 * STEPS // col_freqs
                k = min(j, STEPS - j)
                gc, gs = g[8 * i:8 * i + 8], g[col_freqs + 8 * i:col_freqs + 8 * i + 8]
                ec, es = e[8 * i:8 * i + 8], e[col_freqs + 8 * i:col_freqs + 8 * i + 8]
                term = gc * ec + gs * es
                inner[k] = term if inner[k] is None else inner[k] + term
                if k in (0, STEPS // 2):
                    continue
                term = gs * ec - gc * es if j == k else gc * es - gs * ec
                cross[k] = term if cross[k] is None else cross[k] + term
            value = inner[0] + sign[at] * inner[STEPS // 2]
            for k in range(1, STEPS // 2):
                value = value + turn[k - 1][0][at] * inner[k] + turn[k - 1][1][at] * cross[k]
            ends = g[freqs:] * hat(end_line - q[at])
            acc = acc + (value + (ends[:REACH] + ends[REACH:]))
        mean = jnp.sum(acc, axis=0, keepdims=True) * (1.0 / SITES) + center * BLUR_SUM
        return jnp.broadcast_to(mean, (8, cap))

    first = jnp.where(even, 0, 2)
    arrive(2)
    edge = jnp.concatenate([halo[0], halo[1]], axis=0).astype(BF)
    added = dot(redge[...], edge)
    head = (blurred[:2 * REACH] + added[:2 * REACH]).astype(BF)
    foot = (blurred[rows - 2 * REACH:] + added[2 * REACH:]).astype(BF)
    tile_out[:2 * REACH] = head
    tile_out[rows - 2 * REACH:] = foot
    blank = jnp.zeros((128 - 4 * REACH, half), BF)
    spectra = dot_nt(ftab[...], jnp.concatenate([head, blank, foot], axis=0)) + lacking
    lane = lax.broadcasted_iota(jnp.int32, spectra.shape, 1)
    low_half, high_half = that[:, :128].astype(F32), that[:, rows - 128:].astype(F32)
    that[:, :128] = jnp.where(lane < 2 * REACH, spectra, low_half).astype(BF)
    that[:, rows - 128:] = jnp.where(lane >= 128 - 2 * REACH, spectra, high_half).astype(BF)

    rsnd[first] = evaluate(first)
    start_far(3)
    second = 2 - first
    rsnd[second] = evaluate(second)
    start_near(3)
    ret[1] = evaluate(1)
    arrive(3)
    back = jnp.concatenate([ret[0], ret[1], ret[2]], axis=1)
    found = dot(split3(back), sel[...])
    mean = found[0:1] + found[8:9] + found[16:17]
    load_thresh.wait()
    loads["bias"].wait()
    bias_out[...] = 0.5 * bias[...].astype(F32) - 2.0 * (mean - thresh[0, 0]).reshape(frags)

    for kind in range(4):
        @pl.when(has_left)
        def _():
            pairs[kind][0].wait_send()

        @pl.when(has_right)
        def _():
            pairs[kind][1].wait_send()


def finish(tile, wide, sums, center, bias_h, resist_h, nb_h, out, sem):
    chunks = wide.shape[0]
    width = wide.shape[2]
    through = pltpu.make_async_copy(bias_h, nb_h, sem.at[3])
    stores = [pltpu.make_async_copy(out.at[i], resist_h.at[:, pl.ds(i * width, width)], sem.at[4 + chunks + i])
              for i in range(chunks)]
    through.start()
    for i in range(chunks):
        out[i] = dot(tile[...], wide[i]) + center[0:1, 0:1] * sums[0:1, i * width:(i + 1) * width]
        stores[i].start()
    for store in stores:
        store.wait()
    through.wait()


def shards(mask, kernel_spectra, kernel_weights, threshold, eval_tile, site_coords, bias_steps):
    rows, cols = mask.shape
    row_freqs, kernels, col_freqs = kernel_spectra.shape[1:]
    frags = eval_tile.shape[0]
    cap = frags // 2
    names = ("colf", "rowf", "rinv", "redges", "cinv", "rmid", "redge", "wide", "sums", "ftab", "btab")
    values = dict(zip(names, (jnp.asarray(x) for x in tables(rows, cols, row_freqs, col_freqs))))
    values["mask"] = mask
    values["ks"] = jnp.transpose(kernel_spectra, (0, 2, 1, 3))
    values["ev"] = eval_tile.reshape(1, frags)
    values["sc"] = site_coords
    values["bias"] = bias_steps
    ordered = [values[k] for k in LOADED]
    vmem = pl.BlockSpec(memory_space=pltpu.VMEM)
    hbm = pl.BlockSpec(memory_space=pltpu.HBM)
    anyw = pl.BlockSpec(memory_space=pl.ANY)
    coarse = cols // GRID_STEP
    tile, new_bias, center = pl.pallas_call(
        kernel,
        out_shape=(pltpu.VMEM((rows, coarse), BF), pltpu.VMEM((frags,), F32), pltpu.VMEM((8, 128), F32)),
        in_specs=[hbm] * (2 + len(ordered)),
        out_specs=(vmem, vmem, vmem),
        scratch_shapes=[pltpu.VMEM(x.shape, x.dtype) for x in ordered] + [
            pltpu.SMEM((kernels,), F32),
            pltpu.SMEM((1, 1), F32),
            pltpu.VMEM((2, row_freqs, 2 * col_freqs), BF),
            pltpu.VMEM((2, row_freqs, 2 * col_freqs), BF),
            pltpu.VMEM((kernels // 2, 2 * row_freqs, 2 * col_freqs), BF),
            pltpu.VMEM((rows // STRIP, kernels * STRIP, 2 * col_freqs), BF),
            pltpu.VMEM((3, 2 * SITES, cap), F32),
            pltpu.VMEM((3, 2 * SITES, cap), F32),
            pltpu.VMEM((rows, coarse), BF),
            pltpu.VMEM((2, REACH, coarse), F32),
            pltpu.VMEM((2, REACH, coarse), F32),
            pltpu.VMEM((3, 8, cap), F32),
            pltpu.VMEM((3, 8, cap), F32),
            pltpu.VMEM((3 * cap, frags), BF),
            pltpu.VMEM((2 * col_freqs + 2 * REACH, rows), BF),
            pltpu.VMEM((PREPARED, SITES, rows, cap), BF),
            pltpu.VMEM((PREPARED, SITES, 2 * col_freqs, cap), F32),
            pltpu.SemaphoreType.DMA((len(ordered) + 2,)),
            pltpu.SemaphoreType.DMA((4, 2)),
            pltpu.SemaphoreType.DMA((4, 2)),
        ],
        compiler_params=pltpu.CompilerParams(
            collective_id=0, has_side_effects=True, vmem_limit_bytes=int(60 * 2 ** 20)),
    )(kernel_weights, threshold.reshape(1, 1), *ordered)
    width = cols // CHUNKS
    return pl.pallas_call(
        finish,
        out_shape=(jax.ShapeDtypeStruct((rows, cols), F32), jax.ShapeDtypeStruct((frags,), F32)),
        in_specs=[vmem] * 4 + [anyw],
        out_specs=(anyw, anyw),
        scratch_shapes=[
            pltpu.VMEM((CHUNKS, rows, width), F32),
            pltpu.SemaphoreType.DMA((4 + 2 * CHUNKS,)),
        ],
        compiler_params=pltpu.CompilerParams(vmem_limit_bytes=4 << 20),
    )(tile, values["wide"], values["sums"], center, new_bias)


def solution(mesh):
    placed = (
        P(("groups", "tx"), None),
        P(),
        P(),
        P(),
        P(("groups", "tx")),
        P(None, None, ("groups", "tx")),
        P(("groups", "tx")),
    )
    return jax.shard_map(
        shards,
        mesh=mesh,
        in_specs=placed,
        out_specs=(P(("groups", "tx"), None), P(("groups", "tx"))),
        check_vma=False,
    )
```

```python
import math

import jax
import jax.numpy as jnp
import ml_dtypes
import numpy as np
from jax import lax
from jax.experimental import pallas as pl
from jax.experimental.pallas import tpu as pltpu
from jax.sharding import PartitionSpec as P

HALO = 256
REACH = 8
EARLY = 5
SITES = 16
GRID_STEP = 4
STEPS = 8
SIGMA = 3.0
CHUNKS = 4
STRIP = 32
PREPARED = 1
BF = jnp.bfloat16
F32 = jnp.float32
MESH = pl.DeviceIdType.MESH
LOADED = ("mask", "colf", "rowf", "ev", "sc", "ks", "redges", "rinv", "cinv", "rmid", "redge", "ftab", "btab")


def host_bf16(x):
    return np.asarray(x, np.float32).astype(ml_dtypes.bfloat16)


def twiddle(position, frequency, period, amplitude):
    index = (position[:, None] * frequency[None, :]) % period
    angle = index.astype(np.float64) * (2.0 * math.pi / period)
    return np.cos(angle) * amplitude, np.sin(angle) * amplitude


def gauss(offset):
    every = np.arange(-REACH, REACH + 1)
    norm = np.sum(np.exp(-every * every / (2.0 * SIGMA * SIGMA)))
    value = np.exp(-offset * offset / (2.0 * SIGMA * SIGMA)) / norm
    return np.where(np.abs(offset) <= REACH, value, 0.0)


def tables(rows, cols, row_freqs, col_freqs):
    window = rows + 2 * HALO
    f = np.arange(col_freqs) - col_freqs // 2
    g = np.arange(row_freqs) - row_freqs // 2
    c, s = twiddle(np.arange(cols), f, cols, 1.0 / math.sqrt(cols))
    col_forward = host_bf16(np.concatenate([c, -s], 1))
    c, s = twiddle(g, np.arange(window), window, 1.0 / math.sqrt(window))
    row_forward = host_bf16(np.concatenate([c, -s], 0))
    c, s = twiddle(np.arange(rows) + HALO, g, window, 1.0 / math.sqrt(row_freqs))
    row_inverse = host_bf16(np.block([[c, -s], [s, c]]))
    ends = np.r_[0:REACH, rows - REACH:rows]
    inverse_ends = np.ascontiguousarray(row_inverse[np.concatenate([ends, rows + ends])])
    row_forward = np.concatenate([
        row_forward[:, HALO + rows:], row_forward[:, :HALO], row_forward[:, HALO:HALO + rows]], 0)
    picked = np.arange(0, cols, GRID_STEP)
    c, s = twiddle(f, picked, cols, 1.0 / math.sqrt(col_freqs))
    col_inverse = host_bf16(np.block([[c, s], [-s, c]]))
    diff = np.arange(cols)[None, :] - picked[:, None]
    order = np.arange(1, col_freqs)
    base = np.arange(cols)
    kernel = 1.0 + 2.0 * np.cos(2 * math.pi * ((base[:, None] * order[None, :]) % cols) / cols).sum(1)
    kernel = (kernel + np.cos(2 * math.pi * ((base * col_freqs) % cols) / cols)) / picked.size
    interp = kernel[diff % cols]
    lines = np.arange(cols)
    col_blur = host_bf16(gauss((lines[None, :] - lines[:, None]).astype(np.float64)))
    spread = interp @ col_blur.astype(np.float64)
    high = host_bf16(spread)
    wide = np.ascontiguousarray(high.reshape(picked.size, CHUNKS, cols // CHUNKS).transpose(1, 0, 2))
    sums = spread.sum(0).astype(np.float32)[None]
    row_diff = np.arange(rows + 2 * REACH)[None, :] - REACH - np.arange(rows)[:, None]
    row_blur = host_bf16(gauss(row_diff.astype(np.float64)))
    row_mid = np.ascontiguousarray(row_blur[:, REACH:REACH + rows])
    row_edge = np.concatenate([row_blur[:, :REACH], row_blur[:, REACH + rows:]], 1)
    row_edge = np.concatenate([row_edge[:2 * REACH], row_edge[rows - 2 * REACH:]], 0)
    return (col_forward, row_forward, row_inverse, inverse_ends, col_inverse, row_mid, row_edge, wide,
            sums) + site_tables(cols, col_freqs, interp, spread)


def site_tables(cols, col_freqs, interp, spread):
    coarse = cols // GRID_STEP
    span = cols // STEPS
    line = np.arange(cols)
    reach = np.arange(-REACH, REACH + 1)
    weight = host_bf16(gauss(reach.astype(np.float64))).astype(np.float64)
    periodic = np.zeros((cols, cols))
    for d, w in zip(reach, weight):
        periodic[(line - d) % cols, line] += w
    order = np.concatenate([np.arange(j, col_freqs, STEPS) for j in range(STEPS)])
    angle = 2.0 * math.pi * ((np.arange(col_freqs + 1)[:, None] * reach[None, :]) % cols) / cols
    response = (weight[None, :] * np.cos(angle)).sum(1)
    scale = (np.where(order == 0, 1.0, 2.0) * response[order] / coarse)[:, None]
    angle = 2.0 * math.pi * ((order[:, None] * GRID_STEP * np.arange(coarse)[None, :]) % cols) / cols
    cosine, sine = scale * np.cos(angle), scale * np.sin(angle)
    sine[0] = response[col_freqs] / coarse * np.cos(math.pi * np.arange(coarse))
    ends = np.r_[0:REACH, cols - REACH:cols]
    lacking = (spread - interp @ periodic)[:, ends].T
    steps = np.arange(-(-(span + 1) // 16) * 16)
    angle = 2.0 * math.pi * ((order[:, None] * steps[None, :]) % cols) / cols
    base_cos, base_sin = np.cos(angle), np.sin(angle)
    base_sin[0] = np.cos(2.0 * math.pi * ((col_freqs * steps) % cols) / cols)
    return (host_bf16(np.concatenate([cosine, sine, lacking], 0)), host_bf16(np.concatenate([base_cos, base_sin], 0)))


BLUR_SUM = float(host_bf16(gauss(np.arange(-REACH, REACH + 1.0))).astype(np.float64).sum())


def dot(a, b):
    return jnp.dot(a, b, preferred_element_type=F32)


def dot_nt(a, b):
    return lax.dot_general(a, b, (((1,), (1,)), ((), ())), preferred_element_type=F32)


def split3(x):
    high = x.astype(BF)
    rest = x - high.astype(F32)
    mid = rest.astype(BF)
    low = (rest - mid.astype(F32)).astype(BF)
    return jnp.concatenate([high, mid, low], axis=0)


def hat(distance):
    return jnp.maximum(1.0 - jnp.abs(distance), 0.0)


def kernel(weights_h, *refs):
    n = len(LOADED)
    sources = dict(zip(LOADED, refs[:n]))
    tile_out, sel, means_out, center_out = refs[n:n + 4]
    held = dict(zip(LOADED, refs[n + 4:2 * n + 4]))
    (weights, psnd, prec, prod, fields, snd, recs, inten, hsnd, halo, rsnd, ret, that, row_part, col_part,
     local_sem, send_sem, recv_sem) = refs[2 * n + 4:]
    mask, colf, rowf, ev, sc, ksv, rends, rinv, cinv, rmid, redge, ftab, btab = (held[k] for k in LOADED)
    t = lax.axis_index("tx")
    count = lax.axis_size("tx")
    has_left = t > 0
    has_right = t < count - 1
    rows, cols = mask.shape
    coarse = cols // GRID_STEP
    kernels, row_freqs, col_freqs = ksv.shape[1:]
    frags = ev.shape[1]
    cap = frags // 2

    barrier = pltpu.get_barrier_semaphore()

    @pl.when(has_left)
    def _():
        pl.semaphore_signal(barrier, inc=1, device_id={"tx": t - 1}, device_id_type=MESH)

    @pl.when(has_right)
    def _():
        pl.semaphore_signal(barrier, inc=1, device_id={"tx": t + 1}, device_id_type=MESH)

    loads = {k: pltpu.make_async_copy(sources[k], held[k], local_sem.at[i])
             for i, k in enumerate(LOADED)}
    for k in LOADED[:EARLY]:
        loads[k].start()
    load_weights = pltpu.make_async_copy(weights_h, weights, local_sem.at[n])

    def to_left(kind, src, dst):
        return pltpu.make_async_remote_copy(
            src_ref=src, dst_ref=dst, send_sem=send_sem.at[kind, 0], recv_sem=recv_sem.at[kind, 0],
            device_id={"tx": t - 1}, device_id_type=MESH)

    def to_right(kind, src, dst):
        return pltpu.make_async_remote_copy(
            src_ref=src, dst_ref=dst, send_sem=send_sem.at[kind, 1], recv_sem=recv_sem.at[kind, 1],
            device_id={"tx": t + 1}, device_id_type=MESH)

    pairs = (
        (to_left(0, psnd.at[0], prec.at[1]), to_right(0, psnd.at[1], prec.at[0])),
        (to_left(1, snd.at[0], recs.at[2]), to_right(1, snd.at[2], recs.at[0])),
        (to_left(2, hsnd.at[0], halo.at[1]), to_right(2, hsnd.at[1], halo.at[0])),
        (to_left(3, rsnd.at[0, pl.ds(0, 1)], ret.at[2, pl.ds(0, 1)]),
         to_right(3, rsnd.at[2, pl.ds(0, 1)], ret.at[0, pl.ds(0, 1)])),
    )

    even = t % 2 == 0
    odd = jnp.logical_not(even)

    def start_far(kind):
        @pl.when(jnp.logical_and(even, has_left))
        def _():
            pairs[kind][0].start()

        @pl.when(jnp.logical_and(odd, has_right))
        def _():
            pairs[kind][1].start()

    def start_near(kind):
        @pl.when(jnp.logical_and(even, has_right))
        def _():
            pairs[kind][1].start()

        @pl.when(jnp.logical_and(odd, has_left))
        def _():
            pairs[kind][0].start()

    def start(kind):
        start_far(kind)
        start_near(kind)

    def arrive(kind):
        @pl.when(has_right)
        def _():
            pairs[kind][0].wait_recv()

        @pl.when(has_left)
        def _():
            pairs[kind][1].wait_recv()

    @pl.when(jnp.logical_not(has_left))
    def _():
        prec[0] = jnp.zeros(prec.shape[1:], BF)
        recs[0] = jnp.zeros(recs.shape[1:], F32)
        halo[0] = jnp.zeros(halo.shape[1:], F32)
        ret[0] = jnp.zeros(ret.shape[1:], F32)

    @pl.when(jnp.logical_not(has_right))
    def _():
        prec[1] = jnp.zeros(prec.shape[1:], BF)
        recs[2] = jnp.zeros(recs.shape[1:], F32)
        halo[1] = jnp.zeros(halo.shape[1:], F32)
        ret[2] = jnp.zeros(ret.shape[1:], F32)

    loads["mask"].wait()
    loads["colf"].wait()
    for k in LOADED[EARLY:]:
        loads[k].start()
    load_weights.start()
    win = dot(mask[...], colf[...]).astype(BF)
    loads["rowf"].wait()

    def spectrum(i):
        product = dot(rowf[2 * row_freqs * i:2 * row_freqs * (i + 1)], win)
        upper = product[:row_freqs]
        lower = product[row_freqs:]
        return (upper[:, :col_freqs] - lower[:, col_freqs:], upper[:, col_freqs:] + lower[:, :col_freqs])

    for i in range(2):
        psnd[i] = jnp.concatenate(spectrum(i), axis=1).astype(BF)

    between = jnp.logical_and(has_left, has_right)

    @pl.when(between)
    def _():
        pl.semaphore_wait(barrier, 2)

    @pl.when(jnp.logical_not(between))
    def _():
        pl.semaphore_wait(barrier, 1)

    start(0)
    own_real, own_imag = spectrum(2)

    loads["ev"].wait()
    loads["sc"].wait()
    offset = ev[...] - t + 1
    member = jnp.where(lax.broadcasted_iota(jnp.int32, (8, frags), 0) == offset, 1.0, 0.0)
    upper = jnp.where(
        lax.broadcasted_iota(jnp.int32, (frags, frags), 0)
        <= lax.broadcasted_iota(jnp.int32, (frags, frags), 1), 1.0, 0.0).astype(BF)
    inclusive = dot(member.astype(BF), upper)
    rank = jnp.sum(member * (inclusive - 1.0), axis=0, keepdims=True)
    slot = offset.astype(F32) * float(cap) + rank
    slot_line = lax.broadcasted_iota(jnp.int32, (3 * cap, frags), 0).astype(F32)
    sel[...] = jnp.where(slot_line == slot, 1.0, 0.0).astype(BF)
    records = jnp.concatenate([sc[0], sc[1]], axis=0)
    packed = dot_nt(split3(records), sel[...])
    n_rec = 2 * SITES
    packed = packed[:n_rec] + packed[n_rec:2 * n_rec] + packed[2 * n_rec:]
    snd[0] = packed[:, :cap]
    recs[1] = packed[:, cap:2 * cap]
    snd[2] = packed[:, 2 * cap:]
    start(1)

    for k in ("ks", "redges", "rinv", "cinv", "rmid", "redge"):
        loads[k].wait()
    load_weights.wait()
    arrive(0)
    near = prec[0].astype(F32) + prec[1].astype(F32)
    real = own_real + near[:, :col_freqs]
    imag = own_imag + near[:, col_freqs:]

    half = cinv.shape[1] // 2
    pairs_n = kernels // 2
    ends = []
    for pair in range(pairs_n):
        blocks = []
        for k in (2 * pair, 2 * pair + 1):
            kr = ksv[0, k]
            ki = ksv[1, k]
            blocks.append(jnp.concatenate(
                [(kr * real - ki * imag).astype(BF), (kr * imag + ki * real).astype(BF)], axis=0))
        block = jnp.concatenate(blocks, axis=1)
        prod[pair] = block
        field = dot(rends[...], block).astype(BF)
        for i in range(2):
            part = field[:, i * col_freqs:(i + 1) * col_freqs]
            ends.append(jnp.concatenate([part[:2 * REACH], part[2 * REACH:]], axis=1))
    e = dot(jnp.concatenate(ends, axis=0), cinv[...])
    total = jnp.zeros((2 * REACH, half), F32)
    for k in range(kernels):
        er = e[2 * REACH * k:2 * REACH * (k + 1), :half]
        ei = e[2 * REACH * k:2 * REACH * (k + 1), half:]
        total = total + weights[k] * (er * er + ei * ei)
    rounded = total.astype(BF).astype(F32)
    hsnd[0] = rounded[:REACH]
    hsnd[1] = rounded[REACH:]
    start(2)

    strips = rows // STRIP
    for pair in range(pairs_n):
        field = dot(rinv[...], prod[pair]).astype(BF)
        for i in range(2):
            part = field[:, i * col_freqs:(i + 1) * col_freqs]
            part = jnp.concatenate([part[:rows], part[rows:]], axis=1)
            at = (2 * pair + i) * STRIP
            for strip in range(strips):
                fields[strip, at:at + STRIP] = part[strip * STRIP:(strip + 1) * STRIP]
    sums = jnp.zeros((8, half), F32)
    for strip in range(strips):
        e = dot(fields[strip], cinv[...])
        total = jnp.zeros((STRIP, half), F32)
        for k in range(kernels):
            er = e[STRIP * k:STRIP * (k + 1), :half]
            ei = e[STRIP * k:STRIP * (k + 1), half:]
            total = total + weights[k] * (er * er + ei * ei)
        inten[strip * STRIP:(strip + 1) * STRIP] = total.astype(BF)
        for i in range(STRIP // 8):
            sums = sums + total[8 * i:8 * (i + 1)]
    center = jnp.sum(sums) * (1.0 / (rows * half))
    blurred = dot(rmid[...], inten[...]) - center
    dev = blurred.astype(BF)
    tile_out[...] = dev
    center_out[...] = jnp.zeros(center_out.shape, F32) + center
    loads["ftab"].wait()
    loads["btab"].wait()
    freqs = 2 * col_freqs
    lacking = jnp.sum(ftab[freqs:].astype(F32), axis=1, keepdims=True) * center
    lacking = jnp.concatenate([jnp.zeros((freqs, 1), F32), lacking], axis=0)
    that[...] = (dot_nt(ftab[...], dev) + lacking).astype(BF)
    arrive(1)

    span = cols // STEPS
    row_line = lax.broadcasted_iota(jnp.int32, (rows, cap), 0).astype(BF)
    step_line = lax.broadcasted_iota(jnp.int32, (btab.shape[1], cap), 0).astype(BF)
    end_line = lax.broadcasted_iota(jnp.int32, (2 * REACH, cap), 0).astype(F32)
    end_line = jnp.where(end_line < REACH, end_line, end_line + float(cols - 2 * REACH))

    def pick(index, period, function):
        found = jnp.full(index.shape, float(np.round(function(2.0 * math.pi * (STEPS - 1) * period / STEPS), 9)), F32)
        for i in range(STEPS - 1):
            found = jnp.where(index == i, float(np.round(function(2.0 * math.pi * i * period / STEPS), 9)), found)
        return found

    def ramp(line, low, part):
        zero = jnp.zeros((), BF)
        upper = jnp.where(line == (low + 1.0).astype(BF), part.astype(BF), zero)
        return jnp.where(line == low.astype(BF), (1.0 - part).astype(BF), upper)

    def coords(block):
        p = recs[block, :SITES, :] * float(rows - 1)
        q = recs[block, SITES:, :] * float(cols - 1)
        p0 = jnp.minimum(jnp.floor(p), float(rows - 2))
        q0 = jnp.minimum(jnp.floor(q), float(cols - 2))
        h = jnp.floor(q0 * (1.0 / span))
        return q, h, p0, p - p0, q0 - h * float(span), q - q0

    def prepare(block, slot):
        q, h, p0, p1, low, q1 = coords(block)
        for s in range(SITES):
            at = slice(s, s + 1)
            row_part[slot, s] = ramp(row_line, p0[at], p1[at])
            col_part[slot, s] = dot(btab[...], ramp(step_line, low[at], q1[at]))

    def evaluate(block, slot=None):
        q, h, p0, p1, low, q1 = coords(block)
        turn = [(pick(h, j, math.cos), pick(h, j, math.sin)) for j in range(1, STEPS // 2)]
        sign = pick(h, STEPS // 2, math.cos)
        acc = jnp.zeros((8, cap), F32)
        for s in range(SITES):
            at = slice(s, s + 1)
            if slot is None:
                g = dot(that[...], ramp(row_line, p0[at], p1[at]))
                e = dot(btab[...], ramp(step_line, low[at], q1[at]))
            else:
                g = dot(that[...], row_part[slot, s])
                e = col_part.at[slot, s]
            inner = [None] * (STEPS // 2 + 1)
            cross = [None] * (STEPS // 2 + 1)
            for i in range(col_freqs // 8):
                j = i * 8 * STEPS // col_freqs
                k = min(j, STEPS - j)
                gc, gs = g[8 * i:8 * i + 8], g[col_freqs + 8 * i:col_freqs + 8 * i + 8]
                ec, es = e[8 * i:8 * i + 8], e[col_freqs + 8 * i:col_freqs + 8 * i + 8]
                term = gc * ec + gs * es
                inner[k] = term if inner[k] is None else inner[k] + term
                if k in (0, STEPS // 2):
                    continue
                term = gs * ec - gc * es if j == k else gc * es - gs * ec
                cross[k] = term if cross[k] is None else cross[k] + term
            value = inner[0] + sign[at] * inner[STEPS // 2]
            for k in range(1, STEPS // 2):
                value = value + turn[k - 1][0][at] * inner[k] + turn[k - 1][1][at] * cross[k]
            ends = g[freqs:] * hat(end_line - q[at])
            acc = acc + (value + (ends[:REACH] + ends[REACH:]))
        mean = jnp.sum(acc, axis=0, keepdims=True) * (1.0 / SITES) + center * BLUR_SUM
        return jnp.broadcast_to(mean, (8, cap))

    first = jnp.where(even, 0, 2)
    arrive(2)
    edge = jnp.concatenate([halo[0], halo[1]], axis=0).astype(BF)
    added = dot(redge[...], edge)
    head = (blurred[:2 * REACH] + added[:2 * REACH]).astype(BF)
    foot = (blurred[rows - 2 * REACH:] + added[2 * REACH:]).astype(BF)
    tile_out[:2 * REACH] = head
    tile_out[rows - 2 * REACH:] = foot
    blank = jnp.zeros((128 - 4 * REACH, half), BF)
    spectra = dot_nt(ftab[...], jnp.concatenate([head, blank, foot], axis=0)) + lacking
    lane = lax.broadcasted_iota(jnp.int32, spectra.shape, 1)
    low_half, high_half = that[:, :128].astype(F32), that[:, rows - 128:].astype(F32)
    that[:, :128] = jnp.where(lane < 2 * REACH, spectra, low_half).astype(BF)
    that[:, rows - 128:] = jnp.where(lane >= 128 - 2 * REACH, spectra, high_half).astype(BF)

    rsnd[first] = evaluate(first)
    start_far(3)
    second = 2 - first
    rsnd[second] = evaluate(second)
    start_near(3)
    ret[1] = evaluate(1)
    arrive(3)
    means_out[...] = jnp.broadcast_to(
        jnp.concatenate([ret[0, 0:1], ret[1, 0:1], ret[2, 0:1]], axis=1), means_out.shape)

    for kind in range(4):
        @pl.when(has_left)
        def _():
            pairs[kind][0].wait_send()

        @pl.when(has_right)
        def _():
            pairs[kind][1].wait_send()


def finish(tile, wide, sums, center, sel, means, steps_h, thresh_h, resist_h, nb_h, out, nb, steps, thresh, sem):
    chunks = wide.shape[0]
    width = wide.shape[2]
    ask = pltpu.make_async_copy(thresh_h, thresh, sem.at[0])
    load = pltpu.make_async_copy(steps_h, steps, sem.at[1])
    last = pltpu.make_async_copy(nb, nb_h, sem.at[2])
    stores = [pltpu.make_async_copy(out.at[i], resist_h.at[:, pl.ds(i * width, width)], sem.at[3 + i])
              for i in range(chunks)]
    ask.start(priority=1)
    load.start(priority=1)
    for i in range(chunks):
        out[i] = dot(tile[...], wide[i]) + center[0:1, 0:1] * sums[0:1, i * width:(i + 1) * width]
        stores[i].start()
    found = dot(split3(means[0:1]), sel[...])
    mean = found[0:1] + found[1:2] + found[2:3]
    ask.wait()
    load.wait()
    nb[...] = 0.5 * steps[...].astype(F32) - 2.0 * (mean - thresh[...]).reshape(nb.shape)
    last.start(priority=1)
    for store in stores:
        store.wait()
    last.wait()


def shards(mask, kernel_spectra, kernel_weights, threshold, eval_tile, site_coords, bias_steps):
    rows, cols = mask.shape
    row_freqs, kernels, col_freqs = kernel_spectra.shape[1:]
    frags = eval_tile.shape[0]
    threshold = lax.ppermute(threshold, "tx", [(i, i ^ 1) for i in range(lax.axis_size("tx"))])
    cap = frags // 2
    names = ("colf", "rowf", "rinv", "redges", "cinv", "rmid", "redge", "wide", "sums", "ftab", "btab")
    values = dict(zip(names, (jnp.asarray(x) for x in tables(rows, cols, row_freqs, col_freqs))))
    values["mask"] = mask
    values["ks"] = jnp.transpose(kernel_spectra, (0, 2, 1, 3))
    values["ev"] = eval_tile.reshape(1, frags)
    values["sc"] = site_coords
    ordered = [values[k] for k in LOADED]
    vmem = pl.BlockSpec(memory_space=pltpu.VMEM)
    hbm = pl.BlockSpec(memory_space=pltpu.HBM)
    anyw = pl.BlockSpec(memory_space=pl.ANY)
    coarse = cols // GRID_STEP
    tile, sel, means, center = pl.pallas_call(
        kernel,
        out_shape=(pltpu.VMEM((rows, coarse), BF), pltpu.VMEM((3 * cap, frags), BF),
                   pltpu.VMEM((8, 3 * cap), F32), pltpu.VMEM((8, 128), F32)),
        in_specs=[hbm] * (1 + len(ordered)),
        out_specs=(vmem, vmem, vmem, vmem),
        scratch_shapes=[pltpu.VMEM(x.shape, x.dtype) for x in ordered] + [
            pltpu.SMEM((kernels,), F32),
            pltpu.VMEM((2, row_freqs, 2 * col_freqs), BF),
            pltpu.VMEM((2, row_freqs, 2 * col_freqs), BF),
            pltpu.VMEM((kernels // 2, 2 * row_freqs, 2 * col_freqs), BF),
            pltpu.VMEM((rows // STRIP, kernels * STRIP, 2 * col_freqs), BF),
            pltpu.VMEM((3, 2 * SITES, cap), F32),
            pltpu.VMEM((3, 2 * SITES, cap), F32),
            pltpu.VMEM((rows, coarse), BF),
            pltpu.VMEM((2, REACH, coarse), F32),
            pltpu.VMEM((2, REACH, coarse), F32),
            pltpu.VMEM((3, 8, cap), F32),
            pltpu.VMEM((3, 8, cap), F32),
            pltpu.VMEM((2 * col_freqs + 2 * REACH, rows), BF),
            pltpu.VMEM((PREPARED, SITES, rows, cap), BF),
            pltpu.VMEM((PREPARED, SITES, 2 * col_freqs, cap), F32),
            pltpu.SemaphoreType.DMA((len(ordered) + 1,)),
            pltpu.SemaphoreType.DMA((4, 2)),
            pltpu.SemaphoreType.DMA((4, 2)),
        ],
        compiler_params=pltpu.CompilerParams(
            collective_id=0, has_side_effects=True, vmem_limit_bytes=int(60 * 2 ** 20)),
    )(kernel_weights, *ordered)
    width = cols // CHUNKS
    return pl.pallas_call(
        finish,
        out_shape=(jax.ShapeDtypeStruct((rows, cols), F32), jax.ShapeDtypeStruct((frags,), F32)),
        in_specs=[vmem] * 6 + [anyw] * 2,
        out_specs=(anyw, anyw),
        scratch_shapes=[
            pltpu.VMEM((CHUNKS, rows, width), F32),
            pltpu.VMEM((frags,), F32),
            pltpu.VMEM((frags,), jnp.int32),
            pltpu.VMEM((1, 1), F32),
            pltpu.SemaphoreType.DMA((3 + CHUNKS,)),
        ],
        compiler_params=pltpu.CompilerParams(vmem_limit_bytes=4 << 20),
    )(tile, values["wide"], values["sums"], center, sel, means, bias_steps, threshold.reshape(1, 1))


def solution(mesh):
    placed = (
        P(("groups", "tx"), None),
        P(),
        P(),
        P(),
        P(("groups", "tx")),
        P(None, None, ("groups", "tx")),
        P(("groups", "tx")),
    )
    return jax.shard_map(
        shards,
        mesh=mesh,
        in_specs=placed,
        out_specs=(P(("groups", "tx"), None), P(("groups", "tx"))),
        check_vma=False,
    )
```

```python
import math

import jax
import jax.numpy as jnp
import ml_dtypes
import numpy as np
from jax import lax
from jax.experimental import pallas as pl
from jax.experimental.pallas import tpu as pltpu
from jax.sharding import PartitionSpec as P

HALO = 256
REACH = 8
EARLY = 5
SITES = 16
GRID_STEP = 4
STEPS = 8
SIGMA = 3.0
CHUNKS = 4
STRIP = 32
BF = jnp.bfloat16
F32 = jnp.float32
MESH = pl.DeviceIdType.MESH
LOADED = ("mask", "colf", "rowf", "ev", "sc", "ks", "redges", "rinv", "cinv", "rmid", "redge", "ftab", "btab")


def host_bf16(x):
    return np.asarray(x, np.float32).astype(ml_dtypes.bfloat16)


def twiddle(position, frequency, period, amplitude):
    index = (position[:, None] * frequency[None, :]) % period
    angle = index.astype(np.float64) * (2.0 * math.pi / period)
    return np.cos(angle) * amplitude, np.sin(angle) * amplitude


def gauss(offset):
    every = np.arange(-REACH, REACH + 1)
    norm = np.sum(np.exp(-every * every / (2.0 * SIGMA * SIGMA)))
    value = np.exp(-offset * offset / (2.0 * SIGMA * SIGMA)) / norm
    return np.where(np.abs(offset) <= REACH, value, 0.0)


def tables(rows, cols, row_freqs, col_freqs):
    window = rows + 2 * HALO
    f = np.arange(col_freqs) - col_freqs // 2
    g = np.arange(row_freqs) - row_freqs // 2
    c, s = twiddle(np.arange(cols), f, cols, 1.0 / math.sqrt(cols))
    col_forward = host_bf16(np.concatenate([c, -s], 1))
    c, s = twiddle(g, np.arange(window), window, 1.0 / math.sqrt(window))
    row_forward = host_bf16(np.concatenate([c, -s], 0))
    c, s = twiddle(np.arange(rows) + HALO, g, window, 1.0 / math.sqrt(row_freqs))
    row_inverse = host_bf16(np.block([[c, -s], [s, c]]))
    ends = np.r_[0:REACH, rows - REACH:rows]
    inverse_ends = np.ascontiguousarray(row_inverse[np.concatenate([ends, rows + ends])])
    row_forward = np.concatenate([
        row_forward[:, HALO + rows:], row_forward[:, :HALO], row_forward[:, HALO:HALO + rows]], 0)
    picked = np.arange(0, cols, GRID_STEP)
    c, s = twiddle(f, picked, cols, 1.0 / math.sqrt(col_freqs))
    col_inverse = host_bf16(np.block([[c, s], [-s, c]]))
    diff = np.arange(cols)[None, :] - picked[:, None]
    order = np.arange(1, col_freqs)
    base = np.arange(cols)
    kernel = 1.0 + 2.0 * np.cos(2 * math.pi * ((base[:, None] * order[None, :]) % cols) / cols).sum(1)
    kernel = (kernel + np.cos(2 * math.pi * ((base * col_freqs) % cols) / cols)) / picked.size
    interp = kernel[diff % cols]
    lines = np.arange(cols)
    col_blur = host_bf16(gauss((lines[None, :] - lines[:, None]).astype(np.float64)))
    spread = interp @ col_blur.astype(np.float64)
    high = host_bf16(spread)
    wide = np.ascontiguousarray(high.reshape(picked.size, CHUNKS, cols // CHUNKS).transpose(1, 0, 2))
    sums = spread.sum(0).astype(np.float32)[None]
    row_diff = np.arange(rows + 2 * REACH)[None, :] - REACH - np.arange(rows)[:, None]
    row_blur = host_bf16(gauss(row_diff.astype(np.float64)))
    row_mid = np.ascontiguousarray(row_blur[:, REACH:REACH + rows])
    row_edge = np.concatenate([row_blur[:, :REACH], row_blur[:, REACH + rows:]], 1)
    row_edge = np.concatenate([row_edge[:2 * REACH], row_edge[rows - 2 * REACH:]], 0)
    return (col_forward, row_forward, row_inverse, inverse_ends, col_inverse, row_mid, row_edge, wide,
            sums) + site_tables(cols, col_freqs, interp, spread)


def site_tables(cols, col_freqs, interp, spread):
    coarse = cols // GRID_STEP
    span = cols // STEPS
    line = np.arange(cols)
    reach = np.arange(-REACH, REACH + 1)
    weight = host_bf16(gauss(reach.astype(np.float64))).astype(np.float64)
    periodic = np.zeros((cols, cols))
    for d, w in zip(reach, weight):
        periodic[(line - d) % cols, line] += w
    order = np.concatenate([np.arange(j, col_freqs, STEPS) for j in range(STEPS)])
    angle = 2.0 * math.pi * ((np.arange(col_freqs + 1)[:, None] * reach[None, :]) % cols) / cols
    response = (weight[None, :] * np.cos(angle)).sum(1)
    scale = (np.where(order == 0, 1.0, 2.0) * response[order] / coarse)[:, None]
    angle = 2.0 * math.pi * ((order[:, None] * GRID_STEP * np.arange(coarse)[None, :]) % cols) / cols
    cosine, sine = scale * np.cos(angle), scale * np.sin(angle)
    sine[0] = response[col_freqs] / coarse * np.cos(math.pi * np.arange(coarse))
    ends = np.r_[0:REACH, cols - REACH:cols]
    lacking = (spread - interp @ periodic)[:, ends].T
    steps = np.arange(-(-(span + 1) // 16) * 16)
    angle = 2.0 * math.pi * ((order[:, None] * steps[None, :]) % cols) / cols
    base_cos, base_sin = np.cos(angle), np.sin(angle)
    base_sin[0] = np.cos(2.0 * math.pi * ((col_freqs * steps) % cols) / cols)
    return (host_bf16(np.concatenate([cosine, sine, lacking], 0)), host_bf16(np.concatenate([base_cos, base_sin], 0)))


BLUR_SUM = float(host_bf16(gauss(np.arange(-REACH, REACH + 1.0))).astype(np.float64).sum())


def dot(a, b):
    return jnp.dot(a, b, preferred_element_type=F32)


def dot_nt(a, b):
    return lax.dot_general(a, b, (((1,), (1,)), ((), ())), preferred_element_type=F32)


def split3(x):
    high = x.astype(BF)
    rest = x - high.astype(F32)
    mid = rest.astype(BF)
    low = (rest - mid.astype(F32)).astype(BF)
    return jnp.concatenate([high, mid, low], axis=0)


def hat(distance):
    return jnp.maximum(1.0 - jnp.abs(distance), 0.0)


def kernel(weights_h, thresh_h, *refs):
    n = len(LOADED)
    sources = dict(zip(LOADED, refs[:n]))
    tile_out, sel, means_out, center_out = refs[n:n + 4]
    held = dict(zip(LOADED, refs[n + 4:2 * n + 4]))
    (weights, thresh, psnd, prec, prod, fields, snd, recs, inten, hsnd, halo, rsnd, ret, that,
     local_sem, send_sem, recv_sem) = refs[2 * n + 4:]
    mask, colf, rowf, ev, sc, ksv, rends, rinv, cinv, rmid, redge, ftab, btab = (held[k] for k in LOADED)
    t = lax.axis_index("tx")
    count = lax.axis_size("tx")
    has_left = t > 0
    has_right = t < count - 1
    rows, cols = mask.shape
    coarse = cols // GRID_STEP
    kernels, row_freqs, col_freqs = ksv.shape[1:]
    frags = ev.shape[1]
    cap = frags // 2

    barrier = pltpu.get_barrier_semaphore()

    @pl.when(has_left)
    def _():
        pl.semaphore_signal(barrier, inc=1, device_id={"tx": t - 1}, device_id_type=MESH)

    @pl.when(has_right)
    def _():
        pl.semaphore_signal(barrier, inc=1, device_id={"tx": t + 1}, device_id_type=MESH)

    loads = {k: pltpu.make_async_copy(sources[k], held[k], local_sem.at[i])
             for i, k in enumerate(LOADED)}
    for k in LOADED[:EARLY]:
        loads[k].start()
    load_weights = pltpu.make_async_copy(weights_h, weights, local_sem.at[n])

    load_thresh = pltpu.make_async_copy(thresh_h, thresh, local_sem.at[n + 1])

    def to_left(kind, src, dst):
        return pltpu.make_async_remote_copy(
            src_ref=src, dst_ref=dst, send_sem=send_sem.at[kind, 0], recv_sem=recv_sem.at[kind, 0],
            device_id={"tx": t - 1}, device_id_type=MESH)

    def to_right(kind, src, dst):
        return pltpu.make_async_remote_copy(
            src_ref=src, dst_ref=dst, send_sem=send_sem.at[kind, 1], recv_sem=recv_sem.at[kind, 1],
            device_id={"tx": t + 1}, device_id_type=MESH)

    pairs = (
        (to_left(0, psnd.at[0], prec.at[1]), to_right(0, psnd.at[1], prec.at[0])),
        (to_left(1, snd.at[0], recs.at[2]), to_right(1, snd.at[2], recs.at[0])),
        (to_left(2, hsnd.at[0], halo.at[1]), to_right(2, hsnd.at[1], halo.at[0])),
        (to_left(3, rsnd.at[0, pl.ds(0, 1)], ret.at[2, pl.ds(0, 1)]),
         to_right(3, rsnd.at[2, pl.ds(0, 1)], ret.at[0, pl.ds(0, 1)])),
    )

    even = t % 2 == 0
    odd = jnp.logical_not(even)

    def start_far(kind):
        @pl.when(jnp.logical_and(even, has_left))
        def _():
            pairs[kind][0].start()

        @pl.when(jnp.logical_and(odd, has_right))
        def _():
            pairs[kind][1].start()

    def start_near(kind):
        @pl.when(jnp.logical_and(even, has_right))
        def _():
            pairs[kind][1].start()

        @pl.when(jnp.logical_and(odd, has_left))
        def _():
            pairs[kind][0].start()

    def start(kind):
        start_far(kind)
        start_near(kind)

    def arrive(kind):
        @pl.when(has_right)
        def _():
            pairs[kind][0].wait_recv()

        @pl.when(has_left)
        def _():
            pairs[kind][1].wait_recv()

    @pl.when(jnp.logical_not(has_left))
    def _():
        prec[0] = jnp.zeros(prec.shape[1:], BF)
        recs[0] = jnp.zeros(recs.shape[1:], F32)
        halo[0] = jnp.zeros(halo.shape[1:], F32)
        ret[0] = jnp.zeros(ret.shape[1:], F32)

    @pl.when(jnp.logical_not(has_right))
    def _():
        prec[1] = jnp.zeros(prec.shape[1:], BF)
        recs[2] = jnp.zeros(recs.shape[1:], F32)
        halo[1] = jnp.zeros(halo.shape[1:], F32)
        ret[2] = jnp.zeros(ret.shape[1:], F32)

    loads["mask"].wait()
    loads["colf"].wait()
    for k in LOADED[EARLY:]:
        loads[k].start()
    load_weights.start()
    load_thresh.start()
    win = dot(mask[...], colf[...]).astype(BF)
    loads["rowf"].wait()

    def spectrum(i):
        product = dot(rowf[2 * row_freqs * i:2 * row_freqs * (i + 1)], win)
        upper = product[:row_freqs]
        lower = product[row_freqs:]
        return (upper[:, :col_freqs] - lower[:, col_freqs:], upper[:, col_freqs:] + lower[:, :col_freqs])

    for i in range(2):
        psnd[i] = jnp.concatenate(spectrum(i), axis=1).astype(BF)

    between = jnp.logical_and(has_left, has_right)

    @pl.when(between)
    def _():
        pl.semaphore_wait(barrier, 2)

    @pl.when(jnp.logical_not(between))
    def _():
        pl.semaphore_wait(barrier, 1)

    start(0)
    own_real, own_imag = spectrum(2)

    loads["ev"].wait()
    loads["sc"].wait()
    offset = ev[...] - t + 1
    member = jnp.where(lax.broadcasted_iota(jnp.int32, (8, frags), 0) == offset, 1.0, 0.0)
    upper = jnp.where(
        lax.broadcasted_iota(jnp.int32, (frags, frags), 0)
        <= lax.broadcasted_iota(jnp.int32, (frags, frags), 1), 1.0, 0.0).astype(BF)
    inclusive = dot(member.astype(BF), upper)
    rank = jnp.sum(member * (inclusive - 1.0), axis=0, keepdims=True)
    slot = offset.astype(F32) * float(cap) + rank
    slot_line = lax.broadcasted_iota(jnp.int32, (3 * cap, frags), 0).astype(F32)
    sel[...] = jnp.where(slot_line == slot, 1.0, 0.0).astype(BF)
    records = jnp.concatenate([sc[0], sc[1]], axis=0)
    packed = dot_nt(split3(records), sel[...])
    n_rec = 2 * SITES
    packed = packed[:n_rec] + packed[n_rec:2 * n_rec] + packed[2 * n_rec:]
    snd[0] = packed[:, :cap]
    recs[1] = packed[:, cap:2 * cap]
    snd[2] = packed[:, 2 * cap:]
    start(1)

    for k in ("ks", "redges", "rinv", "cinv", "rmid", "redge"):
        loads[k].wait()
    load_weights.wait()
    arrive(0)
    near = prec[0].astype(F32) + prec[1].astype(F32)
    real = own_real + near[:, :col_freqs]
    imag = own_imag + near[:, col_freqs:]

    half = cinv.shape[1] // 2
    pairs_n = kernels // 2
    ends = []
    for pair in range(pairs_n):
        blocks = []
        for k in (2 * pair, 2 * pair + 1):
            kr = ksv[0, k]
            ki = ksv[1, k]
            blocks.append(jnp.concatenate(
                [(kr * real - ki * imag).astype(BF), (kr * imag + ki * real).astype(BF)], axis=0))
        block = jnp.concatenate(blocks, axis=1)
        prod[pair] = block
        field = dot(rends[...], block).astype(BF)
        for i in range(2):
            part = field[:, i * col_freqs:(i + 1) * col_freqs]
            ends.append(jnp.concatenate([part[:2 * REACH], part[2 * REACH:]], axis=1))
    e = dot(jnp.concatenate(ends, axis=0), cinv[...])
    total = jnp.zeros((2 * REACH, half), F32)
    for k in range(kernels):
        er = e[2 * REACH * k:2 * REACH * (k + 1), :half]
        ei = e[2 * REACH * k:2 * REACH * (k + 1), half:]
        total = total + weights[k] * (er * er + ei * ei)
    rounded = total.astype(BF).astype(F32)
    hsnd[0] = rounded[:REACH]
    hsnd[1] = rounded[REACH:]
    start(2)

    strips = rows // STRIP
    for pair in range(pairs_n):
        field = dot(rinv[...], prod[pair]).astype(BF)
        for i in range(2):
            part = field[:, i * col_freqs:(i + 1) * col_freqs]
            part = jnp.concatenate([part[:rows], part[rows:]], axis=1)
            at = (2 * pair + i) * STRIP
            for strip in range(strips):
                fields[strip, at:at + STRIP] = part[strip * STRIP:(strip + 1) * STRIP]
    sums = jnp.zeros((8, half), F32)
    for strip in range(strips):
        e = dot(fields[strip], cinv[...])
        total = jnp.zeros((STRIP, half), F32)
        for k in range(kernels):
            er = e[STRIP * k:STRIP * (k + 1), :half]
            ei = e[STRIP * k:STRIP * (k + 1), half:]
            total = total + weights[k] * (er * er + ei * ei)
        inten[strip * STRIP:(strip + 1) * STRIP] = total.astype(BF)
        for i in range(STRIP // 8):
            sums = sums + total[8 * i:8 * (i + 1)]
    center = jnp.sum(sums) * (1.0 / (rows * half))
    blurred = dot(rmid[...], inten[...]) - center
    dev = blurred.astype(BF)
    tile_out[...] = dev
    load_thresh.wait()
    center_out[...] = jnp.where(
        lax.broadcasted_iota(jnp.int32, center_out.shape, 0) < 4, center, thresh[0, 0])
    loads["ftab"].wait()
    loads["btab"].wait()
    freqs = 2 * col_freqs
    lacking = jnp.sum(ftab[freqs:].astype(F32), axis=1, keepdims=True) * center
    lacking = jnp.concatenate([jnp.zeros((freqs, 1), F32), lacking], axis=0)
    that[...] = (dot_nt(ftab[...], dev) + lacking).astype(BF)
    arrive(1)

    span = cols // STEPS
    row_line = lax.broadcasted_iota(jnp.int32, (rows, cap), 0).astype(BF)
    step_line = lax.broadcasted_iota(jnp.int32, (btab.shape[1], cap), 0).astype(BF)
    end_line = lax.broadcasted_iota(jnp.int32, (2 * REACH, cap), 0).astype(F32)
    end_line = jnp.where(end_line < REACH, end_line, end_line + float(cols - 2 * REACH))

    def pick(index, period, function):
        found = jnp.full(index.shape, float(np.round(function(2.0 * math.pi * (STEPS - 1) * period / STEPS), 9)), F32)
        for i in range(STEPS - 1):
            found = jnp.where(index == i, float(np.round(function(2.0 * math.pi * i * period / STEPS), 9)), found)
        return found

    def ramp(line, low, part):
        zero = jnp.zeros((), BF)
        upper = jnp.where(line == (low + 1.0).astype(BF), part.astype(BF), zero)
        return jnp.where(line == low.astype(BF), (1.0 - part).astype(BF), upper)

    def coords(block):
        p = recs[block, :SITES, :] * float(rows - 1)
        q = recs[block, SITES:, :] * float(cols - 1)
        p0 = jnp.minimum(jnp.floor(p), float(rows - 2))
        q0 = jnp.minimum(jnp.floor(q), float(cols - 2))
        h = jnp.floor(q0 * (1.0 / span))
        return q, h, p0, p - p0, q0 - h * float(span), q - q0

    def place(block):
        q, h, p0, p1, low, q1 = coords(block)
        turn = [(pick(h, j, math.cos), pick(h, j, math.sin)) for j in range(1, STEPS // 2)]
        return q, p0, p1, low, q1, turn, pick(h, STEPS // 2, math.cos)

    def evaluate(where):
        q, p0, p1, low, q1, turn, sign = where
        acc = jnp.zeros((8, cap), F32)
        for s in range(SITES):
            at = slice(s, s + 1)
            g = dot(that[...], ramp(row_line, p0[at], p1[at]))
            e = dot(btab[...], ramp(step_line, low[at], q1[at]))
            inner = [None] * (STEPS // 2 + 1)
            cross = [None] * (STEPS // 2 + 1)
            for i in range(col_freqs // 8):
                j = i * 8 * STEPS // col_freqs
                k = min(j, STEPS - j)
                gc, gs = g[8 * i:8 * i + 8], g[col_freqs + 8 * i:col_freqs + 8 * i + 8]
                ec, es = e[8 * i:8 * i + 8], e[col_freqs + 8 * i:col_freqs + 8 * i + 8]
                term = gc * ec + gs * es
                inner[k] = term if inner[k] is None else inner[k] + term
                if k in (0, STEPS // 2):
                    continue
                term = gs * ec - gc * es if j == k else gc * es - gs * ec
                cross[k] = term if cross[k] is None else cross[k] + term
            value = inner[0] + sign[at] * inner[STEPS // 2]
            for k in range(1, STEPS // 2):
                value = value + turn[k - 1][0][at] * inner[k] + turn[k - 1][1][at] * cross[k]
            ends = g[freqs:] * hat(end_line - q[at])
            acc = acc + (value + (ends[:REACH] + ends[REACH:]))
        mean = jnp.sum(acc, axis=0, keepdims=True) * (1.0 / SITES) + center * BLUR_SUM
        return jnp.broadcast_to(mean, (8, cap))

    first = jnp.where(even, 0, 2)
    first_place = place(first)
    arrive(2)
    edge = jnp.concatenate([halo[0], halo[1]], axis=0).astype(BF)
    added = dot(redge[...], edge)
    head = (blurred[:2 * REACH] + added[:2 * REACH]).astype(BF)
    foot = (blurred[rows - 2 * REACH:] + added[2 * REACH:]).astype(BF)
    tile_out[:2 * REACH] = head
    tile_out[rows - 2 * REACH:] = foot
    blank = jnp.zeros((128 - 4 * REACH, half), BF)
    spectra = dot_nt(ftab[...], jnp.concatenate([head, blank, foot], axis=0)) + lacking
    lane = lax.broadcasted_iota(jnp.int32, spectra.shape, 1)
    low_half, high_half = that[:, :128].astype(F32), that[:, rows - 128:].astype(F32)
    that[:, :128] = jnp.where(lane < 2 * REACH, spectra, low_half).astype(BF)
    that[:, rows - 128:] = jnp.where(lane >= 128 - 2 * REACH, spectra, high_half).astype(BF)

    rsnd[first] = evaluate(first_place)
    start_far(3)
    second = 2 - first
    rsnd[second] = evaluate(place(second))
    start_near(3)
    ret[1] = evaluate(place(1))
    arrive(3)
    means_out[...] = jnp.broadcast_to(
        jnp.concatenate([ret[0, 0:1], ret[1, 0:1], ret[2, 0:1]], axis=1), means_out.shape)

    for kind in range(4):
        @pl.when(has_left)
        def _():
            pairs[kind][0].wait_send()

        @pl.when(has_right)
        def _():
            pairs[kind][1].wait_send()


def finish(tile, wide, sums, center, sel, means, steps, resist_h, nb_h, out, nb, sem):
    chunks = wide.shape[0]
    width = wide.shape[2]
    last = pltpu.make_async_copy(nb, nb_h, sem.at[2])
    stores = [pltpu.make_async_copy(out.at[i], resist_h.at[:, pl.ds(i * width, width)], sem.at[3 + i])
              for i in range(chunks)]
    for i in range(chunks):
        out[i] = dot(tile[...], wide[i]) + center[0:1, 0:1] * sums[0:1, i * width:(i + 1) * width]
        stores[i].start()
    found = dot(split3(means[0:1]), sel[...])
    mean = found[0:1] + found[1:2] + found[2:3]
    nb[...] = 0.5 * steps[...].astype(F32) - 2.0 * (mean - center[4:5, 0:1]).reshape(nb.shape)
    last.start(priority=1)
    for store in stores:
        store.wait()
    last.wait()


def shards(mask, kernel_spectra, kernel_weights, threshold, eval_tile, site_coords, bias_steps):
    rows, cols = mask.shape
    row_freqs, kernels, col_freqs = kernel_spectra.shape[1:]
    frags = eval_tile.shape[0]
    cap = frags // 2
    names = ("colf", "rowf", "rinv", "redges", "cinv", "rmid", "redge", "wide", "sums", "ftab", "btab")
    values = dict(zip(names, (jnp.asarray(x) for x in tables(rows, cols, row_freqs, col_freqs))))
    values["mask"] = mask
    values["ks"] = jnp.transpose(kernel_spectra, (0, 2, 1, 3))
    values["ev"] = eval_tile.reshape(1, frags)
    values["sc"] = site_coords
    ordered = [values[k] for k in LOADED]
    vmem = pl.BlockSpec(memory_space=pltpu.VMEM)
    hbm = pl.BlockSpec(memory_space=pltpu.HBM)
    anyw = pl.BlockSpec(memory_space=pl.ANY)
    coarse = cols // GRID_STEP
    tile, sel, means, center = pl.pallas_call(
        kernel,
        out_shape=(pltpu.VMEM((rows, coarse), BF), pltpu.VMEM((3 * cap, frags), BF),
                   pltpu.VMEM((8, 3 * cap), F32), pltpu.VMEM((8, 128), F32)),
        in_specs=[hbm] * (2 + len(ordered)),
        out_specs=(vmem, vmem, vmem, vmem),
        scratch_shapes=[pltpu.VMEM(x.shape, x.dtype) for x in ordered] + [
            pltpu.SMEM((kernels,), F32),
            pltpu.SMEM((1, 1), F32),
            pltpu.VMEM((2, row_freqs, 2 * col_freqs), BF),
            pltpu.VMEM((2, row_freqs, 2 * col_freqs), BF),
            pltpu.VMEM((kernels // 2, 2 * row_freqs, 2 * col_freqs), BF),
            pltpu.VMEM((rows // STRIP, kernels * STRIP, 2 * col_freqs), BF),
            pltpu.VMEM((3, 2 * SITES, cap), F32),
            pltpu.VMEM((3, 2 * SITES, cap), F32),
            pltpu.VMEM((rows, coarse), BF),
            pltpu.VMEM((2, REACH, coarse), F32),
            pltpu.VMEM((2, REACH, coarse), F32),
            pltpu.VMEM((3, 8, cap), F32),
            pltpu.VMEM((3, 8, cap), F32),
            pltpu.VMEM((2 * col_freqs + 2 * REACH, rows), BF),
            pltpu.SemaphoreType.DMA((len(ordered) + 2,)),
            pltpu.SemaphoreType.DMA((4, 2)),
            pltpu.SemaphoreType.DMA((4, 2)),
        ],
        compiler_params=pltpu.CompilerParams(
            collective_id=0, has_side_effects=True, vmem_limit_bytes=int(60 * 2 ** 20)),
    )(kernel_weights, threshold.reshape(1, 1), *ordered)
    width = cols // CHUNKS
    return pl.pallas_call(
        finish,
        out_shape=(jax.ShapeDtypeStruct((rows, cols), F32), jax.ShapeDtypeStruct((frags,), F32)),
        in_specs=[vmem] * 7,
        out_specs=(anyw, anyw),
        scratch_shapes=[
            pltpu.VMEM((CHUNKS, rows, width), F32),
            pltpu.VMEM((frags,), F32),
            pltpu.SemaphoreType.DMA((3 + CHUNKS,)),
        ],
        compiler_params=pltpu.CompilerParams(vmem_limit_bytes=4 << 20),
    )(tile, values["wide"], values["sums"], center, sel, means, bias_steps)


def solution(mesh):
    placed = (
        P(("groups", "tx"), None),
        P(),
        P(),
        P(),
        P(("groups", "tx")),
        P(None, None, ("groups", "tx")),
        P(("groups", "tx")),
    )
    return jax.shard_map(
        shards,
        mesh=mesh,
        in_specs=placed,
        out_specs=(P(("groups", "tx"), None), P(("groups", "tx"))),
        check_vma=False,
    )
```

```python
import math

import jax
import jax.numpy as jnp
import ml_dtypes
import numpy as np
from jax import lax
from jax.experimental import pallas as pl
from jax.experimental.pallas import tpu as pltpu
from jax.sharding import PartitionSpec as P

HALO = 256
REACH = 8
EARLY = 5
SITES = 16
GRID_STEP = 4
STEPS = 8
SIGMA = 3.0
CHUNKS = 4
STRIP = 32
BF = jnp.bfloat16
F32 = jnp.float32
MESH = pl.DeviceIdType.MESH
LOADED = ("mask", "colf", "rowf", "ev", "sc", "ks", "redges", "rinv", "cinv", "rmid", "redge", "ftab", "btab")


def host_bf16(x):
    return np.asarray(x, np.float32).astype(ml_dtypes.bfloat16)


def twiddle(position, frequency, period, amplitude):
    index = (position[:, None] * frequency[None, :]) % period
    angle = index.astype(np.float64) * (2.0 * math.pi / period)
    return np.cos(angle) * amplitude, np.sin(angle) * amplitude


def gauss(offset):
    every = np.arange(-REACH, REACH + 1)
    norm = np.sum(np.exp(-every * every / (2.0 * SIGMA * SIGMA)))
    value = np.exp(-offset * offset / (2.0 * SIGMA * SIGMA)) / norm
    return np.where(np.abs(offset) <= REACH, value, 0.0)


def tables(rows, cols, row_freqs, col_freqs):
    window = rows + 2 * HALO
    f = np.arange(col_freqs) - col_freqs // 2
    g = np.arange(row_freqs) - row_freqs // 2
    c, s = twiddle(np.arange(cols), f, cols, 1.0 / math.sqrt(cols))
    col_forward = host_bf16(np.concatenate([c, -s], 1))
    c, s = twiddle(g, np.arange(window), window, 1.0 / math.sqrt(window))
    row_forward = host_bf16(np.concatenate([c, -s], 0))
    c, s = twiddle(np.arange(rows) + HALO, g, window, 1.0 / math.sqrt(row_freqs))
    row_inverse = host_bf16(np.block([[c, -s], [s, c]]))
    ends = np.r_[0:REACH, rows - REACH:rows]
    inverse_ends = np.ascontiguousarray(row_inverse[np.concatenate([ends, rows + ends])])
    row_forward = np.concatenate([
        row_forward[:, HALO + rows:], row_forward[:, :HALO], row_forward[:, HALO:HALO + rows]], 0)
    picked = np.arange(0, cols, GRID_STEP)
    c, s = twiddle(f, picked, cols, 1.0 / math.sqrt(col_freqs))
    col_inverse = host_bf16(np.block([[c, s], [-s, c]]))
    diff = np.arange(cols)[None, :] - picked[:, None]
    order = np.arange(1, col_freqs)
    base = np.arange(cols)
    kernel = 1.0 + 2.0 * np.cos(2 * math.pi * ((base[:, None] * order[None, :]) % cols) / cols).sum(1)
    kernel = (kernel + np.cos(2 * math.pi * ((base * col_freqs) % cols) / cols)) / picked.size
    interp = kernel[diff % cols]
    lines = np.arange(cols)
    col_blur = host_bf16(gauss((lines[None, :] - lines[:, None]).astype(np.float64)))
    spread = interp @ col_blur.astype(np.float64)
    high = host_bf16(spread)
    wide = np.ascontiguousarray(high.reshape(picked.size, CHUNKS, cols // CHUNKS).transpose(1, 0, 2))
    sums = spread.sum(0).astype(np.float32)[None]
    row_diff = np.arange(rows + 2 * REACH)[None, :] - REACH - np.arange(rows)[:, None]
    row_blur = host_bf16(gauss(row_diff.astype(np.float64)))
    row_mid = np.ascontiguousarray(row_blur[:, REACH:REACH + rows])
    row_edge = np.concatenate([row_blur[:, :REACH], row_blur[:, REACH + rows:]], 1)
    row_edge = np.concatenate([row_edge[:2 * REACH], row_edge[rows - 2 * REACH:]], 0)
    return (col_forward, row_forward, row_inverse, inverse_ends, col_inverse, row_mid, row_edge, wide,
            sums) + site_tables(cols, col_freqs, interp, spread)


def site_tables(cols, col_freqs, interp, spread):
    coarse = cols // GRID_STEP
    span = cols // STEPS
    line = np.arange(cols)
    reach = np.arange(-REACH, REACH + 1)
    weight = host_bf16(gauss(reach.astype(np.float64))).astype(np.float64)
    periodic = np.zeros((cols, cols))
    for d, w in zip(reach, weight):
        periodic[(line - d) % cols, line] += w
    order = np.concatenate([np.arange(j, col_freqs, STEPS) for j in range(STEPS)])
    angle = 2.0 * math.pi * ((np.arange(col_freqs + 1)[:, None] * reach[None, :]) % cols) / cols
    response = (weight[None, :] * np.cos(angle)).sum(1)
    scale = (np.where(order == 0, 1.0, 2.0) * response[order] / coarse)[:, None]
    angle = 2.0 * math.pi * ((order[:, None] * GRID_STEP * np.arange(coarse)[None, :]) % cols) / cols
    cosine, sine = scale * np.cos(angle), scale * np.sin(angle)
    sine[0] = response[col_freqs] / coarse * np.cos(math.pi * np.arange(coarse))
    ends = np.r_[0:REACH, cols - REACH:cols]
    lacking = (spread - interp @ periodic)[:, ends].T
    steps = np.arange(-(-(span + 1) // 16) * 16)
    angle = 2.0 * math.pi * ((order[:, None] * steps[None, :]) % cols) / cols
    base_cos, base_sin = np.cos(angle), np.sin(angle)
    base_sin[0] = np.cos(2.0 * math.pi * ((col_freqs * steps) % cols) / cols)
    return (host_bf16(np.concatenate([cosine, sine, lacking], 0)), host_bf16(np.concatenate([base_cos, base_sin], 0)))


BLUR_SUM = float(host_bf16(gauss(np.arange(-REACH, REACH + 1.0))).astype(np.float64).sum())


def dot(a, b):
    return jnp.dot(a, b, preferred_element_type=F32)


def dot_nt(a, b):
    return lax.dot_general(a, b, (((1,), (1,)), ((), ())), preferred_element_type=F32)


def split3(x):
    high = x.astype(BF)
    rest = x - high.astype(F32)
    mid = rest.astype(BF)
    low = (rest - mid.astype(F32)).astype(BF)
    return jnp.concatenate([high, mid, low], axis=0)


def hat(distance):
    return jnp.maximum(1.0 - jnp.abs(distance), 0.0)


def kernel(weights_h, thresh_h, *refs):
    n = len(LOADED)
    sources = dict(zip(LOADED, refs[:n]))
    tile_out, sel, means_out, center_out = refs[n:n + 4]
    held = dict(zip(LOADED, refs[n + 4:2 * n + 4]))
    (weights, thresh, psnd, prec, prod, fields, snd, recs, inten, hsnd, halo, rsnd, ret, that,
     local_sem, send_sem, recv_sem) = refs[2 * n + 4:]
    mask, colf, rowf, ev, sc, ksv, rends, rinv, cinv, rmid, redge, ftab, btab = (held[k] for k in LOADED)
    t = lax.axis_index("tx")
    count = lax.axis_size("tx")
    has_left = t > 0
    has_right = t < count - 1
    rows, cols = mask.shape
    coarse = cols // GRID_STEP
    kernels, row_freqs, col_freqs = ksv.shape[1:]
    frags = ev.shape[1]
    cap = frags // 2

    barrier = pltpu.get_barrier_semaphore()

    @pl.when(has_left)
    def _():
        pl.semaphore_signal(barrier, inc=1, device_id={"tx": t - 1}, device_id_type=MESH)

    @pl.when(has_right)
    def _():
        pl.semaphore_signal(barrier, inc=1, device_id={"tx": t + 1}, device_id_type=MESH)

    loads = {k: pltpu.make_async_copy(sources[k], held[k], local_sem.at[i])
             for i, k in enumerate(LOADED)}
    for k in LOADED[:EARLY]:
        loads[k].start()
    load_weights = pltpu.make_async_copy(weights_h, weights, local_sem.at[n])

    load_thresh = pltpu.make_async_copy(thresh_h, thresh, local_sem.at[n + 1])

    def to_left(kind, src, dst):
        return pltpu.make_async_remote_copy(
            src_ref=src, dst_ref=dst, send_sem=send_sem.at[kind, 0], recv_sem=recv_sem.at[kind, 0],
            device_id={"tx": t - 1}, device_id_type=MESH)

    def to_right(kind, src, dst):
        return pltpu.make_async_remote_copy(
            src_ref=src, dst_ref=dst, send_sem=send_sem.at[kind, 1], recv_sem=recv_sem.at[kind, 1],
            device_id={"tx": t + 1}, device_id_type=MESH)

    pairs = (
        (to_left(0, psnd.at[0], prec.at[1]), to_right(0, psnd.at[1], prec.at[0])),
        (to_left(1, snd.at[0], recs.at[2]), to_right(1, snd.at[2], recs.at[0])),
        (to_left(2, hsnd.at[0], halo.at[1]), to_right(2, hsnd.at[1], halo.at[0])),
        (to_left(3, rsnd.at[0, pl.ds(0, 1)], ret.at[2, pl.ds(0, 1)]),
         to_right(3, rsnd.at[2, pl.ds(0, 1)], ret.at[0, pl.ds(0, 1)])),
    )

    even = t % 2 == 0
    odd = jnp.logical_not(even)

    def start_far(kind):
        @pl.when(jnp.logical_and(even, has_left))
        def _():
            pairs[kind][0].start()

        @pl.when(jnp.logical_and(odd, has_right))
        def _():
            pairs[kind][1].start()

    def start_near(kind):
        @pl.when(jnp.logical_and(even, has_right))
        def _():
            pairs[kind][1].start()

        @pl.when(jnp.logical_and(odd, has_left))
        def _():
            pairs[kind][0].start()

    def start(kind):
        start_far(kind)
        start_near(kind)

    def arrive(kind):
        @pl.when(has_right)
        def _():
            pairs[kind][0].wait_recv()

        @pl.when(has_left)
        def _():
            pairs[kind][1].wait_recv()

    @pl.when(jnp.logical_not(has_left))
    def _():
        prec[0] = jnp.zeros(prec.shape[1:], BF)
        recs[0] = jnp.zeros(recs.shape[1:], F32)
        halo[0] = jnp.zeros(halo.shape[1:], F32)
        ret[0] = jnp.zeros(ret.shape[1:], F32)

    @pl.when(jnp.logical_not(has_right))
    def _():
        prec[1] = jnp.zeros(prec.shape[1:], BF)
        recs[2] = jnp.zeros(recs.shape[1:], F32)
        halo[1] = jnp.zeros(halo.shape[1:], F32)
        ret[2] = jnp.zeros(ret.shape[1:], F32)

    loads["mask"].wait()
    loads["colf"].wait()
    for k in LOADED[EARLY:]:
        loads[k].start()
    load_weights.start()
    load_thresh.start()
    win = dot(mask[...], colf[...]).astype(BF)
    loads["rowf"].wait()

    def spectrum(i):
        product = dot(rowf[2 * row_freqs * i:2 * row_freqs * (i + 1)], win)
        upper = product[:row_freqs]
        lower = product[row_freqs:]
        return (upper[:, :col_freqs] - lower[:, col_freqs:], upper[:, col_freqs:] + lower[:, :col_freqs])

    for i in range(2):
        psnd[i] = jnp.concatenate(spectrum(i), axis=1).astype(BF)

    between = jnp.logical_and(has_left, has_right)

    @pl.when(between)
    def _():
        pl.semaphore_wait(barrier, 2)

    @pl.when(jnp.logical_not(between))
    def _():
        pl.semaphore_wait(barrier, 1)

    start(0)
    own_real, own_imag = spectrum(2)

    loads["ev"].wait()
    loads["sc"].wait()
    offset = ev[...] - t + 1
    member = jnp.where(lax.broadcasted_iota(jnp.int32, (8, frags), 0) == offset, 1.0, 0.0)
    upper = jnp.where(
        lax.broadcasted_iota(jnp.int32, (frags, frags), 0)
        <= lax.broadcasted_iota(jnp.int32, (frags, frags), 1), 1.0, 0.0).astype(BF)
    inclusive = dot(member.astype(BF), upper)
    rank = jnp.sum(member * (inclusive - 1.0), axis=0, keepdims=True)
    slot = offset.astype(F32) * float(cap) + rank
    slot_line = lax.broadcasted_iota(jnp.int32, (3 * cap, frags), 0).astype(F32)
    sel[...] = jnp.where(slot_line == slot, 1.0, 0.0).astype(BF)
    records = jnp.concatenate([sc[0], sc[1]], axis=0)
    packed = dot_nt(split3(records), sel[...])
    n_rec = 2 * SITES
    packed = packed[:n_rec] + packed[n_rec:2 * n_rec] + packed[2 * n_rec:]
    snd[0] = packed[:, :cap]
    recs[1] = packed[:, cap:2 * cap]
    snd[2] = packed[:, 2 * cap:]
    start(1)

    for k in ("ks", "redges", "rinv", "cinv", "rmid", "redge"):
        loads[k].wait()
    load_weights.wait()
    arrive(0)
    near = prec[0].astype(F32) + prec[1].astype(F32)
    real = own_real + near[:, :col_freqs]
    imag = own_imag + near[:, col_freqs:]

    half = cinv.shape[1] // 2
    pairs_n = kernels // 2
    ends = []
    for pair in range(pairs_n):
        blocks = []
        for k in (2 * pair, 2 * pair + 1):
            kr = ksv[0, k]
            ki = ksv[1, k]
            blocks.append(jnp.concatenate(
                [(kr * real - ki * imag).astype(BF), (kr * imag + ki * real).astype(BF)], axis=0))
        block = jnp.concatenate(blocks, axis=1)
        prod[pair] = block
        field = dot(rends[...], block).astype(BF)
        for i in range(2):
            part = field[:, i * col_freqs:(i + 1) * col_freqs]
            ends.append(jnp.concatenate([part[:2 * REACH], part[2 * REACH:]], axis=1))
    e = dot(jnp.concatenate(ends, axis=0), cinv[...])
    total = jnp.zeros((2 * REACH, half), F32)
    for k in range(kernels):
        er = e[2 * REACH * k:2 * REACH * (k + 1), :half]
        ei = e[2 * REACH * k:2 * REACH * (k + 1), half:]
        total = total + weights[k] * (er * er + ei * ei)
    rounded = total.astype(BF).astype(F32)
    hsnd[0] = rounded[:REACH]
    hsnd[1] = rounded[REACH:]
    start(2)

    strips = rows // STRIP
    for pair in range(pairs_n):
        field = dot(rinv[...], prod[pair]).astype(BF)
        for i in range(2):
            part = field[:, i * col_freqs:(i + 1) * col_freqs]
            part = jnp.concatenate([part[:rows], part[rows:]], axis=1)
            at = (2 * pair + i) * STRIP
            for strip in range(strips):
                fields[strip, at:at + STRIP] = part[strip * STRIP:(strip + 1) * STRIP]
    sums = jnp.zeros((8, half), F32)
    for strip in range(strips):
        e = dot(fields[strip], cinv[...])
        total = jnp.zeros((STRIP, half), F32)
        for k in range(kernels):
            er = e[STRIP * k:STRIP * (k + 1), :half]
            ei = e[STRIP * k:STRIP * (k + 1), half:]
            total = total + weights[k] * (er * er + ei * ei)
        inten[strip * STRIP:(strip + 1) * STRIP] = total.astype(BF)
        for i in range(STRIP // 8):
            sums = sums + total[8 * i:8 * (i + 1)]
    center = jnp.sum(sums) * (1.0 / (rows * half))
    blurred = dot(rmid[...], inten[...]) - center
    dev = blurred.astype(BF)
    tile_out[...] = dev
    load_thresh.wait()
    center_out[...] = jnp.where(
        lax.broadcasted_iota(jnp.int32, center_out.shape, 0) < 4, center, thresh[0, 0])
    loads["ftab"].wait()
    loads["btab"].wait()
    freqs = 2 * col_freqs
    lacking = jnp.sum(ftab[freqs:].astype(F32), axis=1, keepdims=True) * center
    lacking = jnp.concatenate([jnp.zeros((freqs, 1), F32), lacking], axis=0)
    that[...] = (dot_nt(ftab[...], dev) + lacking).astype(BF)
    arrive(1)

    span = cols // STEPS
    row_line = lax.broadcasted_iota(jnp.int32, (rows, cap), 0).astype(BF)
    step_line = lax.broadcasted_iota(jnp.int32, (btab.shape[1], cap), 0).astype(BF)
    end_line = lax.broadcasted_iota(jnp.int32, (2 * REACH, cap), 0).astype(F32)
    end_line = jnp.where(end_line < REACH, end_line, end_line + float(cols - 2 * REACH))

    def pick(index, period, function):
        found = jnp.full(index.shape, float(np.round(function(2.0 * math.pi * (STEPS - 1) * period / STEPS), 9)), F32)
        for i in range(STEPS - 1):
            found = jnp.where(index == i, float(np.round(function(2.0 * math.pi * i * period / STEPS), 9)), found)
        return found

    def ramp(line, low, part):
        zero = jnp.zeros((), BF)
        upper = jnp.where(line == (low + 1.0).astype(BF), part.astype(BF), zero)
        return jnp.where(line == low.astype(BF), (1.0 - part).astype(BF), upper)

    def coords(block):
        p = recs[block, :SITES, :] * float(rows - 1)
        q = recs[block, SITES:, :] * float(cols - 1)
        p0 = jnp.minimum(jnp.floor(p), float(rows - 2))
        q0 = jnp.minimum(jnp.floor(q), float(cols - 2))
        h = jnp.floor(q0 * (1.0 / span))
        return q, h, p0, p - p0, q0 - h * float(span), q - q0

    def place(block):
        q, h, p0, p1, low, q1 = coords(block)
        turn = [(pick(h, j, math.cos), pick(h, j, math.sin)) for j in range(1, STEPS // 2)]
        return q, p0, p1, low, q1, turn, pick(h, STEPS // 2, math.cos)

    def evaluate(where):
        q, p0, p1, low, q1, turn, sign = where
        acc = jnp.zeros((8, cap), F32)
        for s in range(SITES):
            at = slice(s, s + 1)
            g = dot(that[...], ramp(row_line, p0[at], p1[at]))
            e = dot(btab[...], ramp(step_line, low[at], q1[at]))
            inner = [None] * (STEPS // 2 + 1)
            cross = [None] * (STEPS // 2 + 1)
            for i in range(col_freqs // 8):
                j = i * 8 * STEPS // col_freqs
                k = min(j, STEPS - j)
                gc, gs = g[8 * i:8 * i + 8], g[col_freqs + 8 * i:col_freqs + 8 * i + 8]
                ec, es = e[8 * i:8 * i + 8], e[col_freqs + 8 * i:col_freqs + 8 * i + 8]
                term = gc * ec + gs * es
                inner[k] = term if inner[k] is None else inner[k] + term
                if k in (0, STEPS // 2):
                    continue
                term = gs * ec - gc * es if j == k else gc * es - gs * ec
                cross[k] = term if cross[k] is None else cross[k] + term
            value = inner[0] + sign[at] * inner[STEPS // 2]
            for k in range(1, STEPS // 2):
                value = value + turn[k - 1][0][at] * inner[k] + turn[k - 1][1][at] * cross[k]
            ends = g[freqs:] * hat(end_line - q[at])
            acc = acc + (value + (ends[:REACH] + ends[REACH:]))
        mean = jnp.sum(acc, axis=0, keepdims=True) * (1.0 / SITES) + center * BLUR_SUM
        return jnp.broadcast_to(mean, (8, cap))

    first = jnp.where(even, 0, 2)
    first_place = place(first)
    arrive(2)
    edge = jnp.concatenate([halo[0], halo[1]], axis=0).astype(BF)
    added = dot(redge[...], edge)
    head = (blurred[:2 * REACH] + added[:2 * REACH]).astype(BF)
    foot = (blurred[rows - 2 * REACH:] + added[2 * REACH:]).astype(BF)
    tile_out[:2 * REACH] = head
    tile_out[rows - 2 * REACH:] = foot
    blank = jnp.zeros((128 - 4 * REACH, half), BF)
    spectra = dot_nt(ftab[...], jnp.concatenate([head, blank, foot], axis=0)) + lacking
    that[:, :2 * REACH] = spectra[:, :2 * REACH].astype(BF)
    that[:, rows - 2 * REACH:] = spectra[:, 128 - 2 * REACH:].astype(BF)

    rsnd[first] = evaluate(first_place)
    start_far(3)
    second = 2 - first
    rsnd[second] = evaluate(place(second))
    start_near(3)
    ret[1] = evaluate(place(1))
    arrive(3)
    means_out[...] = jnp.broadcast_to(
        jnp.concatenate([ret[0, 0:1], ret[1, 0:1], ret[2, 0:1]], axis=1), means_out.shape)

    for kind in range(4):
        @pl.when(has_left)
        def _():
            pairs[kind][0].wait_send()

        @pl.when(has_right)
        def _():
            pairs[kind][1].wait_send()


def finish(tile, wide, sums, center, sel, means, steps, resist_h, nb_h, out, nb, sem):
    chunks = wide.shape[0]
    width = wide.shape[2]
    last = pltpu.make_async_copy(nb, nb_h, sem.at[2])
    stores = [pltpu.make_async_copy(out.at[i], resist_h.at[:, pl.ds(i * width, width)], sem.at[3 + i])
              for i in range(chunks)]
    for i in range(chunks):
        out[i] = dot(tile[...], wide[i]) + center[0:1, 0:1] * sums[0:1, i * width:(i + 1) * width]
        stores[i].start()
    found = dot(split3(means[0:1]), sel[...])
    mean = found[0:1] + found[1:2] + found[2:3]
    nb[...] = 0.5 * steps[...].astype(F32) - 2.0 * (mean - center[4:5, 0:1]).reshape(nb.shape)
    last.start(priority=1)
    for store in stores:
        store.wait()
    last.wait()


def shards(mask, kernel_spectra, kernel_weights, threshold, eval_tile, site_coords, bias_steps):
    rows, cols = mask.shape
    row_freqs, kernels, col_freqs = kernel_spectra.shape[1:]
    frags = eval_tile.shape[0]
    cap = frags // 2
    names = ("colf", "rowf", "rinv", "redges", "cinv", "rmid", "redge", "wide", "sums", "ftab", "btab")
    values = dict(zip(names, (jnp.asarray(x) for x in tables(rows, cols, row_freqs, col_freqs))))
    values["mask"] = mask
    values["ks"] = jnp.transpose(kernel_spectra, (0, 2, 1, 3))
    values["ev"] = eval_tile.reshape(1, frags)
    values["sc"] = site_coords
    ordered = [values[k] for k in LOADED]
    vmem = pl.BlockSpec(memory_space=pltpu.VMEM)
    hbm = pl.BlockSpec(memory_space=pltpu.HBM)
    anyw = pl.BlockSpec(memory_space=pl.ANY)
    coarse = cols // GRID_STEP
    tile, sel, means, center = pl.pallas_call(
        kernel,
        out_shape=(pltpu.VMEM((rows, coarse), BF), pltpu.VMEM((3 * cap, frags), BF),
                   pltpu.VMEM((8, 3 * cap), F32), pltpu.VMEM((8, 128), F32)),
        in_specs=[hbm] * (2 + len(ordered)),
        out_specs=(vmem, vmem, vmem, vmem),
        scratch_shapes=[pltpu.VMEM(x.shape, x.dtype) for x in ordered] + [
            pltpu.SMEM((kernels,), F32),
            pltpu.SMEM((1, 1), F32),
            pltpu.VMEM((2, row_freqs, 2 * col_freqs), BF),
            pltpu.VMEM((2, row_freqs, 2 * col_freqs), BF),
            pltpu.VMEM((kernels // 2, 2 * row_freqs, 2 * col_freqs), BF),
            pltpu.VMEM((rows // STRIP, kernels * STRIP, 2 * col_freqs), BF),
            pltpu.VMEM((3, 2 * SITES, cap), F32),
            pltpu.VMEM((3, 2 * SITES, cap), F32),
            pltpu.VMEM((rows, coarse), BF),
            pltpu.VMEM((2, REACH, coarse), F32),
            pltpu.VMEM((2, REACH, coarse), F32),
            pltpu.VMEM((3, 8, cap), F32),
            pltpu.VMEM((3, 8, cap), F32),
            pltpu.VMEM((2 * col_freqs + 2 * REACH, rows), BF),
            pltpu.SemaphoreType.DMA((len(ordered) + 2,)),
            pltpu.SemaphoreType.DMA((4, 2)),
            pltpu.SemaphoreType.DMA((4, 2)),
        ],
        compiler_params=pltpu.CompilerParams(
            collective_id=0, has_side_effects=True, vmem_limit_bytes=int(60 * 2 ** 20)),
    )(kernel_weights, threshold.reshape(1, 1), *ordered)
    width = cols // CHUNKS
    return pl.pallas_call(
        finish,
        out_shape=(jax.ShapeDtypeStruct((rows, cols), F32), jax.ShapeDtypeStruct((frags,), F32)),
        in_specs=[vmem] * 7,
        out_specs=(anyw, anyw),
        scratch_shapes=[
            pltpu.VMEM((CHUNKS, rows, width), F32),
            pltpu.VMEM((frags,), F32),
            pltpu.SemaphoreType.DMA((3 + CHUNKS,)),
        ],
        compiler_params=pltpu.CompilerParams(vmem_limit_bytes=4 << 20),
    )(tile, values["wide"], values["sums"], center, sel, means, bias_steps)


def solution(mesh):
    placed = (
        P(("groups", "tx"), None),
        P(),
        P(),
        P(),
        P(("groups", "tx")),
        P(None, None, ("groups", "tx")),
        P(("groups", "tx")),
    )
    return jax.shard_map(
        shards,
        mesh=mesh,
        in_specs=placed,
        out_specs=(P(("groups", "tx"), None), P(("groups", "tx"))),
        check_vma=False,
    )
```
